32 devices in a mesh: dp: 4 (over x, core), fsdp: 8 (over z, y).
Axes of the slice: x: 2, y: 2, z: 4, core: 2. Of those that a mesh axis runs over, the one named last changes fastest.
Arguments:
- inputs: bfloat16 [64, 256, 768], P(('dp', 'fsdp')), may hold values from -6 to 6
- cotangent: bfloat16 [64, 256, 768], P(('dp', 'fsdp')), may hold values from -6 to 6
- image_shape: int32 [64, 2], P(('dp', 'fsdp')), may hold values from 8 to 16, as said below
- time_bins: int32 [64], P(('dp', 'fsdp')), may hold values from 0 to 999
- time_table: float32 [1000, 768], replicated, may hold values from -6 to 6
- modulation_master: float32 [6, 768, 768], P(None, 'fsdp'), may hold values from -0.21875 to 0.21875
- projection_master: float32 [3, 768, 768], P(None, 'fsdp'), may hold values from -0.21875 to 0.21875
- output_master: float32 [768, 768], P('fsdp'), may hold values from -1.75 to 1.75
- expand_master: float32 [2, 768, 2048], P(None, 'fsdp'), may hold values from -0.21875 to 0.21875
- shrink_master: float32 [2048, 768], P(None, 'fsdp'), may hold values from -0.125 to 0.125
- modulation_moment: float32 [6, 768, 768], P(None, 'fsdp'), may hold values from -80 to 80
- projection_moment: float32 [3, 768, 768], P(None, 'fsdp'), may hold values from -448 to 448
- output_moment: float32 [768, 768], P('fsdp'), may hold values from -80 to 80
- expand_moment: float32 [2, 768, 2048], P(None, 'fsdp'), may hold values from -80 to 80
- shrink_moment: float32 [2048, 768], P(None, 'fsdp'), may hold values from -80 to 80
Outputs:
- block_output: bfloat16 [64, 256, 768], P(('dp', 'fsdp'))
- input_gradient: float32 [64, 256, 768], P(('dp', 'fsdp'))
- modulation_gradient: float32 [6, 768, 768], P(None, 'fsdp')
- projection_gradient: float32 [3, 768, 768], P(None, 'fsdp')
- output_gradient: float32 [768, 768], P('fsdp')
- expand_gradient: float32 [2, 768, 2048], P(None, 'fsdp')
- shrink_gradient: float32 [2048, 768], P(None, 'fsdp')
- modulation_weight: float32 [6, 768, 768], P(None, 'fsdp')
- projection_weight: float32 [3, 768, 768], P(None, 'fsdp')
- output_weight: float32 [768, 768], P('fsdp')
- expand_weight: float32 [2, 768, 2048], P(None, 'fsdp')
- shrink_weight: float32 [2048, 768], P(None, 'fsdp')
- modulation_state: float32 [6, 768, 768], P(None, 'fsdp')
- projection_state: float32 [3, 768, 768], P(None, 'fsdp')
- output_state: float32 [768, 768], P('fsdp')
- expand_state: float32 [2, 768, 2048], P(None, 'fsdp')
- shrink_state: float32 [2048, 768], P(None, 'fsdp')
The draws below stay inside these ranges and needn't reach their ends.
Inputs may be any that keep to these rules, and one draw needn't show every extreme that they name: Image b has image_shape[b, 0] patch rows and image_shape[b, 1] patch columns; in every draw some image is 16 x 16, filling all 256 slots.
All inputs are finite; a program needn't handle non-finite values.
Results may differ from the reference program's by a relative error of at most 0.02.
The reference program's roundings to bfloat16 on the way count: a program that leaves them out, or rounds other values in their place, can miss the bound.
Values may be sent and summed in bfloat16 or wider, within the bound.
No kernel may reach another device: no remote copies, remote signals or barrier semaphores. Data moves between devices by JAX's collectives and lax.ppermute only.
A program may use at most 192 MiB of HBM per device.

```python
import jax
import jax.numpy as jnp
from jax import lax

D = 768
HEADS = 12
HDIM = 64
FF = 2048
SIDE = 16
TBINS = 1000
NS_ITERS = 5
SEQ = 256
IMAGES = 64


def draw_image_shape(key, part):
    first_key, second_key = jax.random.split(key)
    sides_drawn = jax.random.randint(first_key, (IMAGES, 2), SIDE // 2, SIDE + 1)
    chosen = jax.random.randint(second_key, (), 0, IMAGES)
    full_image = jnp.arange(IMAGES, dtype=jnp.int32)[:, None] == chosen
    return jnp.where(full_image, SIDE, sides_drawn).astype(jnp.int32)


def set_ends(entries, own_key, smallest, top_value):
    shape = entries.shape
    index_at = [jax.random.randint(jax.random.fold_in(own_key, axis), (), 0, shape[axis]) for axis in range(len(shape))]
    entries = entries.at[tuple(index_at)].set(smallest)
    longest = shape.index(max(shape))
    index_at[longest] = (index_at[longest] + 1) % shape[longest]
    return entries.at[tuple(index_at)].set(top_value)


def levels(stream_key, extent, pieces, least, high):
    factor_of, own = 1.0, jax.random.fold_in(stream_key, 6)
    for dim, shards_of in pieces:
        steps = jnp.exp(jax.random.uniform(jax.random.fold_in(own, dim), (shards_of,), jnp.float32, least / len(pieces), high / len(pieces)))
        factor_of = factor_of * jnp.repeat(steps, extent[dim] // shards_of).reshape([-1 if axis == dim else 1 for axis in range(len(extent))])
    return factor_of


def normal_values(rng, dims, scale, limit, cuts=(), held_as=jnp.bfloat16):
    gain = levels(rng, dims, cuts, -0.22, 0.18) if cuts else 1.0
    values = jax.random.normal(rng, dims, jnp.float32) * scale * gain
    return jnp.minimum(jnp.maximum(values, -limit), limit).astype(held_as)


def setup_inputs(seed: int = 0) -> dict:
    streams_of = jax.random.split(jax.random.key(seed), 16)
    return {
        "inputs": normal_values(streams_of[0], (IMAGES, SEQ, D), 1.0, 6.0, ((0, 32),)),
        "cotangent": normal_values(streams_of[1], (IMAGES, SEQ, D), 1.0, 6.0, ((0, 32),)),
        "image_shape": draw_image_shape(jax.random.fold_in(streams_of[15], 71), 0),
        "time_bins": set_ends(jax.random.randint(streams_of[3], (IMAGES,), 0, TBINS), jax.random.fold_in(streams_of[3], 1), 0, TBINS - 1).astype(jnp.int32),
        "time_table": normal_values(streams_of[4], (TBINS, D), 1.0, 6.0, (), jnp.float32),
        "modulation_master": normal_values(streams_of[5], (6, D, D), D ** -0.5, 0.21875, ((1, 8),), jnp.float32),
        "projection_master": normal_values(streams_of[6], (3, D, D), D ** -0.5, 0.21875, ((1, 8),), jnp.float32),
        "output_master": normal_values(streams_of[7], (D, D), (D // 64) ** -0.5, 1.75, ((0, 8),), jnp.float32),
        "expand_master": normal_values(streams_of[8], (2, D, FF), D ** -0.5, 0.21875, ((1, 8),), jnp.float32),
        "shrink_master": normal_values(streams_of[9], (FF, D), FF ** -0.5, 0.125, ((1, 8),), jnp.float32),
        "modulation_moment": normal_values(streams_of[10], (6, D, D), (0.1 * (IMAGES * SEQ) ** 0.5), 80.0, ((1, 8),), jnp.float32),
        "projection_moment": normal_values(streams_of[11], (3, D, D), (0.6 * (IMAGES * SEQ) ** 0.5), 448.0, ((1, 8),), jnp.float32),
        "output_moment": normal_values(streams_of[12], (D, D), (0.1 * (IMAGES * SEQ) ** 0.5), 80.0, ((0, 8),), jnp.float32),
        "expand_moment": normal_values(streams_of[13], (2, D, FF), (0.1 * (IMAGES * SEQ) ** 0.5), 80.0, ((1, 8),), jnp.float32),
        "shrink_moment": normal_values(streams_of[14], (FF, D), (0.1 * (IMAGES * SEQ) ** 0.5), 80.0, ((1, 8),), jnp.float32),
    }


NORM_EPS = 1e-06
FROBENIUS_EPS = 1e-07
COEFF_FIRST = 3.4445
COEFF_SECOND = -4.775
COEFF_THIRD = 2.0315
MOMENTUM_DECAY = 0.9
LEARN_RATE = 1.0
HIGHEST = lax.Precision.HIGHEST

@jax.custom_vjp
def low(v):
    return lax.optimization_barrier(v.astype(jnp.bfloat16)).astype(jnp.float32)

@jax.custom_vjp
def low_back(v):
    return v

def low_keep(v):
    return (low(v), None)

def low_pass(kept, grad):
    return (grad,)

def back_keep(v):
    return (v, None)

def back_low(kept, grad):
    return (low(grad),)
low.defvjp(low_keep, low_pass)
low_back.defvjp(back_keep, back_low)

def swish_value(values):
    return values / (1.0 + jnp.exp(-values))

def layer_norm(values):
    centred = values - lax.optimization_barrier(jnp.mean(values, axis=-1, keepdims=True))
    return centred * lax.rsqrt(lax.optimization_barrier(jnp.mean(centred * centred, axis=-1, keepdims=True)) + NORM_EPS)

def rotate(tensor):
    first, second, third, fourth = jnp.split(tensor, 4, axis=-1)
    return jnp.concatenate([-second, first, -fourth, third], axis=-1)

def rope_tables(extents):
    quarter = HDIM // 4
    places = jnp.arange(SEQ, dtype=jnp.int32)
    widths = extents[:, 1]
    row_place = (places[None, :] // widths[:, None]).astype(jnp.float32)
    col_place = (places[None, :] % widths[:, None]).astype(jnp.float32)
    frequency = 10000.0 ** (-jnp.arange(quarter).astype(jnp.float32) / quarter)
    row_angle = row_place[:, :, None] * frequency
    col_angle = col_place[:, :, None] * frequency
    cosine_table = jnp.concatenate([jnp.cos(row_angle), jnp.cos(row_angle), jnp.cos(col_angle), jnp.cos(col_angle)], axis=-1)
    sine_table = jnp.concatenate([jnp.sin(row_angle), jnp.sin(row_angle), jnp.sin(col_angle), jnp.sin(col_angle)], axis=-1)
    return (cosine_table[:, :, None, :], sine_table[:, :, None, :])

def block(stream, modulation_weight, projection_weight, output_weight, expand_weight, shrink_weight, activated, key_mask, cosine_table, sine_table):
    images_here = stream.shape[0]
    modulation = low_back(jnp.einsum('bd,kde->kbe', activated, modulation_weight, precision=HIGHEST))
    shift_one, scale_one, gate_one, shift_two, scale_two, gate_two = [modulation[which][:, None, :] for which in range(6)]
    first_input = low(layer_norm(stream) * (1.0 + scale_one) + shift_one)

    def project(matrix):
        return low_back(jnp.einsum('bsd,de->bse', first_input, matrix, precision=HIGHEST)).reshape(images_here, SEQ, HEADS, HDIM)
    queries = project(projection_weight[0])
    keys_all = project(projection_weight[1])
    values_all = project(projection_weight[2])
    query_rot = low(queries * cosine_table + rotate(queries) * sine_table)
    key_rot = low(keys_all * cosine_table + rotate(keys_all) * sine_table)
    value_heads = low(values_all)
    scores = low_back(jnp.einsum('bqhd,bkhd->bhqk', query_rot, key_rot, precision=HIGHEST) * HDIM ** (-0.5))
    scores = jnp.where(key_mask[:, None, None, :], scores, -1000000000.0)
    exponent = jnp.exp(scores - lax.optimization_barrier(jnp.max(scores, axis=-1, keepdims=True)))
    softmax_out = exponent / lax.optimization_barrier(jnp.sum(exponent, axis=-1, keepdims=True))
    softmax_low = low(softmax_out)
    attended = low(low_back(jnp.einsum('bhqk,bkhd->bqhd', softmax_low, value_heads, precision=HIGHEST))).reshape(images_here, SEQ, D)
    attention = low_back(jnp.einsum('bsd,de->bse', attended, output_weight, precision=HIGHEST))
    middle = stream + gate_one * attention
    second_input = low(layer_norm(middle) * (1.0 + scale_two) + shift_two)
    gate_pre = low_back(jnp.einsum('bsd,df->bsf', second_input, expand_weight[0], precision=HIGHEST))
    up_pre = low_back(jnp.einsum('bsd,df->bsf', second_input, expand_weight[1], precision=HIGHEST))
    hidden = low(swish_value(gate_pre) * up_pre)
    branch_out = low_back(jnp.einsum('bsf,fd->bsd', hidden, shrink_weight, precision=HIGHEST))
    return middle + gate_two * branch_out

def orthogonalize(matrix):
    current = matrix / (jnp.sqrt(jnp.sum(matrix * matrix)) + FROBENIUS_EPS)
    for iteration in range(NS_ITERS):
        gram = jnp.dot(current, current.T, precision=HIGHEST)
        poly = COEFF_SECOND * gram + COEFF_THIRD * jnp.dot(gram, gram, precision=HIGHEST)
        current = COEFF_FIRST * current + jnp.dot(poly, current, precision=HIGHEST)
    return current

def reference(inputs, cotangent, image_shape, time_bins, time_table, modulation_master, projection_master, output_master, expand_master, shrink_master, modulation_moment, projection_moment, output_moment, expand_moment, shrink_moment):
    masters = (modulation_master, projection_master, output_master, expand_master, shrink_master)
    moments = (modulation_moment, projection_moment, output_moment, expand_moment, shrink_moment)
    rounded = tuple((low(master) for master in masters))
    group_size = 16
    group_count = IMAGES // group_size
    stream = inputs.astype(jnp.float32).reshape(group_count, group_size, SEQ, D)
    upstream = cotangent.astype(jnp.float32).reshape(group_count, group_size, SEQ, D)
    extents_all = image_shape.reshape(group_count, group_size, 2)
    bins_all = time_bins.reshape(group_count, group_size)

    def one_group(totals, batch):
        tokens, incoming, extents, bin_ids = batch
        activated = low(swish_value(time_table[bin_ids]))
        places = jnp.arange(SEQ, dtype=jnp.int32)
        lengths = extents[:, 0] * extents[:, 1]
        key_mask = places[None, :] < lengths[:, None]
        cosine_table, sine_table = rope_tables(extents)

        def forward(tokens_in, *weights):
            return block(tokens_in, *weights, activated, key_mask, cosine_table, sine_table)
        result, pullback = jax.vjp(forward, tokens, *rounded)
        gradients = pullback(incoming * key_mask[:, :, None].astype(jnp.float32))
        totals = tuple((total + gradient for total, gradient in zip(totals, gradients[1:])))
        return (totals, (result.astype(jnp.bfloat16), gradients[0]))
    initial = tuple((jnp.zeros(master.shape, jnp.float32) for master in masters))
    totals, (outputs, input_grads) = lax.scan(one_group, initial, (stream, upstream, extents_all, bins_all))
    block_output = outputs.reshape(IMAGES, SEQ, D)
    input_gradient = input_grads.reshape(IMAGES, SEQ, D)
    states = tuple((MOMENTUM_DECAY * moment + total for moment, total in zip(moments, totals)))
    feeds = tuple((total + MOMENTUM_DECAY * state for total, state in zip(totals, states)))
    modulation_step = jnp.stack([orthogonalize(feeds[0][which]) for which in range(6)])
    projection_step = jnp.stack([orthogonalize(feeds[1][which]) for which in range(3)])
    output_step = orthogonalize(feeds[2])
    expand_step = jnp.stack([orthogonalize(feeds[3][which]) for which in range(2)]) * (FF / D) ** 0.5
    shrink_step = orthogonalize(feeds[4].T).T
    steps_all = (modulation_step, projection_step, output_step, expand_step, shrink_step)
    updated = tuple((master - LEARN_RATE * step for master, step in zip(masters, steps_all)))
    return (block_output, input_gradient, totals[0], totals[1], totals[2], totals[3], totals[4], updated[0], updated[1], updated[2], updated[3], updated[4], states[0], states[1], states[2], states[3], states[4])
```

```python
import functools
import itertools

import jax
import jax.numpy as jnp
from jax import lax
from jax.experimental import pallas as pl
from jax.experimental.pallas import tpu as pltpu
from jax.sharding import Mesh, PartitionSpec as P

D = 768
HEADS = 12
HDIM = 64
FF = 2048
NS_ITERS = 5
NORM_EPS = 1e-06
FROBENIUS_EPS = 1e-07
COEFF_FIRST = 3.4445
COEFF_SECOND = -4.775
COEFF_THIRD = 2.0315
MOMENTUM_DECAY = 0.9
LEARN_RATE = 1.0
HIGHEST = lax.Precision.HIGHEST
BF16 = jnp.bfloat16
F32 = jnp.float32
ITEMS = 13
NT = (((1,), (1,)), ((), ()))
NN = (((1,), (0,)), ((), ()))
TN = (((0,), (0,)), ((), ()))


def dot(a, b, dims=NN):
    return lax.dot_general(a, b, dims, preferred_element_type=F32)


def newton_schulz_kernel(width, active_ref, feed_ref, left_ref, right_ref, out_ref, x, xb, gram, low, poly):
    tile = 256
    tiles = D // tile
    blocks = width // tile
    spans = [slice(i * tile, (i + 1) * tile) for i in range(tiles)]

    def diagonal(part, other):
        rows = lax.broadcasted_iota(jnp.int32, (tile, tile), 0)
        cols = lax.broadcasted_iota(jnp.int32, (tile, tile), 1)
        return jnp.where(rows == cols, part, other)

    def block(b):
        return pl.ds(pl.multiple_of(b * tile, tile), tile)

    @pl.when(active_ref[0] != 0)
    def _():
        def load(b, acc):
            v = feed_ref[:, block(b)].astype(F32)
            if right_ref is not None:
                v = v + (1.0 + MOMENTUM_DECAY) * dot(left_ref[...], right_ref[:, block(b)], TN)
            x[:, block(b)] = v
            return acc + jnp.sum(v * v, axis=0, keepdims=True)

        total = lax.fori_loop(0, blocks, load, jnp.zeros((1, tile), F32))
        total = jnp.sum(total, keepdims=True)
        inverse = 1.0 / (jnp.sqrt(total) + FROBENIUS_EPS)

        def scale_block(b, carry):
            v = x[:, block(b)] * inverse
            x[:, block(b)] = v
            xb[:, block(b)] = v.astype(BF16)
            return carry

        lax.fori_loop(0, blocks, scale_block, 0)

        def iterate(step, carry):
            trace = jnp.zeros((1, tile), F32)
            for i in range(tiles):
                for j in range(i + 1):
                    part = dot(xb[spans[i], :], xb[spans[j], :], NT)
                    gram[spans[i], spans[j]] = part
                    if i == j:
                        trace = trace + jnp.sum(diagonal(part, 0.0), axis=0, keepdims=True)
                    else:
                        lower = part.astype(BF16)
                        low[spans[i], spans[j]] = lower
                        low[spans[j], spans[i]] = lower.T
            shift = jnp.sum(trace, keepdims=True) / D
            for i in range(tiles):
                part = gram[spans[i], spans[i]]
                part = diagonal(part - shift, part)
                gram[spans[i], spans[i]] = part
                low[spans[i], spans[i]] = part.astype(BF16)
            linear = COEFF_SECOND + 2.0 * COEFF_THIRD * shift
            level = COEFF_SECOND * shift + COEFF_THIRD * shift * shift
            trace = jnp.zeros((1, tile), F32)
            for i in range(tiles):
                for j in range(i + 1):
                    part = linear * gram[spans[i], spans[j]] + COEFF_THIRD * dot(
                        low[spans[i], :], low[spans[j], :], NT
                    )
                    if i == j:
                        gram[spans[i], spans[j]] = part
                        trace = trace + jnp.sum(diagonal(part, 0.0), axis=0, keepdims=True)
                    else:
                        lower = part.astype(BF16)
                        poly[spans[i], spans[j]] = lower
                        poly[spans[j], spans[i]] = lower.T
            mean = jnp.sum(trace, keepdims=True) / D
            for i in range(tiles):
                part = gram[spans[i], spans[i]]
                poly[spans[i], spans[i]] = diagonal(part - mean, part).astype(BF16)
            scale = COEFF_FIRST + level + mean

            def update(b, inner):
                new = scale * x[:, block(b)] + dot(poly[...], xb[:, block(b)])
                x[:, block(b)] = new
                xb[:, block(b)] = new.astype(BF16)
                return inner

            lax.fori_loop(0, blocks, update, 0)
            return carry

        lax.fori_loop(0, NS_ITERS, iterate, 0)
        out_ref[...] = xb[...]

    @pl.when(active_ref[0] == 0)
    def _():
        out_ref[...] = jnp.zeros_like(out_ref)


def newton_schulz(active, feed, left=None, right=None):
    width = feed.shape[1]
    operands = [active.reshape(1).astype(jnp.int32), feed]
    if left is None:

        def body(active_ref, feed_ref, *rest):
            newton_schulz_kernel(width, active_ref, feed_ref, None, None, *rest)

    else:
        body = functools.partial(newton_schulz_kernel, width)
        operands += [left, right]
    vmem = pl.BlockSpec(memory_space=pltpu.VMEM)
    return pl.pallas_call(
        body,
        out_shape=jax.ShapeDtypeStruct((D, width), BF16),
        in_specs=[pl.BlockSpec(memory_space=pltpu.SMEM)] + [vmem] * (len(operands) - 1),
        out_specs=vmem,
        scratch_shapes=[
            pltpu.VMEM((D, width), F32),
            pltpu.VMEM((D, width), BF16),
            pltpu.VMEM((D, D), F32),
            pltpu.VMEM((D, D), BF16),
            pltpu.VMEM((D, D), BF16),
        ],
        compiler_params=pltpu.CompilerParams(vmem_limit_bytes=40 * 1024 * 1024),
        cost_estimate=pl.CostEstimate(
            flops=NS_ITERS * 4 * D * D * (width + D), bytes_accessed=4 * D * width, transcendentals=0
        ),
        name="newton_schulz",
    )(*operands)


def tie(value, *others):
    return lax.optimization_barrier((value, *others))[0]


def place(parts, slots, lead=None, moves=None):
    count = len(parts)
    if lead is None:
        lead = (count, *parts[0].shape[:-2])
        moves = lambda slot: [(i, (), (slot[i],)) for i in range(count)]
    total = len(moves([0] * len(slots)))

    def body(slot_ref, *refs):
        ins, out, sem = refs[:count], refs[count], refs[count + 1]
        copies = []
        for i, (part, source, target) in enumerate(moves(slot_ref)):
            from_ref = ins[part].at[source] if source else ins[part]
            copies.append(pltpu.make_async_copy(from_ref, out.at[target], sem.at[i]))
        for copy in copies:
            copy.start()
        for copy in copies:
            copy.wait()

    size = count * parts[0].size * parts[0].dtype.itemsize
    return pl.pallas_call(
        body,
        out_shape=jax.ShapeDtypeStruct((*lead, *parts[0].shape[-2:]), parts[0].dtype),
        in_specs=[pl.BlockSpec(memory_space=pltpu.SMEM)]
        + [pl.BlockSpec(memory_space=pl.ANY)] * count,
        out_specs=pl.BlockSpec(memory_space=pl.ANY),
        scratch_shapes=[pltpu.SemaphoreType.DMA((total,))],
        cost_estimate=pl.CostEstimate(flops=0, bytes_accessed=2 * size, transcendentals=0),
        name="place",
    )(jnp.stack(slots).astype(jnp.int32), *parts)


def every(*sizes):
    return list(itertools.product(*[range(size) for size in sizes]))


class Plain:
    images = ("dp", "fsdp")
    rows = "fsdp"
    wide_parts = 1

    def __init__(self, mesh):
        self.mesh = mesh
        self.row_shards = mesh.shape["fsdp"]
        self.owners = mesh.shape["fsdp"]
        self.wide_slots = [(i, 0) for i in range(3)]
        self.wide_slots += [None] * (self.owners - 3)
        self.slots = [None] * 3 + list(range(10))
        self.slots += [None] * (self.owners - ITEMS)

    def row_index(self):
        return lax.axis_index("fsdp")

    def group_index(self):
        return lax.axis_index("dp")

    def owner_index(self):
        return lax.axis_index("fsdp")

    def gather_weights(self, chunks):
        gathered = []
        for left, right in chunks:
            gathered.append(
                [lax.all_gather(half, "fsdp", axis=0, tiled=True) for half in (left, right)]
            )
        return gathered

    def gather_images(self, value):
        return lax.all_gather(value, ("dp", "fsdp"), axis=0, tiled=True)

    def sum_group(self, value):
        return lax.psum_scatter(value, "fsdp", scatter_dimension=0, tiled=True)

    def reduce_core(self, partial):
        return partial

    def reduce_first(self, value):
        return value

    def reduce_second(self, value):
        return value

    def reduce_last(self, value):
        shard = lax.psum_scatter(value, "fsdp", scatter_dimension=0, tiled=True)
        return lax.psum(shard.astype(F32), "dp")

    def own_rows(self, shard, dim=-2):
        return shard

    def complete(self, piece):
        return piece

    def to_owners(self, pieces):
        got = lax.all_to_all(pieces, "fsdp", split_axis=0, concat_axis=0, tiled=True)
        return got.reshape(-1, got.shape[2])

    def to_rows(self, whole):
        blocks = whole.reshape(self.row_shards, -1, whole.shape[1])
        return lax.all_to_all(blocks, "fsdp", split_axis=0, concat_axis=0, tiled=True)


class Torus:
    images = ("x", "c", "z", "y")
    rows = ("z", "y")
    chips = ("x", "z", "y")
    wide_parts = 2

    def __init__(self, mesh):
        self.mesh = Mesh(mesh.devices.reshape(2, 2, 4, 2), ("x", "c", "z", "y"))
        self.row_shards = 8
        self.owners = 16
        wide_places = [(1, 0), (2, 1), (1, 1)]
        self.wide_slots = [None] * 16
        self.slots = [None] * 16
        for item, (z, y) in enumerate(wide_places):
            for part in range(2):
                self.wide_slots[(part * 4 + z) * 2 + y] = (item, part)
        free = [i for i in range(16) if self.wide_slots[i] is None]
        for item, slot in enumerate(free):
            self.slots[slot] = item

    def row_index(self):
        return lax.axis_index("z") * 2 + lax.axis_index("y")

    def group_index(self):
        return lax.axis_index("x") * 2 + lax.axis_index("c")

    def owner_index(self):
        return (lax.axis_index("x") * 4 + lax.axis_index("z")) * 2 + lax.axis_index("y")

    def swap(self, value, axis):
        return lax.ppermute(value, axis, [(0, 1), (1, 0)])

    def shift(self, value, by):
        return lax.ppermute(value, "z", [(i, (i + by) % 4) for i in range(4)])

    def exchange(self, value, axis):
        here = lax.axis_index(axis)
        return place([value, self.swap(value, axis)], [here, 1 - here])

    def spread_z(self, value):
        z = lax.axis_index("z")
        ring = [value] + [self.shift(value, by) for by in range(1, 4)]
        return place(ring, [(z - by) % 4 for by in range(4)])

    def gather_weights(self, chunks):
        spread = []
        for left, right in chunks:
            left, right = self.own_rows(left), self.own_rows(right)
            if spread:
                left, right = lax.optimization_barrier((left, right, *spread[-1]))[:2]
            spread.append((self.spread_z(left), self.spread_z(right)))
        done = []
        for left, right in spread:
            if done:
                left, right = lax.optimization_barrier((left, right, *done[-1]))[:2]
            left = self.exchange(left, "y")
            right = self.exchange(right, "x")
            left = self.exchange(left, "x")
            right = self.exchange(right, "y")
            done.append((left, right))
        full = []
        for left, right in done:
            pair = []
            for half, order in ((left, (2, 1, 0)), (right, (2, 0, 1))):
                c = lax.axis_index("c")

                def moves(slot, order=order):
                    found = []
                    for part in range(2):
                        for at in every(2, 2, 4):
                            found.append((part, at, (*[at[i] for i in order], slot[part])))
                    return found

                whole = place([half, self.swap(half, "c")], [c, 1 - c], (4, 2, 2, 2), moves)
                pair.append(whole.reshape(D, -1))
            full.append(pair)
        return full

    def gather_images(self, value):
        shape = (64,) + value.shape[1:]

        def both(v, axis):
            other = self.swap(v, axis)
            first = lax.axis_index(axis) == 0
            return jnp.where(first, jnp.stack([v, other]), jnp.stack([other, v]))

        z = lax.axis_index("z")
        value = both(value, "y")
        ring = jnp.stack([value] + [self.shift(value, by) for by in range(1, 4)])
        value = jnp.take(ring, (z - jnp.arange(4)) % 4, axis=0)
        value = both(value, "c")
        value = both(value, "x")
        return value.reshape(shape)

    def sum_group(self, value):
        blocks = value.reshape(8, -1, *value.shape[1:])
        got = lax.all_to_all(blocks, ("z", "y"), split_axis=0, concat_axis=0, tiled=True)
        return jnp.sum(got, axis=0)

    def halve(self, value, axis, dim):
        here = lax.axis_index(axis)
        take = lambda at: lax.dynamic_index_in_dim(value, at, dim, keepdims=False)
        got = self.swap(take(1 - here), axis)
        return (take(here).astype(F32) + got.astype(F32)).astype(BF16)

    def reduce_core(self, partial):
        return self.halve(partial.reshape(4, 2, 2, 2, D // 32, partial.shape[1]), "c", 3)

    def reduce_first(self, value):
        half = value.shape[-1] // 2
        return (
            self.halve(value[..., :half], "x", 2),
            self.halve(value[..., half:], "y", 1),
        )

    def reduce_second(self, value):
        left = self.halve(value[0], "y", 1)
        right = self.halve(value[1], "x", 1)
        return jnp.concatenate([left, right], axis=-1)

    def reduce_last(self, value):
        z = lax.axis_index("z")
        take = lambda at: lax.dynamic_index_in_dim(value, at, 0, keepdims=False)
        got = [self.shift(take((z + by) % 4), by) for by in range(1, 4)]
        total = take(z).astype(F32)
        for part in got:
            total = total + part.astype(F32)
        return total

    def own_rows(self, shard, dim=-2):
        return lax.dynamic_slice_in_dim(
            shard, self.group_index() * (D // 32), D // 32, dim % shard.ndim
        )

    def complete(self, piece):
        value = self.exchange(piece, "x")
        c = lax.axis_index("c")
        moves = lambda slot: [(part, (x,), (x, slot[part])) for part in range(2) for x in range(2)]
        value = place([value, self.swap(value, "c")], [c, 1 - c], (2, 2), moves)
        return value.reshape(D // 8, -1)

    def to_owners(self, pieces):
        cols = pieces.shape[2]
        got = lax.all_to_all(pieces, self.chips, split_axis=0, concat_axis=0, tiled=True)
        got = got.reshape(2, 4, 2, D // 32, cols)
        c = lax.axis_index("c")

        def moves(slot):
            return [
                (part, (x, z, y), (z, y, x, slot[part]))
                for part in range(2)
                for x, z, y in every(2, 4, 2)
            ]

        whole = place([got, self.swap(got, "c")], [c, 1 - c], (4, 2, 2, 2), moves)
        return whole.reshape(D, cols)

    def to_rows(self, whole):
        cols = whole.shape[1]
        blocks = whole.reshape(4, 2, 2, 2, D // 32, cols)
        blocks = lax.dynamic_index_in_dim(blocks, lax.axis_index("c"), 3, keepdims=False)
        blocks = blocks.transpose(2, 0, 1, 3, 4).reshape(16, D // 32, cols)
        return lax.all_to_all(blocks, self.chips, split_axis=0, concat_axis=0, tiled=True)


def swish_value(values):
    return values / (1.0 + jnp.exp(-values))


def layer_norm(values):
    centred = values - jnp.mean(values, axis=-1, keepdims=True)
    inverse = lax.rsqrt(jnp.mean(centred * centred, axis=-1, keepdims=True) + NORM_EPS)
    return (centred * inverse, inverse)


def norm_back(incoming, normed, inverse):
    return inverse * (
        incoming
        - jnp.mean(incoming, axis=-1, keepdims=True)
        - normed * jnp.mean(incoming * normed, axis=-1, keepdims=True)
    )


def rotate(tensor):
    first, second, third, fourth = jnp.split(tensor, 4, axis=-1)
    return jnp.concatenate([-second, first, -fourth, third], axis=-1)


def rope_tables(extents, positions):
    quarter = HDIM // 4
    places = jnp.arange(positions, dtype=jnp.int32)
    widths = extents[:, 1]
    row_place = (places[None, :] // widths[:, None]).astype(F32)
    col_place = (places[None, :] % widths[:, None]).astype(F32)
    frequency = 10000.0 ** (-jnp.arange(quarter).astype(F32) / quarter)
    row_angle = row_place[:, :, None] * frequency
    col_angle = col_place[:, :, None] * frequency
    cosine_table = jnp.concatenate(
        [jnp.cos(row_angle), jnp.cos(row_angle), jnp.cos(col_angle), jnp.cos(col_angle)], axis=-1
    )
    sine_table = jnp.concatenate(
        [jnp.sin(row_angle), jnp.sin(row_angle), jnp.sin(col_angle), jnp.sin(col_angle)], axis=-1
    )
    return (cosine_table[:, :, None, :], sine_table[:, :, None, :])


def local(
    comm,
    inputs,
    cotangent,
    image_shape,
    time_bins,
    time_table,
    modulation_master,
    projection_master,
    output_master,
    expand_master,
    shrink_master,
    modulation_moment,
    projection_moment,
    output_moment,
    expand_moment,
    shrink_moment,
):
    masters = (modulation_master, projection_master, output_master, expand_master, shrink_master)
    moments = (modulation_moment, projection_moment, output_moment, expand_moment, shrink_moment)
    images, positions, features = inputs.shape
    tokens = images * positions
    rows = modulation_master.shape[1]
    row_index = comm.row_index()

    shrink_low = shrink_master.astype(BF16).T
    chunks = comm.gather_weights(
        [
            (
                jnp.concatenate([projection_master[0], projection_master[1]], axis=1).astype(BF16),
                jnp.concatenate([projection_master[2], output_master], axis=1).astype(BF16),
            ),
            (expand_master[0].astype(BF16), expand_master[1].astype(BF16)),
            (shrink_low[:, : FF // 2], shrink_low[:, FF // 2 :]),
        ]
    )
    (query_key_weight, value_output_weight), (gate_weight, up_weight) = chunks[:2]
    value_weight = value_output_weight[:, :D]
    output_weight = value_output_weight[:, D:]
    shrink_left, shrink_right = chunks[2]

    bins = comm.gather_images(time_bins)
    selector = (
        bins[:, None] == jnp.arange(time_table.shape[0], dtype=jnp.int32)[None, :]
    ).astype(F32)
    active = swish_value(jnp.dot(selector, time_table, precision=HIGHEST)).astype(BF16)
    active_rows = lax.dynamic_slice_in_dim(active, row_index * rows, rows, 1)
    group_images = images * comm.row_shards
    active_group = lax.dynamic_slice_in_dim(
        active_rows, comm.group_index() * group_images, group_images, 0
    )
    modulation = comm.sum_group(
        jnp.einsum(
            "bd,kde->bke", active_group, modulation_master.astype(BF16), preferred_element_type=F32
        )
    )
    shift_one, scale_one, gate_one, shift_two, scale_two, gate_two = [
        modulation[:, which, None, :] for which in range(6)
    ]

    stream = inputs.astype(F32)
    places = jnp.arange(positions, dtype=jnp.int32)
    lengths = image_shape[:, 0] * image_shape[:, 1]
    key_mask = places[None, :] < lengths[:, None]
    cosine_table, sine_table = rope_tables(image_shape, positions)

    def product(left, right, dims=NN):
        return dot(left.reshape(tokens, -1), right, dims).reshape(images, positions, -1)

    def outer(left, right):
        return dot(left.reshape(tokens, -1), right.reshape(tokens, -1), TN).astype(BF16)

    def split_heads(value):
        return value.reshape(images, positions, HEADS, HDIM)

    normed_one, inverse_one = layer_norm(stream)
    first_input = (normed_one * (1.0 + scale_one) + shift_one).astype(BF16)
    query_key = product(first_input, query_key_weight)
    queries, keys = split_heads(query_key[..., :D]), split_heads(query_key[..., D:])
    value_heads = split_heads(product(first_input, value_weight).astype(BF16))
    query_rot = (queries * cosine_table + rotate(queries) * sine_table).astype(BF16)
    key_rot = (keys * cosine_table + rotate(keys) * sine_table).astype(BF16)
    scores = jnp.einsum(
        "bqhd,bkhd->bhqk", query_rot, key_rot, preferred_element_type=F32
    ) * HDIM ** (-0.5)
    scores = jnp.where(key_mask[:, None, None, :], scores, -1000000000.0)
    exponent = jnp.exp(scores - jnp.max(scores, axis=-1, keepdims=True))
    softmax_out = exponent / jnp.sum(exponent, axis=-1, keepdims=True)
    softmax_low = softmax_out.astype(BF16)
    attended = jnp.einsum(
        "bhqk,bkhd->bqhd", softmax_low, value_heads, preferred_element_type=F32
    )
    attended = attended.astype(BF16).reshape(images, positions, features)
    attention = product(attended, output_weight)
    middle = stream + gate_one * attention
    normed_two, inverse_two = layer_norm(middle)
    second_input = (normed_two * (1.0 + scale_two) + shift_two).astype(BF16)
    gate_pre = product(second_input, gate_weight)
    up_pre = product(second_input, up_weight)
    sigmoid_gate = 1.0 / (1.0 + jnp.exp(-gate_pre))
    hidden = (swish_value(gate_pre) * up_pre).astype(BF16)
    branch_out = product(hidden[..., : FF // 2], shrink_left, NT) + product(
        hidden[..., FF // 2 :], shrink_right, NT
    )
    block_output = (middle + gate_two * branch_out).astype(BF16)

    upstream = cotangent.astype(F32) * key_mask[:, :, None].astype(F32)
    grad_gate_two = jnp.sum(upstream * branch_out, axis=1)
    grad_branch = (gate_two * upstream).astype(BF16)
    shrink_sum = comm.reduce_core(outer(grad_branch, hidden))
    grad_hidden = jnp.concatenate(
        [product(grad_branch, shrink_left), product(grad_branch, shrink_right)], axis=-1
    )
    grad_gate = grad_hidden * up_pre * sigmoid_gate * (1.0 + gate_pre * (1.0 - sigmoid_gate))
    grad_up = grad_hidden * gate_pre * sigmoid_gate
    grad_gate, grad_up = grad_gate.astype(BF16), grad_up.astype(BF16)
    grad_gate, grad_up, shrink_sum = lax.optimization_barrier((grad_gate, grad_up, shrink_sum))
    expand_sum = comm.reduce_core(
        outer(second_input, jnp.concatenate([grad_gate, grad_up], axis=-1))
    )
    shrink_sum = comm.reduce_first(shrink_sum)
    grad_second = product(grad_gate, gate_weight, NT) + product(grad_up, up_weight, NT)
    grad_scale_two = jnp.sum(grad_second * normed_two, axis=1)
    grad_shift_two = jnp.sum(grad_second, axis=1)
    grad_stream = upstream + norm_back(grad_second * (1.0 + scale_two), normed_two, inverse_two)
    grad_stream, shrink_sum, expand_sum = lax.optimization_barrier(
        (grad_stream, shrink_sum, expand_sum)
    )
    shrink_sum = comm.reduce_second(shrink_sum)
    expand_sum = comm.reduce_first(expand_sum)
    grad_gate_one = jnp.sum(grad_stream * attention, axis=1)
    grad_attention = (gate_one * grad_stream).astype(BF16)
    grad_output = outer(attended, grad_attention)
    grad_attended = split_heads(product(grad_attention, output_weight, NT).astype(BF16))
    grad_soft = jnp.einsum(
        "bqhd,bkhd->bhqk", grad_attended, value_heads, preferred_element_type=F32
    )
    grad_values = jnp.einsum(
        "bhqk,bqhd->bkhd", softmax_low, grad_attended, preferred_element_type=F32
    )
    grad_scores = softmax_out * (
        grad_soft - jnp.sum(grad_soft * softmax_out, axis=-1, keepdims=True)
    )
    grad_scores = grad_scores.astype(BF16)
    grad_scores, shrink_sum, expand_sum = lax.optimization_barrier(
        (grad_scores, shrink_sum, expand_sum)
    )
    shrink_piece = comm.reduce_last(shrink_sum)
    expand_sum = comm.reduce_second(expand_sum)
    grad_qrot = jnp.einsum(
        "bhqk,bkhd->bqhd", grad_scores, key_rot, preferred_element_type=F32
    ) * HDIM ** (-0.5)
    grad_krot = jnp.einsum(
        "bhqk,bqhd->bkhd", grad_scores, query_rot, preferred_element_type=F32
    ) * HDIM ** (-0.5)
    grad_query = grad_qrot * cosine_table - rotate(grad_qrot * sine_table)
    grad_key = grad_krot * cosine_table - rotate(grad_krot * sine_table)
    grad_project_in = jnp.concatenate(
        [
            v.astype(BF16).reshape(images, positions, features)
            for v in (grad_query, grad_key, grad_values)
        ],
        axis=-1,
    )
    grad_project_in, shrink_piece, expand_sum = lax.optimization_barrier(
        (grad_project_in, shrink_piece, expand_sum)
    )
    expand_piece = comm.reduce_last(expand_sum)
    grad_projection = outer(first_input, grad_project_in)
    attention_sum = comm.reduce_core(jnp.concatenate([grad_projection, grad_output], axis=1))
    grad_first = product(grad_project_in[..., : 2 * D], query_key_weight, NT) + product(
        grad_project_in[..., 2 * D :], value_weight, NT
    )
    grad_scale_one = jnp.sum(grad_first * normed_one, axis=1)
    grad_shift_one = jnp.sum(grad_first, axis=1)
    input_gradient = grad_stream + norm_back(
        grad_first * (1.0 + scale_one), normed_one, inverse_one
    )
    grad_modulation = jnp.concatenate(
        [
            grad_shift_one,
            grad_scale_one,
            grad_gate_one,
            grad_shift_two,
            grad_scale_two,
            grad_gate_two,
        ],
        axis=1,
    ).astype(BF16)
    grad_modulation, attention_sum = lax.optimization_barrier((grad_modulation, attention_sum))
    attention_sum = comm.reduce_first(attention_sum)
    grad_modulation = comm.gather_images(grad_modulation)

    def feed_of(piece, moment):
        return (
            (1.0 + MOMENTUM_DECAY) * piece + MOMENTUM_DECAY * MOMENTUM_DECAY * moment
        ).astype(BF16)

    owner = comm.owner_index()
    wide_feed = [
        feed_of(expand_piece[:, :FF], comm.own_rows(expand_moment[0])),
        feed_of(expand_piece[:, FF:], comm.own_rows(expand_moment[1])),
        feed_of(shrink_piece, comm.own_rows(shrink_moment.T)),
    ]
    empty = jnp.zeros_like(wide_feed[0])
    wide = comm.to_owners(
        jnp.stack([empty if slot is None else wide_feed[slot[0]] for slot in comm.wide_slots])
    )
    active_wide = jnp.array([0 if slot is None else 1 for slot in comm.wide_slots], jnp.int32)[owner]
    wide = newton_schulz(active_wide, wide)
    attention_sum = comm.reduce_second(attention_sum)
    if comm.wide_parts > 1:
        part = jnp.array([0 if slot is None else slot[1] for slot in comm.wide_slots])[owner]
        size = FF // comm.wide_parts
        wide = lax.dynamic_slice_in_dim(wide, part * size, size, 1)
    wide_back = comm.to_rows(wide)

    attention_piece = comm.reduce_last(attention_sum)
    decay = MOMENTUM_DECAY * MOMENTUM_DECAY
    own_moment = comm.own_rows(modulation_moment)
    square_feed = [(decay * own_moment[k]).astype(BF16) for k in range(6)]
    for k in range(3):
        square_feed.append(
            feed_of(attention_piece[:, k * D : (k + 1) * D], comm.own_rows(projection_moment[k]))
        )
    square_feed.append(feed_of(attention_piece[:, 3 * D :], comm.own_rows(output_moment)))
    empty = jnp.zeros_like(square_feed[0])
    square = comm.to_owners(
        jnp.stack([empty if slot is None else square_feed[slot] for slot in comm.slots])
    )
    item = jnp.array([-1 if slot is None else slot for slot in comm.slots], jnp.int32)[owner]
    by_map = jnp.concatenate(
        [grad_modulation.reshape(-1, 6, D), jnp.zeros((grad_modulation.shape[0], 1, D), BF16)], axis=1
    )
    which = jnp.where((item >= 0) & (item < 6), item, 6)
    right = lax.dynamic_index_in_dim(by_map, which, 1, keepdims=False)
    square = newton_schulz((item >= 0).astype(jnp.int32), square, active, right)
    square_back = comm.to_rows(square)

    totals_low = comm.complete(
        jnp.concatenate([expand_piece, shrink_piece, attention_piece], axis=1).astype(BF16)
    ).astype(F32)
    wide_parts = [
        wide_back[comm.wide_slots.index((i, p))]
        for i in range(3)
        for p in range(comm.wide_parts)
    ]
    steps = comm.complete(
        jnp.concatenate(wide_parts + [square_back[comm.slots.index(i)] for i in range(10)], axis=1)
    ).astype(F32)
    modulation_total = jnp.einsum(
        "bd,bke->kde",
        active_rows,
        grad_modulation.reshape(-1, 6, features),
        preferred_element_type=F32,
    )
    after = 3 * FF
    totals = (
        modulation_total,
        jnp.stack([totals_low[:, after + i * D : after + (i + 1) * D] for i in range(3)]),
        totals_low[:, after + 3 * D :],
        jnp.stack([totals_low[:, :FF], totals_low[:, FF : 2 * FF]]),
        totals_low[:, 2 * FF : after].T,
    )
    states = tuple((MOMENTUM_DECAY * moment + total for moment, total in zip(moments, totals)))
    square_step = [steps[:, after + i * D : after + (i + 1) * D] for i in range(10)]
    steps_all = (
        jnp.stack(square_step[:6]),
        jnp.stack(square_step[6:9]),
        square_step[9],
        jnp.stack([steps[:, :FF], steps[:, FF : 2 * FF]]) * (FF / D) ** 0.5,
        steps[:, 2 * FF : after].T,
    )
    updated = tuple((master - LEARN_RATE * step for master, step in zip(masters, steps_all)))
    return (block_output, input_gradient, *totals, *updated, *states)


def solution(mesh):
    if mesh.shape["dp"] == 4 and mesh.shape["fsdp"] == 8:
        comm = Torus(mesh)
    else:
        comm = Plain(mesh)
    images, rows = comm.images, comm.rows
    by_row = (
        P(None, rows, None),
        P(None, rows, None),
        P(rows, None),
        P(None, rows, None),
        P(None, rows),
    )
    return jax.shard_map(
        functools.partial(local, comm),
        mesh=comm.mesh,
        in_specs=(
            P(images, None, None),
            P(images, None, None),
            P(images, None),
            P(images),
            P(),
            *by_row,
            *by_row,
        ),
        out_specs=(P(images, None, None), P(images, None, None), *by_row, *by_row, *by_row),
        check_vma=False,
    )
```

```python
import functools
import itertools

import jax
import jax.numpy as jnp
from jax import lax
from jax.experimental import pallas as pl
from jax.experimental.pallas import tpu as pltpu
from jax.sharding import Mesh, PartitionSpec as P

D = 768
HEADS = 12
HDIM = 64
FF = 2048
NS_ITERS = 5
NORM_EPS = 1e-06
FROBENIUS_EPS = 1e-07
COEFF_FIRST = 3.4445
COEFF_SECOND = -4.775
COEFF_THIRD = 2.0315
MOMENTUM_DECAY = 0.9
LEARN_RATE = 1.0
HIGHEST = lax.Precision.HIGHEST
BF16 = jnp.bfloat16
F32 = jnp.float32
ITEMS = 13
NT = (((1,), (1,)), ((), ()))
NN = (((1,), (0,)), ((), ()))
TN = (((0,), (0,)), ((), ()))


def dot(a, b, dims=NN):
    return lax.dot_general(a, b, dims, preferred_element_type=F32)


def newton_schulz_kernel(width, active_ref, feed_ref, left_ref, right_ref, out_ref, x, xb, gram, low, poly):
    tile = 256
    tiles = D // tile
    blocks = width // tile
    spans = [slice(i * tile, (i + 1) * tile) for i in range(tiles)]

    def diagonal(part, other):
        rows = lax.broadcasted_iota(jnp.int32, (tile, tile), 0)
        cols = lax.broadcasted_iota(jnp.int32, (tile, tile), 1)
        return jnp.where(rows == cols, part, other)

    def block(b):
        return pl.ds(pl.multiple_of(b * tile, tile), tile)

    @pl.when(active_ref[0] != 0)
    def _():
        def load(b, acc):
            v = feed_ref[:, block(b)].astype(F32)
            if right_ref is not None:
                v = v + (1.0 + MOMENTUM_DECAY) * dot(left_ref[...], right_ref[:, block(b)], TN)
            x[:, block(b)] = v
            return acc + jnp.sum(v * v, axis=0, keepdims=True)

        total = lax.fori_loop(0, blocks, load, jnp.zeros((1, tile), F32))
        total = jnp.sum(total, keepdims=True)
        inverse = 1.0 / (jnp.sqrt(total) + FROBENIUS_EPS)

        def scale_block(b, carry):
            v = x[:, block(b)] * inverse
            x[:, block(b)] = v
            xb[:, block(b)] = v.astype(BF16)
            return carry

        lax.fori_loop(0, blocks, scale_block, 0)

        def iterate(step, carry):
            trace = jnp.zeros((1, tile), F32)
            for i in range(tiles):
                for j in range(i + 1):
                    part = dot(xb[spans[i], :], xb[spans[j], :], NT)
                    gram[spans[i], spans[j]] = part
                    if i == j:
                        trace = trace + jnp.sum(diagonal(part, 0.0), axis=0, keepdims=True)
                    else:
                        lower = part.astype(BF16)
                        low[spans[i], spans[j]] = lower
                        low[spans[j], spans[i]] = lower.T
            shift = jnp.sum(trace, keepdims=True) / D
            for i in range(tiles):
                part = gram[spans[i], spans[i]]
                part = diagonal(part - shift, part)
                gram[spans[i], spans[i]] = part
                low[spans[i], spans[i]] = part.astype(BF16)
            linear = COEFF_SECOND + 2.0 * COEFF_THIRD * shift
            level = COEFF_SECOND * shift + COEFF_THIRD * shift * shift
            trace = jnp.zeros((1, tile), F32)
            for i in range(tiles):
                for j in range(i + 1):
                    part = linear * gram[spans[i], spans[j]] + COEFF_THIRD * dot(
                        low[spans[i], :], low[spans[j], :], NT
                    )
                    if i == j:
                        gram[spans[i], spans[j]] = part
                        trace = trace + jnp.sum(diagonal(part, 0.0), axis=0, keepdims=True)
                    else:
                        lower = part.astype(BF16)
                        poly[spans[i], spans[j]] = lower
                        poly[spans[j], spans[i]] = lower.T
            mean = jnp.sum(trace, keepdims=True) / D
            for i in range(tiles):
                part = gram[spans[i], spans[i]]
                poly[spans[i], spans[i]] = diagonal(part - mean, part).astype(BF16)
            scale = COEFF_FIRST + level + mean

            def update(b, inner):
                new = scale * x[:, block(b)] + dot(poly[...], xb[:, block(b)])
                x[:, block(b)] = new
                xb[:, block(b)] = new.astype(BF16)
                return inner

            lax.fori_loop(0, blocks, update, 0)
            return carry

        lax.fori_loop(0, NS_ITERS, iterate, 0)
        out_ref[...] = xb[...]

    @pl.when(active_ref[0] == 0)
    def _():
        out_ref[...] = jnp.zeros_like(out_ref)


def newton_schulz(active, feed, left=None, right=None):
    width = feed.shape[1]
    operands = [active.reshape(1).astype(jnp.int32), feed]
    if left is None:

        def body(active_ref, feed_ref, *rest):
            newton_schulz_kernel(width, active_ref, feed_ref, None, None, *rest)

    else:
        body = functools.partial(newton_schulz_kernel, width)
        operands += [left, right]
    vmem = pl.BlockSpec(memory_space=pltpu.VMEM)
    return pl.pallas_call(
        body,
        out_shape=jax.ShapeDtypeStruct((D, width), BF16),
        in_specs=[pl.BlockSpec(memory_space=pltpu.SMEM)] + [vmem] * (len(operands) - 1),
        out_specs=vmem,
        scratch_shapes=[
            pltpu.VMEM((D, width), F32),
            pltpu.VMEM((D, width), BF16),
            pltpu.VMEM((D, D), F32),
            pltpu.VMEM((D, D), BF16),
            pltpu.VMEM((D, D), BF16),
        ],
        compiler_params=pltpu.CompilerParams(vmem_limit_bytes=40 * 1024 * 1024),
        cost_estimate=pl.CostEstimate(
            flops=NS_ITERS * 4 * D * D * (width + D), bytes_accessed=4 * D * width, transcendentals=0
        ),
        name="newton_schulz",
    )(*operands)


def tie(value, *others):
    return lax.optimization_barrier((value, *others))[0]


def place(parts, slots, lead=None, moves=None):
    count = len(parts)
    if lead is None:
        lead = (count, *parts[0].shape[:-2])
        moves = lambda slot: [(i, (), (slot[i],)) for i in range(count)]

    def body(slot_ref, *refs):
        ins, out = refs[:count], refs[count]
        for part, source, target in moves(slot_ref):
            out[target] = ins[part][source] if source else ins[part][...]

    size = count * parts[0].size * parts[0].dtype.itemsize
    vmem = pl.BlockSpec(memory_space=pltpu.VMEM)
    return pl.pallas_call(
        body,
        out_shape=jax.ShapeDtypeStruct((*lead, *parts[0].shape[-2:]), parts[0].dtype),
        in_specs=[pl.BlockSpec(memory_space=pltpu.SMEM)] + [vmem] * count,
        out_specs=vmem,
        cost_estimate=pl.CostEstimate(flops=0, bytes_accessed=2 * size, transcendentals=0),
        compiler_params=pltpu.CompilerParams(vmem_limit_bytes=24 * 1024 * 1024),
        name="place",
    )(jnp.stack(slots).astype(jnp.int32), *parts)


def place_halves(parts, slots):
    count = len(parts)
    rows, cols = parts[0].shape
    half = cols // 2

    def body(slot_ref, *refs):
        left, right = refs[count:]
        for i, ref in enumerate(refs[:count]):
            left[slot_ref[i]] = ref[:, :half]
            right[slot_ref[i]] = ref[:, half:]

    vmem = pl.BlockSpec(memory_space=pltpu.VMEM)
    shape = jax.ShapeDtypeStruct((count, rows, half), parts[0].dtype)
    return pl.pallas_call(
        body,
        out_shape=(shape, shape),
        in_specs=[pl.BlockSpec(memory_space=pltpu.SMEM)] + [vmem] * count,
        out_specs=(vmem, vmem),
        cost_estimate=pl.CostEstimate(flops=0, bytes_accessed=16 * rows * cols, transcendentals=0),
        compiler_params=pltpu.CompilerParams(vmem_limit_bytes=24 * 1024 * 1024),
        name="place_halves",
    )(jnp.stack(slots).astype(jnp.int32), *parts)


def slots_of(feeds, owners, width):
    arrays, index = [], {}

    def note(array):
        if array is None:
            return None
        source, columns = array
        if id(source) not in index:
            index[id(source)] = len(arrays)
            arrays.append(source)
        return (index[id(source)], columns)

    noted = [[(note(total), note(moment)) for total, moment in feed] for feed in feeds]
    rows = arrays[0].shape[-2]

    def body(*refs):
        out = refs[-1]

        def read(what):
            place_of, (lead, start, size) = what
            ref = refs[place_of]
            return ref[(*lead, slice(None), slice(start, start + size))].astype(F32)

        first = {}
        for slot in range(owners):
            if not noted[slot]:
                out[slot] = jnp.zeros((rows, width), BF16)
                continue
            key = str(noted[slot])
            if key in first:
                out[slot] = out[first[key]]
                continue
            first[key] = slot
            at = 0
            for total, moment in noted[slot]:
                value = MOMENTUM_DECAY * MOMENTUM_DECAY * read(moment)
                if total is not None:
                    value = value + (1.0 + MOMENTUM_DECAY) * read(total)
                out[slot, :, at : at + value.shape[1]] = value.astype(BF16)
                at += value.shape[1]

    vmem = pl.BlockSpec(memory_space=pltpu.VMEM)
    return pl.pallas_call(
        body,
        out_shape=jax.ShapeDtypeStruct((owners, rows, width), BF16),
        in_specs=[vmem] * len(arrays),
        out_specs=vmem,
        cost_estimate=pl.CostEstimate(
            flops=0, bytes_accessed=2 * owners * rows * width, transcendentals=0
        ),
        compiler_params=pltpu.CompilerParams(vmem_limit_bytes=24 * 1024 * 1024),
        name="slots",
    )(*arrays)


def every(*sizes):
    return list(itertools.product(*[range(size) for size in sizes]))


class Plain:
    images = ("dp", "fsdp")
    rows = "fsdp"
    wide_parts = 1

    def __init__(self, mesh):
        self.mesh = mesh
        self.row_shards = mesh.shape["fsdp"]
        self.owners = mesh.shape["fsdp"]
        self.wide_slots = [(i, 0) for i in range(3)]
        self.wide_slots += [None] * (self.owners - 3)
        self.slots = [None] * 3 + list(range(10))
        self.slots += [None] * (self.owners - ITEMS)

    def row_index(self):
        return lax.axis_index("fsdp")

    def group_index(self):
        return lax.axis_index("dp")

    def owner_index(self):
        return lax.axis_index("fsdp")

    def gather_weights(self, chunks):
        full = [lax.all_gather(chunk, "fsdp", axis=0, tiled=True) for chunk in chunks]
        return [jnp.split(chunk, 2, axis=1) for chunk in full]

    def gather_images(self, value):
        return lax.all_gather(value, ("dp", "fsdp"), axis=0, tiled=True)

    def to_group(self, value):
        return lax.all_to_all(value, "fsdp", split_axis=0, concat_axis=0, tiled=True)

    def reduce_core(self, partial):
        return partial

    def reduce_first(self, value, route):
        return value

    def reduce_second(self, value, route):
        return value

    def reduce_last(self, value):
        shard = lax.psum_scatter(value, "fsdp", scatter_dimension=1, tiled=True)
        return lax.psum(shard.astype(F32), "dp")

    def own_rows(self, shard, dim=-2):
        return shard

    def complete(self, piece):
        return piece

    def to_owners(self, pieces):
        got = lax.all_to_all(pieces, "fsdp", split_axis=0, concat_axis=0, tiled=True)
        return got.reshape(-1, got.shape[2])

    def to_rows(self, whole):
        blocks = whole.reshape(self.row_shards, -1, whole.shape[1])
        return lax.all_to_all(blocks, "fsdp", split_axis=0, concat_axis=0, tiled=True)


class Torus:
    images = ("x", "c", "z", "y")
    rows = ("z", "y")
    chips = ("x", "z", "y")
    wide_parts = 2

    def __init__(self, mesh):
        self.mesh = Mesh(mesh.devices.reshape(2, 2, 4, 2), ("x", "c", "z", "y"))
        self.row_shards = 8
        self.owners = 16
        wide_places = [(1, 0), (2, 1), (1, 1)]
        self.wide_slots = [None] * 16
        self.slots = [None] * 16
        for item, (z, y) in enumerate(wide_places):
            for part in range(2):
                self.wide_slots[(part * 4 + z) * 2 + y] = (item, part)
        free = [i for i in range(16) if self.wide_slots[i] is None]
        for item, slot in enumerate(free):
            self.slots[slot] = item

    def row_index(self):
        return lax.axis_index("z") * 2 + lax.axis_index("y")

    def group_index(self):
        return lax.axis_index("x") * 2 + lax.axis_index("c")

    def owner_index(self):
        return (lax.axis_index("x") * 4 + lax.axis_index("z")) * 2 + lax.axis_index("y")

    def swap(self, value, axis):
        return lax.ppermute(value, axis, [(0, 1), (1, 0)])

    def shift(self, value, by):
        return lax.ppermute(value, "z", [(i, (i + by) % 4) for i in range(4)])

    def exchange(self, value, axis):
        here = lax.axis_index(axis)
        return place([value, self.swap(value, axis)], [here, 1 - here])

    def spread_z(self, value):
        z = lax.axis_index("z")
        ring = [value] + [self.shift(value, by) for by in range(1, 4)]
        return place(ring, [(z - by) % 4 for by in range(4)])

    def gather_weights(self, chunks):
        x, y, z, c = [lax.axis_index(axis) for axis in "xyzc"]
        spread = []
        for chunk in chunks:
            piece = self.own_rows(chunk)
            if spread:
                piece = tie(piece, *spread[-1])
            ring = [piece] + [self.shift(piece, by) for by in range(1, 4)]
            spread.append(place_halves(ring, [(z - by) % 4 for by in range(4)]))
        done = []
        for left, right in spread:
            if done:
                left, right = lax.optimization_barrier((left, right, *done[-1]))[:2]
            left_other, right_other = self.swap(left, "y"), self.swap(right, "x")
            left = place([left, left_other], [y, 1 - y])
            right = place([right, right_other], [x, 1 - x])
            left_other, right_other = self.swap(left, "x"), self.swap(right, "y")
            left = place([left, left_other], [x, 1 - x])
            right = place([right, right_other], [y, 1 - y])
            done.append((left, right))
        full = []
        for left, right in done:
            others = self.swap(left, "c"), self.swap(right, "c")
            pair = []
            for half, other, order in ((left, others[0], (2, 1, 0)), (right, others[1], (2, 0, 1))):

                def moves(slot, order=order):
                    found = []
                    for part in range(2):
                        for at in every(2, 2, 4):
                            found.append((part, at, (*[at[i] for i in order], slot[part])))
                    return found

                pair.append(place([half, other], [c, 1 - c], (4, 2, 2, 2), moves).reshape(D, -1))
            full.append(pair)
        return full

    def gather_images(self, value):

        def both(v, axis):
            other = self.swap(v, axis)
            first = lax.axis_index(axis) == 0
            return jnp.where(first, jnp.stack([v, other]), jnp.stack([other, v]))

        z = lax.axis_index("z")
        shape = (32 * value.shape[0],) + value.shape[1:]
        value = both(value, "y")
        ring = jnp.stack([value] + [self.shift(value, by) for by in range(1, 4)])
        value = jnp.take(ring, (z - jnp.arange(4)) % 4, axis=0)
        value = both(value, "c")
        value = both(value, "x")
        return value.reshape(shape)

    def to_group(self, value):
        return lax.all_to_all(value, ("z", "y"), split_axis=0, concat_axis=0, tiled=True)

    def halve(self, value, axis, dim):
        here = lax.axis_index(axis)
        take = lambda at: lax.dynamic_index_in_dim(value, at, dim, keepdims=False)
        got = self.swap(take(1 - here), axis)
        return (take(here).astype(F32) + got.astype(F32)).astype(BF16)

    def reduce_core(self, partial):
        k, _, cols = partial.shape
        return self.halve(partial.reshape(k, 4, 2, 2, 2, D // 32, cols), "c", 4)

    def reduce_first(self, value, route):
        return self.halve(value, route[0], 3 if route[0] == "x" else 2)

    def reduce_second(self, value, route):
        return self.halve(value, route[1], 2)

    def reduce_last(self, value):
        z = lax.axis_index("z")
        take = lambda at: lax.dynamic_index_in_dim(value, at, 1, keepdims=False)
        got = [self.shift(take((z + by) % 4), by) for by in range(1, 4)]
        total = take(z).astype(F32)
        for part in got:
            total = total + part.astype(F32)
        return total

    def own_rows(self, shard, dim=-2):
        return lax.dynamic_slice_in_dim(
            shard, self.group_index() * (D // 32), D // 32, dim % shard.ndim
        )

    def complete(self, piece):
        value = self.exchange(piece, "x")
        c = lax.axis_index("c")
        moves = lambda slot: [(part, (x,), (x, slot[part])) for part in range(2) for x in range(2)]
        value = place([value, self.swap(value, "c")], [c, 1 - c], (2, 2), moves)
        return value.reshape(D // 8, -1)

    def to_owners(self, pieces):
        cols = pieces.shape[2]
        got = lax.all_to_all(pieces, self.chips, split_axis=0, concat_axis=0, tiled=True)
        got = got.reshape(2, 4, 2, D // 32, cols)
        c = lax.axis_index("c")

        def moves(slot):
            return [
                (part, (x, z, y), (z, y, x, slot[part]))
                for part in range(2)
                for x, z, y in every(2, 4, 2)
            ]

        whole = place([got, self.swap(got, "c")], [c, 1 - c], (4, 2, 2, 2), moves)
        return whole.reshape(D, cols)

    def to_rows(self, whole):
        cols = whole.shape[1]
        blocks = whole.reshape(4, 2, 2, 2, D // 32, cols)
        blocks = lax.dynamic_index_in_dim(blocks, lax.axis_index("c"), 3, keepdims=False)
        blocks = blocks.transpose(2, 0, 1, 3, 4).reshape(16, D // 32, cols)
        return lax.all_to_all(blocks, self.chips, split_axis=0, concat_axis=0, tiled=True)


def lanes(shape, dim):
    return lax.broadcasted_iota(jnp.int32, shape, dim)


def norm_of(values):
    centred = values - jnp.mean(values, axis=-1, keepdims=True)
    inverse = lax.rsqrt(jnp.mean(centred * centred, axis=-1, keepdims=True) + NORM_EPS)
    return centred * inverse, inverse


def norm_back(incoming, normed, inverse):
    return inverse * (
        incoming
        - jnp.mean(incoming, axis=-1, keepdims=True)
        - normed * jnp.mean(incoming * normed, axis=-1, keepdims=True)
    )


def rotate_pair(value):
    first = lanes(value.shape, 1) % 32 < 16
    return jnp.where(first, -pltpu.roll(value, 112, 1), pltpu.roll(value, 16, 1))


def two_heads(value):
    low = lanes(value.shape, 1) < HDIM
    zero = jnp.zeros_like(value)
    return jnp.where(low, value, zero), jnp.where(low, zero, value)


def pair_at(pair):
    return slice(pair * 2 * HDIM, (pair + 1) * 2 * HDIM)


def attention_forward_kernel(
    length_ref,
    input_ref,
    cotangent_ref,
    modulation_ref,
    cosine_ref,
    sine_ref,
    query_key_ref,
    value_output_ref,
    first_ref,
    query_ref,
    key_ref,
    value_ref,
    probs_ref,
    attended_ref,
    attention_ref,
    middle_ref,
    second_ref,
    branch_ref,
):
    length = length_ref[pl.program_id(0)]
    row = lambda which: modulation_ref[0, which : which + 1, :]
    stream = input_ref[0].astype(F32)
    positions = stream.shape[0]
    normed, _ = norm_of(stream)
    first = (normed * (1.0 + row(1)) + row(0)).astype(BF16)
    first_ref[0] = first
    inside = lanes((positions, D), 0) < length
    upstream = jnp.where(inside, cotangent_ref[0].astype(F32), 0.0)
    branch_ref[0] = (row(5) * upstream).astype(BF16)
    value_ref[0] = dot(first, value_output_ref[:, :D]).astype(BF16)
    cosine, sine = cosine_ref[0], sine_ref[0]
    keep = lanes((positions, positions), 1) < length
    for pair in range(HEADS // 2):
        at = pair_at(pair)
        query = dot(first, query_key_ref[:, at])
        key = dot(first, query_key_ref[:, D + pair * 128 : D + (pair + 1) * 128])
        query = (query * cosine + rotate_pair(query) * sine).astype(BF16)
        key = (key * cosine + rotate_pair(key) * sine).astype(BF16)
        query_ref[0, :, at] = query
        key_ref[0, :, at] = key
        low = []
        for head, masked in enumerate(two_heads(query)):
            scores = dot(masked, key, NT) * HDIM ** (-0.5)
            scores = jnp.where(keep, scores, -1000000000.0)
            exponent = jnp.exp(scores - jnp.max(scores, axis=-1, keepdims=True))
            probs = exponent * (1.0 / jnp.sum(exponent, axis=-1, keepdims=True))
            probs_ref[0, 2 * pair + head] = probs
            low.append(probs.astype(BF16))
        values = two_heads(value_ref[0, :, at])
        attended_ref[0, :, at] = dot(
            jnp.concatenate(low, axis=1), jnp.concatenate(values, axis=0)
        ).astype(BF16)
    attention = dot(attended_ref[0], value_output_ref[:, D:])
    attention_ref[0] = attention
    middle = stream + row(2) * attention
    middle_ref[0] = middle
    normed, _ = norm_of(middle)
    second_ref[0] = (normed * (1.0 + row(4)) + row(3)).astype(BF16)


def feed_forward_kernel(
    second_ref, branch_ref, gate_ref, up_ref, down_ref, out_ref, back_ref, grads_ref, second_t, branch_t
):
    step = pl.program_id(0)

    @pl.when(step == 0)
    def _():
        second_t[...] = second_ref[...].T
        branch_t[...] = branch_ref[...].T
        out_ref[...] = jnp.zeros_like(out_ref)
        back_ref[...] = jnp.zeros_like(back_ref)

    gate, up, down = gate_ref[...], up_ref[...], down_ref[...]
    gate_pre = dot(second_ref[...], gate)
    up_pre = dot(second_ref[...], up)
    sigmoid = 1.0 / (1.0 + jnp.exp(-gate_pre))
    swish = gate_pre * sigmoid
    hidden = (swish * up_pre).astype(BF16)
    out_ref[...] += dot(hidden, down, NT)
    grad_hidden = dot(branch_ref[...], down)
    grad_gate = (grad_hidden * up_pre * sigmoid * (1.0 + gate_pre * (1.0 - sigmoid))).astype(BF16)
    grad_up = (grad_hidden * swish).astype(BF16)
    back_ref[...] += dot(grad_gate, gate, NT) + dot(grad_up, up, NT)
    grads_ref[0] = dot(second_t[...], grad_gate).astype(BF16)
    grads_ref[1] = dot(second_t[...], grad_up).astype(BF16)
    grads_ref[2] = dot(branch_t[...], hidden).astype(BF16)


def attention_backward_kernel(
    length_ref,
    branch_left_ref,
    branch_right_ref,
    second_left_ref,
    second_right_ref,
    middle_ref,
    cotangent_ref,
    modulation_ref,
    attention_ref,
    value_output_ref,
    query_ref,
    key_ref,
    value_ref,
    probs_ref,
    cosine_ref,
    sine_ref,
    output_ref,
    stream_ref,
    grads_ref,
    sums_ref,
    attended_grad,
):
    length = length_ref[pl.program_id(0)]
    row = lambda which: modulation_ref[0, which : which + 1, :]
    middle = middle_ref[0]
    positions = middle.shape[0]
    inside = lanes((positions, D), 0) < length
    upstream = jnp.where(inside, cotangent_ref[0].astype(F32), 0.0)
    branch = branch_left_ref[0] + branch_right_ref[0]
    output_ref[0] = (middle + row(5) * branch).astype(BF16)
    total = lambda value: jnp.sum(value, axis=0, keepdims=True)
    gate_two = total(upstream * branch)
    second = second_left_ref[0] + second_right_ref[0]
    normed, inverse = norm_of(middle)
    scale_two = total(second * normed)
    shift_two = total(second)
    stream = upstream + norm_back(second * (1.0 + row(4)), normed, inverse)
    stream_ref[0] = stream
    gate_one = total(stream * attention_ref[0])
    blank = jnp.zeros_like(gate_one)
    sums_ref[0] = jnp.concatenate(
        [blank, blank, gate_one, shift_two, scale_two, gate_two, blank, blank], axis=0
    )
    grad_attention = (row(2) * stream).astype(BF16)
    grads_ref[3, 0] = grad_attention
    attended_grad[...] = dot(grad_attention, value_output_ref[:, D:], NT).astype(BF16)
    cosine, sine = cosine_ref[0], sine_ref[0]
    for pair in range(HEADS // 2):
        at = pair_at(pair)
        query, key, value = query_ref[0, :, at], key_ref[0, :, at], value_ref[0, :, at]
        attended = two_heads(attended_grad[:, at])
        low, scores = [], []
        for head in range(2):
            probs = probs_ref[0, 2 * pair + head]
            grad_probs = dot(attended[head], value, NT)
            inner = jnp.sum(grad_probs * probs, axis=-1, keepdims=True)
            scores.append((probs * (grad_probs - inner)).astype(BF16))
            low.append(probs.astype(BF16))
        grads_ref[2, 0, :, at] = dot(
            jnp.concatenate(low, axis=0), jnp.concatenate(attended, axis=0), TN
        ).astype(BF16)
        grad_query = dot(
            jnp.concatenate(scores, axis=1), jnp.concatenate(two_heads(key), axis=0)
        ) * HDIM ** (-0.5)
        grad_key = dot(
            jnp.concatenate(scores, axis=0), jnp.concatenate(two_heads(query), axis=0), TN
        ) * HDIM ** (-0.5)
        grads_ref[0, 0, :, at] = (grad_query * cosine - rotate_pair(grad_query * sine)).astype(BF16)
        grads_ref[1, 0, :, at] = (grad_key * cosine - rotate_pair(grad_key * sine)).astype(BF16)


def projection_backward_kernel(
    grads_in_ref,
    first_ref,
    attended_ref,
    input_ref,
    modulation_ref,
    stream_ref,
    sums_ref,
    active_ref,
    query_key_ref,
    value_output_ref,
    grads_ref,
    input_grad_ref,
    modulation_grad_ref,
    first_t,
    first_grad,
):
    images, positions = input_ref.shape[:2]
    tokens = images * positions
    flat = lambda ref: ref[...].reshape(tokens, D)
    step = pl.program_id(0)

    @pl.when(step == 0)
    def _():
        first_t[...] = flat(first_ref).T
        grads = grads_in_ref[0].reshape(tokens, D)
        grads_ref[0] = dot(first_t[...], grads).astype(BF16)
        first_grad[...] = dot(grads, query_key_ref[:, :D], NT)

    @pl.when(step == 1)
    def _():
        grads = grads_in_ref[0].reshape(tokens, D)
        grads_ref[0] = dot(first_t[...], grads).astype(BF16)
        first_grad[...] += dot(grads, query_key_ref[:, D:], NT)

    @pl.when(step == 2)
    def _():
        grads = grads_in_ref[0].reshape(tokens, D)
        grads_ref[0] = dot(first_t[...], grads).astype(BF16)
        first_grad[...] += dot(grads, value_output_ref[:, :D], NT)

    @pl.when(step == 3)
    def _():
        first_t[...] = flat(attended_ref).T
        grads_ref[0] = dot(first_t[...], grads_in_ref[0].reshape(tokens, D)).astype(BF16)
        for image in range(images):
            at = slice(image * positions, (image + 1) * positions)
            normed, inverse = norm_of(input_ref[image].astype(F32))
            first = first_grad[at, :]
            scale_one = jnp.sum(first * normed, axis=0, keepdims=True)
            shift_one = jnp.sum(first, axis=0, keepdims=True)
            scaled = first * (1.0 + modulation_ref[image, 1:2, :])
            input_grad_ref[image] = stream_ref[image] + norm_back(scaled, normed, inverse)
            modulation_grad_ref[image] = jnp.concatenate(
                [
                    shift_one,
                    scale_one,
                    sums_ref[image, 2:6, :],
                    active_ref[image : image + 1, :].astype(F32),
                    jnp.zeros_like(shift_one),
                ],
                axis=0,
            ).astype(BF16)


BIG_VMEM = 58 * 1024 * 1024


def whole(array):
    return pl.BlockSpec(array.shape, lambda *_: (0,) * array.ndim)


def by_image(array):
    return pl.BlockSpec((1, *array.shape[1:]), lambda b: (b,) + (0,) * (array.ndim - 1))


def call(body, grid, ins, in_specs, outs, out_specs, scratch, flops, name):
    size = sum(a.size * a.dtype.itemsize for a in (*ins, *outs))
    return pl.pallas_call(
        body,
        grid=grid,
        out_shape=outs,
        in_specs=in_specs,
        out_specs=out_specs,
        scratch_shapes=scratch,
        compiler_params=pltpu.CompilerParams(vmem_limit_bytes=BIG_VMEM),
        cost_estimate=pl.CostEstimate(flops=flops, bytes_accessed=size, transcendentals=0),
        name=name,
    )(*ins)


def attention_forward(lengths, inputs, cotangent, modulation, cosine, sine, query_key, value_output):
    images, positions, _ = inputs.shape
    ins = (lengths, inputs, cotangent, modulation, cosine, sine, query_key, value_output)
    in_specs = [pl.BlockSpec(memory_space=pltpu.SMEM)]
    in_specs += [by_image(a) for a in ins[1:6]] + [whole(a) for a in ins[6:]]
    token = lambda dtype: jax.ShapeDtypeStruct((images, positions, D), dtype)
    outs = (
        token(BF16),
        token(BF16),
        token(BF16),
        token(BF16),
        jax.ShapeDtypeStruct((images, HEADS, positions, positions), F32),
        token(BF16),
        token(F32),
        token(F32),
        token(BF16),
        token(BF16),
    )
    flops = 2 * images * positions * D * (4 * D + 2 * positions)
    return call(
        attention_forward_kernel,
        (images,),
        ins,
        in_specs,
        outs,
        [by_image(a) for a in outs],
        [],
        flops,
        "attention_forward",
    )


def feed_forward(second, branch, weight):
    tokens = second.shape[0]
    units = weight.shape[1] // 3
    tile = 256
    steps = units // tile
    ins = (second, branch, weight, weight, weight)
    in_specs = [whole(second), whole(branch)] + [
        pl.BlockSpec((D, tile), lambda t, which=which: (0, which * steps + t)) for which in range(3)
    ]
    outs = (
        jax.ShapeDtypeStruct((tokens, D), F32),
        jax.ShapeDtypeStruct((tokens, D), F32),
        jax.ShapeDtypeStruct((3, D, units), BF16),
    )
    out_specs = [
        whole(outs[0]),
        whole(outs[1]),
        pl.BlockSpec((3, D, tile), lambda t: (0, 0, t)),
    ]
    scratch = [pltpu.VMEM((D, tokens), BF16), pltpu.VMEM((D, tokens), BF16)]
    flops = 2 * 9 * tokens * D * units
    return call(
        feed_forward_kernel, (steps,), ins, in_specs, outs, out_specs, scratch, flops, "feed_forward"
    )


def attention_backward(lengths, *ins):
    images, positions, _ = ins[0].shape
    shared = 8
    in_specs = [pl.BlockSpec(memory_space=pltpu.SMEM)]
    in_specs += [whole(a) if i == shared else by_image(a) for i, a in enumerate(ins)]
    outs = (
        jax.ShapeDtypeStruct((images, positions, D), BF16),
        jax.ShapeDtypeStruct((images, positions, D), F32),
        jax.ShapeDtypeStruct((4, images, positions, D), BF16),
        jax.ShapeDtypeStruct((images, 8, D), F32),
    )
    out_specs = [
        by_image(outs[0]),
        by_image(outs[1]),
        pl.BlockSpec((4, 1, positions, D), lambda b: (0, b, 0, 0)),
        by_image(outs[3]),
    ]
    flops = 2 * images * positions * D * (D + 5 * positions)
    return call(
        attention_backward_kernel,
        (images,),
        (lengths, *ins),
        in_specs,
        outs,
        out_specs,
        [pltpu.VMEM((positions, D), BF16)],
        flops,
        "attention_backward",
    )


def projection_backward(*ins):
    _, images, positions, _ = ins[0].shape
    tokens = images * positions
    in_specs = [pl.BlockSpec((1, images, positions, D), lambda k: (k, 0, 0, 0))]
    in_specs += [whole(a) for a in ins[1:]]
    outs = (
        jax.ShapeDtypeStruct((4, D, D), BF16),
        jax.ShapeDtypeStruct((images, positions, D), F32),
        jax.ShapeDtypeStruct((images, 8, D), BF16),
    )
    out_specs = [pl.BlockSpec((1, D, D), lambda k: (k, 0, 0)), whole(outs[1]), whole(outs[2])]
    scratch = [pltpu.VMEM((D, tokens), BF16), pltpu.VMEM((tokens, D), F32)]
    return call(
        projection_backward_kernel,
        (4,),
        ins,
        in_specs,
        outs,
        out_specs,
        scratch,
        2 * 7 * tokens * D * D,
        "projection_backward",
    )


def swish_value(values):
    return values / (1.0 + jnp.exp(-values))


def rope_tables(extents, positions):
    quarter = HDIM // 4
    places = jnp.arange(positions, dtype=jnp.int32)
    widths = extents[:, 1]
    row_place = (places[None, :] // widths[:, None]).astype(F32)
    col_place = (places[None, :] % widths[:, None]).astype(F32)
    lane = jnp.arange(2 * HDIM) % HDIM
    frequency = 10000.0 ** (-(lane % quarter).astype(F32) / quarter)
    by_row = lane < 2 * quarter
    angle = jnp.where(by_row, row_place[:, :, None], col_place[:, :, None]) * frequency
    return jnp.cos(angle), jnp.sin(angle)


def local(
    comm,
    inputs,
    cotangent,
    image_shape,
    time_bins,
    time_table,
    modulation_master,
    projection_master,
    output_master,
    expand_master,
    shrink_master,
    modulation_moment,
    projection_moment,
    output_moment,
    expand_moment,
    shrink_moment,
):
    masters = (modulation_master, projection_master, output_master, expand_master, shrink_master)
    moments = (modulation_moment, projection_moment, output_moment, expand_moment, shrink_moment)
    images, positions, features = inputs.shape
    tokens = images * positions
    rows = modulation_master.shape[1]
    row_index = comm.row_index()

    half = FF // 2
    shrink_low = shrink_master.astype(BF16).T
    (query_key_weight, value_output_weight), (left_weight, right_weight) = comm.gather_weights(
        [
            jnp.concatenate(
                [projection_master[i].astype(BF16) for i in range(3)] + [output_master.astype(BF16)],
                axis=1,
            ),
            jnp.concatenate(
                [
                    part
                    for cols in (slice(None, half), slice(half, None))
                    for part in (
                        expand_master[0, :, cols].astype(BF16),
                        expand_master[1, :, cols].astype(BF16),
                        shrink_low[:, cols],
                    )
                ],
                axis=1,
            ),
        ]
    )
    selector = (
        time_bins[:, None] == jnp.arange(time_table.shape[0], dtype=jnp.int32)[None, :]
    ).astype(F32)
    active = swish_value(jnp.dot(selector, time_table, precision=HIGHEST)).astype(BF16)
    active_group = comm.to_group(
        active.reshape(images, comm.row_shards, rows).transpose(1, 0, 2)
    ).reshape(-1, rows)
    partial = jnp.einsum(
        "bd,kde->bke", active_group, modulation_master.astype(BF16), preferred_element_type=F32
    )
    modulation = jnp.sum(
        comm.to_group(partial.reshape(comm.row_shards, images, 6, features)), axis=0
    )
    cosine, sine = rope_tables(image_shape, positions)
    lengths = image_shape[:, 0] * image_shape[:, 1]
    (first_input, query, key, value, probs, attended, attention, middle, second_input, grad_branch) = (
        attention_forward(
            lengths, inputs, cotangent, modulation, cosine, sine, query_key_weight, value_output_weight
        )
    )
    second_flat = second_input.reshape(tokens, D)
    branch_flat = grad_branch.reshape(tokens, D)
    shaped = lambda v: v.reshape(images, positions, D)
    branch_left, back_left, grads = feed_forward(second_flat, branch_flat, left_weight)
    left_sum = comm.reduce_core(grads)
    second_flat = tie(second_flat, back_left)
    branch_right, back_right, grads = feed_forward(second_flat, branch_flat, right_weight)
    left_sum, grads = lax.optimization_barrier((left_sum, grads))
    left_sum = comm.reduce_first(left_sum, "xy")
    right_sum = comm.reduce_core(grads)
    block_output, grad_stream, grads, sums = attention_backward(
        lengths,
        shaped(branch_left),
        shaped(branch_right),
        shaped(back_left),
        shaped(back_right),
        middle,
        cotangent,
        modulation,
        attention,
        value_output_weight,
        query,
        key,
        value,
        probs,
        cosine,
        sine,
    )
    left_sum, right_sum, grads = lax.optimization_barrier((left_sum, right_sum, grads))
    left_sum = comm.reduce_second(left_sum, "xy")
    right_sum = comm.reduce_first(right_sum, "yx")
    grads, input_gradient, grad_modulation = projection_backward(
        grads,
        first_input,
        attended,
        inputs,
        modulation,
        grad_stream,
        sums,
        active,
        query_key_weight,
        value_output_weight,
    )
    left_sum, right_sum, grads, grad_modulation = lax.optimization_barrier(
        (left_sum, right_sum, grads, grad_modulation)
    )
    right_sum = comm.reduce_second(right_sum, "yx")
    left_piece = comm.reduce_last(left_sum)
    attention_sum = comm.reduce_core(grads)
    left_piece, right_sum, attention_sum = lax.optimization_barrier(
        (left_piece, right_sum, attention_sum)
    )
    right_piece = comm.reduce_last(right_sum)
    first_sum = comm.reduce_first(attention_sum[:2], "xy")
    second_sum = comm.reduce_first(attention_sum[2:], "yx")
    first_sum, second_sum, right_piece = lax.optimization_barrier(
        (first_sum, second_sum, right_piece)
    )

    owner = comm.owner_index()
    own_expand = comm.own_rows(expand_moment)
    own_shrink = comm.own_rows(shrink_moment.T)
    wide_feed = [
        [
            (
                (piece, ((which,), 0, half)),
                (own_shrink, ((), side * half, half))
                if which == 2
                else (own_expand, ((which,), side * half, half)),
            )
            for side, piece in enumerate((left_piece, right_piece))
        ]
        for which in range(3)
    ]
    wide = comm.to_owners(
        slots_of(
            [[] if slot is None else wide_feed[slot[0]] for slot in comm.wide_slots],
            comm.owners,
            FF,
        )
    )
    gathered = comm.gather_images(grad_modulation)
    attention_piece = comm.reduce_last(
        jnp.concatenate(
            [comm.reduce_second(first_sum, "xy"), comm.reduce_second(second_sum, "yx")], axis=0
        )
    )
    active_all = gathered[:, 6]

    own_modulation = comm.own_rows(modulation_moment)
    own_projection = comm.own_rows(projection_moment)
    own_output = comm.own_rows(output_moment)
    square_feed = [[(None, (own_modulation, ((k,), 0, D)))] for k in range(6)]
    for k in range(3):
        square_feed.append(
            [((attention_piece, ((k,), 0, D)), (own_projection, ((k,), 0, D)))]
        )
    square_feed.append([((attention_piece, ((3,), 0, D)), (own_output, ((), 0, D)))])
    square = comm.to_owners(
        slots_of(
            [[] if slot is None else square_feed[slot] for slot in comm.slots], comm.owners, D
        )
    )
    item = jnp.array([-1 if slot is None else slot for slot in comm.slots], jnp.int32)[owner]
    which = jnp.where((item >= 0) & (item < 6), item, 0)
    right = lax.dynamic_index_in_dim(gathered, which, 1, keepdims=False)
    right = jnp.where(item < 6, right, jnp.zeros_like(right))
    active_wide = jnp.array([0 if slot is None else 1 for slot in comm.wide_slots], jnp.int32)[owner]
    wide, square = lax.optimization_barrier((wide, square))
    wide_done = newton_schulz(active_wide, wide)
    square_done = newton_schulz((item >= 0).astype(jnp.int32), square, active_all, right)
    size = FF // comm.wide_parts
    part = jnp.array([0 if slot is None else slot[1] for slot in comm.wide_slots])[owner]
    mine = lax.dynamic_slice_in_dim(wide_done, part * size, size, 1)
    mine = mine + jnp.pad(square_done, ((0, 0), (0, size - D)))
    back = comm.to_rows(mine)

    pieces = [left_piece[i] for i in range(3)] + [right_piece[i] for i in range(3)]
    pieces += [attention_piece[i] for i in range(4)]
    totals_low = comm.complete(jnp.concatenate([p.astype(BF16) for p in pieces], axis=1)).astype(F32)
    by_unit = [
        jnp.concatenate(
            [totals_low[:, (side * 3 + i) * half : (side * 3 + i + 1) * half] for side in range(2)],
            axis=1,
        )
        for i in range(3)
    ]
    wide_back = [
        back[comm.wide_slots.index((i, p))] for i in range(3) for p in range(comm.wide_parts)
    ]
    square_back = [back[comm.slots.index(i), :, :D] for i in range(10)]
    steps = comm.complete(jnp.concatenate(wide_back + square_back, axis=1)).astype(F32)
    active_rows = lax.dynamic_slice_in_dim(active_all, row_index * rows, rows, 1)
    modulation_total = jnp.einsum(
        "bd,bke->kde",
        active_rows,
        gathered[:, :6],
        preferred_element_type=F32,
    )
    after = 3 * FF
    totals = (
        modulation_total,
        jnp.stack([totals_low[:, after + i * D : after + (i + 1) * D] for i in range(3)]),
        totals_low[:, after + 3 * D :],
        jnp.stack(by_unit[:2]),
        by_unit[2].T,
    )
    states = tuple((MOMENTUM_DECAY * moment + total for moment, total in zip(moments, totals)))
    square_step = [steps[:, after + i * D : after + (i + 1) * D] for i in range(10)]
    steps_all = (
        jnp.stack(square_step[:6]),
        jnp.stack(square_step[6:9]),
        square_step[9],
        jnp.stack([steps[:, :FF], steps[:, FF : 2 * FF]]) * (FF / D) ** 0.5,
        steps[:, 2 * FF : after].T,
    )
    updated = tuple((master - LEARN_RATE * step for master, step in zip(masters, steps_all)))
    return (block_output, input_gradient, *totals, *updated, *states)


def solution(mesh):
    if mesh.shape["dp"] == 4 and mesh.shape["fsdp"] == 8:
        comm = Torus(mesh)
    else:
        comm = Plain(mesh)
    images, rows = comm.images, comm.rows
    by_row = (
        P(None, rows, None),
        P(None, rows, None),
        P(rows, None),
        P(None, rows, None),
        P(None, rows),
    )
    return jax.shard_map(
        functools.partial(local, comm),
        mesh=comm.mesh,
        in_specs=(
            P(images, None, None),
            P(images, None, None),
            P(images, None),
            P(images),
            P(),
            *by_row,
            *by_row,
        ),
        out_specs=(P(images, None, None), P(images, None, None), *by_row, *by_row, *by_row),
        check_vma=False,
    )
```

```python
import functools
import itertools

import jax
import jax.numpy as jnp
from jax import lax
from jax.experimental import pallas as pl
from jax.experimental.pallas import tpu as pltpu
from jax.sharding import Mesh, PartitionSpec as P

D = 768
HEADS = 12
HDIM = 64
FF = 2048
NS_ITERS = 5
NORM_EPS = 1e-06
FROBENIUS_EPS = 1e-07
COEFF_FIRST = 3.4445
COEFF_SECOND = -4.775
COEFF_THIRD = 2.0315
MOMENTUM_DECAY = 0.9
LEARN_RATE = 1.0
HIGHEST = lax.Precision.HIGHEST
BF16 = jnp.bfloat16
F32 = jnp.float32
ITEMS = 13
NT = (((1,), (1,)), ((), ()))
NN = (((1,), (0,)), ((), ()))
TN = (((0,), (0,)), ((), ()))


def dot(a, b, dims=NN):
    return lax.dot_general(a, b, dims, preferred_element_type=F32)


def newton_schulz_kernel(width, active_ref, feed_ref, left_ref, right_ref, out_ref, x, xb, gram, low, poly):
    tile = 256
    tiles = D // tile
    blocks = width // tile
    spans = [slice(i * tile, (i + 1) * tile) for i in range(tiles)]

    def diagonal(part, other):
        rows = lax.broadcasted_iota(jnp.int32, (tile, tile), 0)
        cols = lax.broadcasted_iota(jnp.int32, (tile, tile), 1)
        return jnp.where(rows == cols, part, other)

    def block(b):
        return pl.ds(pl.multiple_of(b * tile, tile), tile)

    @pl.when(active_ref[0] != 0)
    def _():
        def load(b, acc):
            if len(feed_ref.shape) == 3:
                per = feed_ref.shape[2] // tile
                v = feed_ref[b // per, :, block(lax.rem(b, per))].astype(F32)
            else:
                v = feed_ref[:, block(b)].astype(F32)
            if right_ref is not None:
                v = v + (1.0 + MOMENTUM_DECAY) * dot(left_ref[...], right_ref[:, block(b)], TN)
            x[:, block(b)] = v
            return acc + jnp.sum(v * v, axis=0, keepdims=True)

        total = lax.fori_loop(0, blocks, load, jnp.zeros((1, tile), F32))
        total = jnp.sum(total, keepdims=True)
        inverse = 1.0 / (jnp.sqrt(total) + FROBENIUS_EPS)

        def scale_block(b, carry):
            v = x[:, block(b)] * inverse
            x[:, block(b)] = v
            xb[:, block(b)] = v.astype(BF16)
            return carry

        lax.fori_loop(0, blocks, scale_block, 0)

        def iterate(step, carry):
            trace = jnp.zeros((1, tile), F32)
            for i in range(tiles):
                for j in range(i + 1):
                    part = dot(xb[spans[i], :], xb[spans[j], :], NT)
                    gram[spans[i], spans[j]] = part
                    if i == j:
                        trace = trace + jnp.sum(diagonal(part, 0.0), axis=0, keepdims=True)
                    else:
                        lower = part.astype(BF16)
                        low[spans[i], spans[j]] = lower
                        low[spans[j], spans[i]] = lower.T
            shift = jnp.sum(trace, keepdims=True) / D
            for i in range(tiles):
                part = gram[spans[i], spans[i]]
                part = diagonal(part - shift, part)
                gram[spans[i], spans[i]] = part
                low[spans[i], spans[i]] = part.astype(BF16)
            linear = COEFF_SECOND + 2.0 * COEFF_THIRD * shift
            level = COEFF_SECOND * shift + COEFF_THIRD * shift * shift
            trace = jnp.zeros((1, tile), F32)
            for i in range(tiles):
                for j in range(i + 1):
                    part = linear * gram[spans[i], spans[j]] + COEFF_THIRD * dot(
                        low[spans[i], :], low[spans[j], :], NT
                    )
                    if i == j:
                        gram[spans[i], spans[j]] = part
                        trace = trace + jnp.sum(diagonal(part, 0.0), axis=0, keepdims=True)
                    else:
                        lower = part.astype(BF16)
                        poly[spans[i], spans[j]] = lower
                        poly[spans[j], spans[i]] = lower.T
            mean = jnp.sum(trace, keepdims=True) / D
            for i in range(tiles):
                part = gram[spans[i], spans[i]]
                poly[spans[i], spans[i]] = diagonal(part - mean, part).astype(BF16)
            scale = COEFF_FIRST + level + mean

            size = width // 2 if width > 1024 else width
            for b in range(width // size):
                cols = slice(b * size, (b + 1) * size)
                new = scale * x[:, cols] + dot(poly[...], xb[:, cols])
                x[:, cols] = new
                xb[:, cols] = new.astype(BF16)
            return carry

        lax.fori_loop(0, NS_ITERS, iterate, 0)
        out_ref[...] = xb[...]

    @pl.when(active_ref[0] == 0)
    def _():
        out_ref[...] = jnp.zeros_like(out_ref)


def newton_schulz(active, feed, left=None, right=None):
    width = feed.size // D
    operands = [active.reshape(1).astype(jnp.int32), feed]
    if left is None:

        def body(active_ref, feed_ref, *rest):
            newton_schulz_kernel(width, active_ref, feed_ref, None, None, *rest)

    else:
        body = functools.partial(newton_schulz_kernel, width)
        operands += [left, right]
    vmem = pl.BlockSpec(memory_space=pltpu.VMEM)
    return pl.pallas_call(
        body,
        out_shape=jax.ShapeDtypeStruct((D, width), BF16),
        in_specs=[pl.BlockSpec(memory_space=pltpu.SMEM)] + [vmem] * (len(operands) - 1),
        out_specs=vmem,
        scratch_shapes=[
            pltpu.VMEM((D, width), F32),
            pltpu.VMEM((D, width), BF16),
            pltpu.VMEM((D, D), F32),
            pltpu.VMEM((D, D), BF16),
            pltpu.VMEM((D, D), BF16),
        ],
        compiler_params=pltpu.CompilerParams(vmem_limit_bytes=40 * 1024 * 1024),
        cost_estimate=pl.CostEstimate(
            flops=NS_ITERS * 4 * D * D * (width + D), bytes_accessed=4 * D * width, transcendentals=0
        ),
        name="newton_schulz",
    )(*operands)


def tie(value, *others):
    return lax.optimization_barrier((value, *others))[0]


def meet(*values):
    flat, tree = jax.tree.flatten(values)
    return jax.tree.unflatten(tree, lax.optimization_barrier(tuple(flat)))


def fold(mine, other, here, view, start, count):
    before, after = view
    rows, cols = mine.shape[-2:]
    shape = (mine.shape[0], before, 2, after, rows, cols)
    block = pl.BlockSpec((1, *shape[1:]), lambda k: (start + k, 0, 0, 0, 0, 0))
    out = jax.ShapeDtypeStruct((count, before, after, rows, cols), BF16)
    out_block = pl.BlockSpec((1, *out.shape[1:]), lambda k: (k, 0, 0, 0, 0))

    def body(here_ref, mine_ref, other_ref, keep_ref, send_ref):
        here = here_ref[0]
        for ref, at in ((send_ref, 1 - here), (keep_ref, here)):
            ref[0] = (mine_ref[0, :, at].astype(F32) + other_ref[0, :, at].astype(F32)).astype(BF16)

    size = 6 * count * before * after * rows * cols * 2
    keep, send = pl.pallas_call(
        body,
        grid=(count,),
        out_shape=(out, out),
        in_specs=[pl.BlockSpec(memory_space=pltpu.SMEM), block, block],
        out_specs=(out_block, out_block),
        compiler_params=pltpu.CompilerParams(vmem_limit_bytes=24 * 1024 * 1024),
        cost_estimate=pl.CostEstimate(flops=0, bytes_accessed=size, transcendentals=0),
        name="fold",
    )(here.reshape(1).astype(jnp.int32), mine.reshape(shape), other.reshape(shape))
    flat = lambda v: v.reshape(count, before * after, rows, cols)
    return flat(keep), flat(send)


def fold_last(mine, other, here):
    k, _, rows, cols = mine.shape

    def body(here_ref, mine_ref, other_ref, keep_ref, *send_refs):
        for by, ref in enumerate((keep_ref, *send_refs)):
            at = lax.rem(here_ref[0] + by, 4)
            total = mine_ref[:, at].astype(F32) + other_ref[:, at].astype(F32)
            ref[...] = total.astype(ref.dtype)

    vmem = pl.BlockSpec(memory_space=pltpu.VMEM)
    return pl.pallas_call(
        body,
        out_shape=(jax.ShapeDtypeStruct((k, rows, cols), F32),)
        + (jax.ShapeDtypeStruct((k, rows, cols), BF16),) * 3,
        in_specs=[pl.BlockSpec(memory_space=pltpu.SMEM), vmem, vmem],
        out_specs=(vmem,) * 4,
        compiler_params=pltpu.CompilerParams(vmem_limit_bytes=24 * 1024 * 1024),
        cost_estimate=pl.CostEstimate(
            flops=0, bytes_accessed=28 * k * rows * cols, transcendentals=0
        ),
        name="fold_last",
    )(here.reshape(1).astype(jnp.int32), mine, other)


def place(parts, slots, lead=None, moves=None):
    count = len(parts)
    if lead is None:
        lead = (count, *parts[0].shape[:-2])
        moves = lambda slot: [(i, (), (slot[i],)) for i in range(count)]

    def body(slot_ref, *refs):
        ins, out = refs[:count], refs[count]
        for part, source, target in moves(slot_ref):
            out[target] = ins[part][source] if source else ins[part][...]

    size = count * parts[0].size * parts[0].dtype.itemsize
    vmem = pl.BlockSpec(memory_space=pltpu.VMEM)
    return pl.pallas_call(
        body,
        out_shape=jax.ShapeDtypeStruct((*lead, *parts[0].shape[-2:]), parts[0].dtype),
        in_specs=[pl.BlockSpec(memory_space=pltpu.SMEM)] + [vmem] * count,
        out_specs=vmem,
        cost_estimate=pl.CostEstimate(flops=0, bytes_accessed=2 * size, transcendentals=0),
        compiler_params=pltpu.CompilerParams(vmem_limit_bytes=24 * 1024 * 1024),
        name="place",
    )(jnp.stack(slots).astype(jnp.int32), *parts)


def place_halves(parts, slots):
    count = len(parts)
    rows, cols = parts[0].shape
    half = cols // 2

    def body(slot_ref, *refs):
        left, right = refs[count:]
        for i, ref in enumerate(refs[:count]):
            left[slot_ref[i]] = ref[:, :half]
            right[slot_ref[i]] = ref[:, half:]

    vmem = pl.BlockSpec(memory_space=pltpu.VMEM)
    shape = jax.ShapeDtypeStruct((count, rows, half), parts[0].dtype)
    return pl.pallas_call(
        body,
        out_shape=(shape, shape),
        in_specs=[pl.BlockSpec(memory_space=pltpu.SMEM)] + [vmem] * count,
        out_specs=(vmem, vmem),
        cost_estimate=pl.CostEstimate(flops=0, bytes_accessed=16 * rows * cols, transcendentals=0),
        compiler_params=pltpu.CompilerParams(vmem_limit_bytes=24 * 1024 * 1024),
        name="place_halves",
    )(jnp.stack(slots).astype(jnp.int32), *parts)


def slots_of(feeds, owners, width, extra=None):
    arrays, index = [], {}

    def note(array):
        if array is None:
            return None
        source, columns = array
        if id(source) not in index:
            index[id(source)] = len(arrays)
            arrays.append(source)
        return (index[id(source)], columns)

    noted = [[(note(total), note(moment)) for total, moment in feed] for feed in feeds]
    rows = arrays[0].shape[-2]
    more = 0 if extra is None else extra.shape[0]

    def body(*refs):
        out = refs[-1].at[:, :rows] if more else refs[-1]
        if more:
            for slot in range(owners):
                refs[-1][slot, rows:] = refs[-2][...]

        def read(what):
            place_of, (lead, start, size) = what
            ref = refs[place_of]
            return ref[(*lead, slice(None), slice(start, start + size))].astype(F32)

        first = {}
        for slot in range(owners):
            if not noted[slot]:
                out[slot] = jnp.zeros((rows, width), BF16)
                continue
            key = str(noted[slot])
            if key in first:
                out[slot] = out[first[key]]
                continue
            first[key] = slot
            at = 0
            for total, moment in noted[slot]:
                value = MOMENTUM_DECAY * MOMENTUM_DECAY * read(moment)
                if total is not None:
                    value = value + (1.0 + MOMENTUM_DECAY) * read(total)
                out[slot, :, at : at + value.shape[1]] = value.astype(BF16)
                at += value.shape[1]

    vmem = pl.BlockSpec(memory_space=pltpu.VMEM)
    return pl.pallas_call(
        body,
        out_shape=jax.ShapeDtypeStruct((owners, rows + more, width), BF16),
        in_specs=[vmem] * (len(arrays) + (more > 0)),
        out_specs=vmem,
        cost_estimate=pl.CostEstimate(
            flops=0, bytes_accessed=2 * owners * rows * width, transcendentals=0
        ),
        compiler_params=pltpu.CompilerParams(vmem_limit_bytes=24 * 1024 * 1024),
        name="slots",
    )(*arrays, *([extra] if more else []))


def pack(parts):
    arrays, index = [], {}
    for array, _, _ in parts:
        if id(array) not in index:
            index[id(array)] = len(arrays)
            arrays.append(array)
    rows = arrays[0].shape[-2]
    total = sum(cols for _, _, cols in parts)

    def body(*refs):
        at = 0
        for array, lead, cols in parts:
            value = refs[index[id(array)]][(*lead, slice(None), slice(0, cols))]
            refs[-1][:, at : at + cols] = value.astype(BF16)
            at += cols

    vmem = pl.BlockSpec(memory_space=pltpu.VMEM)
    return pl.pallas_call(
        body,
        out_shape=jax.ShapeDtypeStruct((rows, total), BF16),
        in_specs=[vmem] * len(arrays),
        out_specs=vmem,
        cost_estimate=pl.CostEstimate(flops=0, bytes_accessed=6 * rows * total, transcendentals=0),
        compiler_params=pltpu.CompilerParams(vmem_limit_bytes=24 * 1024 * 1024),
        name="pack",
    )(*arrays)


def pick(values, index):
    found = jnp.int32(values[0])
    for i, value in enumerate(values):
        if value != values[0]:
            found = jnp.where(index == i, jnp.int32(value), found)
    return found


def update_kernel(quarters, slot_ref, *refs):
    step_refs, refs = refs[:quarters], refs[quarters:]
    modulation, projection, output, expand, shrink = refs[:5]
    out_modulation, out_projection, out_output, out_expand, out_shrink = refs[5:10]
    quarter = pl.program_id(0)
    rows = step_refs[0].shape[0]
    ratio = LEARN_RATE * (FF / D) ** 0.5
    for which, steps in enumerate(step_refs):

        @pl.when(slot_ref[quarter] == which)
        def _(steps=steps):
            at = 3 * FF
            for k in range(2):
                step = steps[:, k * FF : (k + 1) * FF].astype(F32)
                out_expand[k] = expand[k] - ratio * step
            out_shrink[...] = shrink[...] - LEARN_RATE * steps[:, 2 * FF : at].astype(F32)
            for master, out, count in (
                (modulation, out_modulation, 6),
                (projection, out_projection, 3),
            ):
                for k in range(count):
                    out[k] = master[k] - LEARN_RATE * steps[:, at : at + D].astype(F32)
                    at += D
            out_output[...] = output[...] - LEARN_RATE * steps[:, at : at + D].astype(F32)


def update(slots, steps, masters):
    quarters = len(steps)
    rows = steps[0].shape[0]
    third = lambda a: pl.BlockSpec((a.shape[0], rows, a.shape[2]), lambda q: (0, q, 0))
    masters = (*masters[:4], masters[4].T)
    modulation, projection, output, expand, shrink = masters
    specs = [
        third(modulation),
        third(projection),
        pl.BlockSpec((rows, D), lambda q: (q, 0)),
        third(expand),
        pl.BlockSpec((rows, FF), lambda q: (q, 0)),
    ]
    updated = pl.pallas_call(
        functools.partial(update_kernel, quarters),
        grid=(quarters,),
        out_shape=tuple(jax.ShapeDtypeStruct(a.shape, F32) for a in masters),
        in_specs=[pl.BlockSpec(memory_space=pltpu.SMEM)] + [whole(a) for a in steps] + specs,
        out_specs=tuple(specs),
        cost_estimate=pl.CostEstimate(flops=0, bytes_accessed=14_000_000, transcendentals=0),
        compiler_params=pltpu.CompilerParams(vmem_limit_bytes=24 * 1024 * 1024),
        name="update",
    )(
        jnp.stack(slots).astype(jnp.int32),
        *steps,
        *[pltpu.with_memory_space_constraint(a, pltpu.HBM) for a in masters],
    )
    return (*updated[:4], updated[4].T)


def every(*sizes):
    return list(itertools.product(*[range(size) for size in sizes]))


class Plain:
    images = ("dp", "fsdp")
    rows = "fsdp"
    wide_parts = 1

    def __init__(self, mesh):
        self.mesh = mesh
        self.row_shards = mesh.shape["fsdp"]
        self.owners = mesh.shape["fsdp"]
        self.wide_slots = [(i, 0) for i in range(3)]
        self.wide_slots += [None] * (self.owners - 3)
        self.slots = [None] * 3 + list(range(10))
        self.slots += [None] * (self.owners - ITEMS)

    def row_index(self):
        return lax.axis_index("fsdp")

    def group_index(self):
        return lax.axis_index("dp")

    def owner_index(self):
        return lax.axis_index("fsdp")

    def gather_weights(self, first, second, modulate, attend):
        full = [lax.all_gather(chunk, "fsdp", axis=0, tiled=True) for chunk in (first, second)]
        first, second = [jnp.split(chunk, 2, axis=1) for chunk in full]
        modulation = modulate[1](modulate[0]())
        return first, second, modulation, attend(first, modulation)

    def to_group(self, value):
        return lax.all_to_all(value, "fsdp", split_axis=0, concat_axis=0, tiled=True)

    def halves(self):
        return jnp.int32(0)

    def begin(self, mine, send):
        k, n, rows, cols = mine.shape
        return (jnp.stack([mine, send], axis=2).reshape(k, 2 * n * rows, cols),)

    def step(self, state, axis, start=0, count=None):
        return (state[0][start : start + (count or state[0].shape[0])],)

    def last(self, *states):
        value = jnp.concatenate([state[0] for state in states], axis=0)
        shard = lax.psum_scatter(value, "fsdp", scatter_dimension=1, tiled=True)
        return lax.psum(shard.astype(F32), "dp")

    def own_rows(self, shard, dim=-2):
        return shard

    def complete(self, piece):
        return piece

    def quarters(self, piece):
        return [jnp.int32(0)], [piece]

    def images_begin(self, rows):
        return lax.all_gather(rows, ("dp", "fsdp"), axis=0, tiled=True)

    def images_end(self, got):
        return got

    def to_owners(self, pieces):
        got = lax.all_to_all(pieces, "fsdp", split_axis=0, concat_axis=0, tiled=True)
        return got.reshape(-1, got.shape[2])

    def wide_slots_of(self, feeds):
        return slots_of(
            [[] if slot is None else feeds[slot[0]] for slot in self.wide_slots], self.owners, FF
        )

    def wide_halves(self, got):
        return got

    def wide_whole(self, got):
        return jnp.stack(jnp.split(got, 2, axis=1))

    def square_slots(self, feeds):
        return slots_of([[] if slot is None else feeds[slot] for slot in self.slots], self.owners, D)

    def square_to_owners(self, slots, beside):
        return self.to_owners(slots), beside

    def to_rows(self, whole):
        blocks = whole.reshape(self.row_shards, -1, whole.shape[1])
        return lax.all_to_all(blocks, "fsdp", split_axis=0, concat_axis=0, tiled=True)


class Torus:
    images = ("x", "c", "z", "y")
    rows = ("z", "y")
    chips = ("x", "z", "y")
    wide_parts = 2

    def __init__(self, mesh):
        self.mesh = Mesh(mesh.devices.reshape(2, 2, 4, 2), ("x", "c", "z", "y"))
        self.row_shards = 8
        self.owners = 16
        wide_places = [(1, 0), (2, 1), (1, 1)]
        self.wide_slots = [None] * 16
        self.slots = [None] * 16
        for item, (z, y) in enumerate(wide_places):
            for part in range(2):
                self.wide_slots[(part * 4 + z) * 2 + y] = (item, part)
        free = [i for i in range(16) if self.wide_slots[i] is None]
        for item, slot in enumerate(free):
            self.slots[slot] = item

    def row_index(self):
        return lax.axis_index("z") * 2 + lax.axis_index("y")

    def group_index(self):
        return lax.axis_index("x") * 2 + lax.axis_index("c")

    def owner_index(self):
        return (lax.axis_index("x") * 4 + lax.axis_index("z")) * 2 + lax.axis_index("y")

    def swap(self, value, axis):
        return lax.ppermute(value, axis, [(0, 1), (1, 0)])

    def shift(self, value, by):
        return lax.ppermute(value, "z", [(i, (i + by) % 4) for i in range(4)])

    def exchange(self, value, axis):
        here = lax.axis_index(axis)
        return place([value, self.swap(value, axis)], [here, 1 - here])

    def spread_z(self, value):
        z = lax.axis_index("z")
        ring = [value] + [self.shift(value, by) for by in range(1, 4)]
        return place(ring, [(z - by) % 4 for by in range(4)])

    def gather_weights(self, first, second, modulate, attend):
        x, y, z, c = [lax.axis_index(axis) for axis in "xyzc"]
        slots = [(z - by) % 4 for by in range(4)]

        def ring_of(chunk, *others):
            piece = self.own_rows(chunk)
            if others:
                piece = tie(piece, *others)
            return [piece] + [self.shift(piece, by) for by in range(1, 4)]

        def one_hop(left, right):
            left_other, right_other = self.swap(left, "y"), self.swap(right, "x")
            left = place([left, left_other], [y, 1 - y])
            right = place([right, right_other], [x, 1 - x])
            return left, right

        def other_hop(left, right):
            left, right = meet(left, right)
            left_other, right_other = meet(self.swap(left, "x"), self.swap(right, "y"))
            left = place([left, left_other], [x, 1 - x])
            right = place([right, right_other], [y, 1 - y])
            return left, right

        def by_core(left, right):
            others = self.swap(left, "c"), self.swap(right, "c")
            pair = []
            for half, other, order in ((left, others[0], (2, 1, 0)), (right, others[1], (2, 0, 1))):

                def moves(slot, order=order):
                    found = []
                    for part in range(2):
                        for at in every(2, 2, 4):
                            found.append((part, at, (*[at[i] for i in order], slot[part])))
                    return found

                pair.append(place([half, other], [c, 1 - c], (4, 2, 2, 2), moves).reshape(D, -1))
            return pair

        group = modulate[0]()
        left, right = place_halves(ring_of(first), slots)
        ring = ring_of(second, left, right)
        left, right, group = meet(left, right, group)
        left, right = one_hop(left, right)
        modulation = modulate[1](group)
        left, right, modulation, ring[0], ring[1], ring[3] = meet(
            left, right, modulation, ring[0], ring[1], ring[3]
        )
        left, right = other_hop(left, right)
        left, right, ring[2] = meet(left, right, ring[2])
        done = by_core(left, right)
        done, ring = meet(done, ring)
        left, right = place_halves(ring, slots)
        others = self.swap(left, "y"), self.swap(right, "x")
        *done, left, right = meet(*done, left, right)
        results = attend(done, modulation)
        left_other, right_other, *results = meet(*others, *results)
        left = place([left, left_other], [y, 1 - y])
        right = place([right, right_other], [x, 1 - x])
        left, right = other_hop(left, right)
        return done, by_core(left, right), modulation, results

    def to_group(self, value):
        return lax.all_to_all(value, ("z", "y"), split_axis=0, concat_axis=0, tiled=True)

    def halves(self):
        return lax.axis_index("c")

    def begin(self, mine, send):
        return (mine, self.swap(send, "c"))

    def step(self, state, axis, start=0, count=None):
        mine, other = state
        parts = mine.shape[1]
        view = (4, 2) if (parts, axis) == (16, "y") else (parts // 2, 1)
        keep, send = fold(
            mine, other, lax.axis_index(axis), view, start, count or mine.shape[0]
        )
        return (keep, self.swap(send, axis))

    def last(self, *states):
        folded = [fold_last(mine, other, lax.axis_index("z")) for mine, other in states]
        keep, *sends = [
            parts[0] if len(states) == 1 else jnp.concatenate(parts, axis=0) for parts in zip(*folded)
        ]
        got = [self.shift(send, by) for by, send in enumerate(sends, 1)]
        total = keep
        for part in got:
            total = total + part.astype(F32)
        return total

    def own_rows(self, shard, dim=-2):
        return lax.dynamic_slice_in_dim(
            shard, self.group_index() * (D // 32), D // 32, dim % shard.ndim
        )

    def quarters(self, piece):
        x, c = lax.axis_index("x"), lax.axis_index("c")
        by_x = self.swap(piece, "x")
        by_c = self.swap(piece, "c")
        by_both = self.swap(by_x, "c")
        slots = []
        for at_x, at_c in every(2, 2):
            slots.append(jnp.where(at_x == x, 0, 1) + jnp.where(at_c == c, 0, 2))
        return slots, [piece, by_x, by_c, by_both]

    def images_begin(self, rows):
        own = rows.reshape(-1, D)
        return self.to_owners(jnp.broadcast_to(own[None], (16, *own.shape)))

    def images_end(self, got):
        c = lax.axis_index("c")
        return place([got, self.swap(got, "c")], [c, 1 - c]).reshape(-1, 8, D)

    def complete(self, piece):
        value = self.exchange(piece, "x")
        c = lax.axis_index("c")
        moves = lambda slot: [(part, (x,), (x, slot[part])) for part in range(2) for x in range(2)]
        value = place([value, self.swap(value, "c")], [c, 1 - c], (2, 2), moves)
        return value.reshape(D // 8, -1)

    def to_owners(self, pieces):
        return lax.all_to_all(pieces, self.chips, split_axis=0, concat_axis=0, tiled=True)

    def wide_slots_of(self, feeds):
        halved = []
        for slot in self.wide_slots:
            halved.append([] if slot is None else [feeds[slot[0]][slot[1]]])
        return slots_of(halved, self.owners, FF // 2)

    def wide_halves(self, got):
        return got, self.swap(got, "x")

    def wide_whole(self, got):
        half = FF // 2
        x, c = lax.axis_index("x"), lax.axis_index("c")
        both = place(list(got), [x, 1 - x])
        both = both.reshape(2, 2, 4, 2, D // 32, half)

        def moves(slot):
            return [
                (part, (p, x, z, y), (p, z, y, x, slot[part]))
                for part in range(2)
                for p, x, z, y in every(2, 2, 4, 2)
            ]

        whole = place([both, self.swap(both, "c")], [c, 1 - c], (2, 4, 2, 2, 2), moves)
        return whole.reshape(2, D, half)

    def square_slots(self, feeds):
        return slots_of([[] if slot is None else feeds[slot] for slot in self.slots], self.owners, D)

    def square_to_owners(self, slots, beside):
        got = self.to_owners(slots)
        got, beside = meet(got, beside)
        got = got.reshape(2, 4, 2, D // 32, D)
        c = lax.axis_index("c")

        def moves(slot):
            return [
                (part, (x, z, y), (z, y, x, slot[part]))
                for part in range(2)
                for x, z, y in every(2, 4, 2)
            ]

        return place([got, self.swap(got, "c")], [c, 1 - c], (4, 2, 2, 2), moves).reshape(D, D), beside

    def to_rows(self, whole):
        cols = whole.shape[1]
        blocks = whole.reshape(4, 2, 2, 2, D // 32, cols)
        blocks = lax.dynamic_index_in_dim(blocks, lax.axis_index("c"), 3, keepdims=False)
        blocks = blocks.transpose(2, 0, 1, 3, 4).reshape(16, D // 32, cols)
        return lax.all_to_all(blocks, self.chips, split_axis=0, concat_axis=0, tiled=True)


def lanes(shape, dim):
    return lax.broadcasted_iota(jnp.int32, shape, dim)


def norm_of(values):
    centred = values - jnp.mean(values, axis=-1, keepdims=True)
    inverse = lax.rsqrt(jnp.mean(centred * centred, axis=-1, keepdims=True) + NORM_EPS)
    return centred * inverse, inverse


def norm_back(incoming, normed, inverse):
    return inverse * (
        incoming
        - jnp.mean(incoming, axis=-1, keepdims=True)
        - normed * jnp.mean(incoming * normed, axis=-1, keepdims=True)
    )


def rotate_pair(value):
    first = lanes(value.shape, 1) % 32 < 16
    return jnp.where(first, -pltpu.roll(value, 112, 1), pltpu.roll(value, 16, 1))


def two_heads(value):
    low = lanes(value.shape, 1) < HDIM
    zero = jnp.zeros_like(value)
    return jnp.where(low, value, zero), jnp.where(low, zero, value)


def pair_at(pair):
    return slice(pair * 2 * HDIM, (pair + 1) * 2 * HDIM)


def attention_forward_kernel(
    length_ref,
    input_ref,
    cotangent_ref,
    modulation_ref,
    cosine_ref,
    sine_ref,
    query_key_ref,
    value_output_ref,
    first_ref,
    query_ref,
    key_ref,
    value_ref,
    probs_ref,
    attended_ref,
    attention_ref,
    middle_ref,
    second_ref,
    branch_ref,
):
    length = length_ref[pl.program_id(0)]
    row = lambda which: modulation_ref[0, which : which + 1, :]
    stream = input_ref[0].astype(F32)
    positions = stream.shape[0]
    normed, _ = norm_of(stream)
    first = (normed * (1.0 + row(1)) + row(0)).astype(BF16)
    first_ref[0] = first
    inside = lanes((positions, D), 0) < length
    upstream = jnp.where(inside, cotangent_ref[0].astype(F32), 0.0)
    branch_ref[0] = (row(5) * upstream).astype(BF16)
    value_ref[0] = dot(first, value_output_ref[:, :D]).astype(BF16)
    cosine, sine = cosine_ref[0], sine_ref[0]
    keep = lanes((positions, positions), 1) < length
    for pair in range(HEADS // 2):
        at = pair_at(pair)
        query = dot(first, query_key_ref[:, at])
        key = dot(first, query_key_ref[:, D + pair * 128 : D + (pair + 1) * 128])
        query = (query * cosine + rotate_pair(query) * sine).astype(BF16)
        key = (key * cosine + rotate_pair(key) * sine).astype(BF16)
        query_ref[0, :, at] = query
        key_ref[0, :, at] = key
        low = []
        for head, masked in enumerate(two_heads(query)):
            scores = dot(masked, key, NT) * HDIM ** (-0.5)
            scores = jnp.where(keep, scores, -1000000000.0)
            exponent = jnp.exp(scores - jnp.max(scores, axis=-1, keepdims=True))
            probs = exponent * (1.0 / jnp.sum(exponent, axis=-1, keepdims=True))
            probs_ref[0, 2 * pair + head] = probs
            low.append(probs.astype(BF16))
        values = two_heads(value_ref[0, :, at])
        attended_ref[0, :, at] = dot(
            jnp.concatenate(low, axis=1), jnp.concatenate(values, axis=0)
        ).astype(BF16)
    attention = dot(attended_ref[0], value_output_ref[:, D:])
    attention_ref[0] = attention
    middle = stream + row(2) * attention
    middle_ref[0] = middle
    normed, _ = norm_of(middle)
    second_ref[0] = (normed * (1.0 + row(4)) + row(3)).astype(BF16)


def split_rows(value, scratch, here, keep_ref, send_ref, which, cols):
    scratch[...] = value
    rows = keep_ref.shape[2]
    for i in range(keep_ref.shape[1]):
        for ref, at in ((keep_ref, here), (send_ref, 1 - here)):
            start = pl.multiple_of((2 * i + at) * rows, 8)
            ref[which, i, :, cols] = scratch[pl.ds(start, rows), :].astype(BF16)


def feed_forward_kernel(
    here_ref,
    second_ref,
    branch_ref,
    gate_ref,
    up_ref,
    down_ref,
    out_ref,
    back_ref,
    keep_ref,
    send_ref,
    second_t,
    branch_t,
    rows,
):
    step = pl.program_id(0)

    @pl.when(step == 0)
    def _():
        second_t[...] = second_ref[...].T
        branch_t[...] = branch_ref[...].T
        out_ref[...] = jnp.zeros_like(out_ref)
        back_ref[...] = jnp.zeros_like(back_ref)

    gate, up, down = gate_ref[...], up_ref[...], down_ref[...]
    gate_pre = dot(second_ref[...], gate)
    up_pre = dot(second_ref[...], up)
    sigmoid = 1.0 / (1.0 + jnp.exp(-gate_pre))
    swish = gate_pre * sigmoid
    hidden = (swish * up_pre).astype(BF16)
    out_ref[...] += dot(hidden, down, NT)
    grad_hidden = dot(branch_ref[...], down)
    grad_gate = (grad_hidden * up_pre * sigmoid * (1.0 + gate_pre * (1.0 - sigmoid))).astype(BF16)
    grad_up = (grad_hidden * swish).astype(BF16)
    back_ref[...] += dot(grad_gate, gate, NT) + dot(grad_up, up, NT)
    everything = slice(None)
    products = ((second_t, grad_gate), (second_t, grad_up), (branch_t, hidden))
    for which, (left, right) in enumerate(products):
        split_rows(
            dot(left[...], right), rows, here_ref[0], keep_ref, send_ref, which, everything
        )


def attention_backward_kernel(
    length_ref,
    branch_left_ref,
    branch_right_ref,
    second_left_ref,
    second_right_ref,
    middle_ref,
    cotangent_ref,
    modulation_ref,
    attention_ref,
    value_output_ref,
    query_ref,
    key_ref,
    value_ref,
    probs_ref,
    cosine_ref,
    sine_ref,
    output_ref,
    stream_ref,
    grads_ref,
    sums_ref,
    attended_grad,
):
    length = length_ref[pl.program_id(0)]
    row = lambda which: modulation_ref[0, which : which + 1, :]
    middle = middle_ref[0]
    positions = middle.shape[0]
    inside = lanes((positions, D), 0) < length
    upstream = jnp.where(inside, cotangent_ref[0].astype(F32), 0.0)
    branch = branch_left_ref[0] + branch_right_ref[0]
    output_ref[0] = (middle + row(5) * branch).astype(BF16)
    total = lambda value: jnp.sum(value, axis=0, keepdims=True)
    gate_two = total(upstream * branch)
    second = second_left_ref[0] + second_right_ref[0]
    normed, inverse = norm_of(middle)
    scale_two = total(second * normed)
    shift_two = total(second)
    stream = upstream + norm_back(second * (1.0 + row(4)), normed, inverse)
    stream_ref[0] = stream
    gate_one = total(stream * attention_ref[0])
    blank = jnp.zeros_like(gate_one)
    sums_ref[0] = jnp.concatenate(
        [blank, blank, gate_one, shift_two, scale_two, gate_two, blank, blank], axis=0
    )
    grad_attention = (row(2) * stream).astype(BF16)
    grads_ref[3, 0] = grad_attention
    attended_grad[...] = dot(grad_attention, value_output_ref[:, D:], NT).astype(BF16)
    cosine, sine = cosine_ref[0], sine_ref[0]
    for pair in range(HEADS // 2):
        at = pair_at(pair)
        query, key, value = query_ref[0, :, at], key_ref[0, :, at], value_ref[0, :, at]
        attended = two_heads(attended_grad[:, at])
        low, scores = [], []
        for head in range(2):
            probs = probs_ref[0, 2 * pair + head]
            grad_probs = dot(attended[head], value, NT)
            inner = jnp.sum(grad_probs * probs, axis=-1, keepdims=True)
            scores.append((probs * (grad_probs - inner)).astype(BF16))
            low.append(probs.astype(BF16))
        grads_ref[2, 0, :, at] = dot(
            jnp.concatenate(low, axis=0), jnp.concatenate(attended, axis=0), TN
        ).astype(BF16)
        grad_query = dot(
            jnp.concatenate(scores, axis=1), jnp.concatenate(two_heads(key), axis=0)
        ) * HDIM ** (-0.5)
        grad_key = dot(
            jnp.concatenate(scores, axis=0), jnp.concatenate(two_heads(query), axis=0), TN
        ) * HDIM ** (-0.5)
        grads_ref[0, 0, :, at] = (grad_query * cosine - rotate_pair(grad_query * sine)).astype(BF16)
        grads_ref[1, 0, :, at] = (grad_key * cosine - rotate_pair(grad_key * sine)).astype(BF16)


def projection_backward_kernel(
    here_ref,
    grads_in_ref,
    first_ref,
    attended_ref,
    input_ref,
    modulation_ref,
    stream_ref,
    sums_ref,
    active_ref,
    query_key_ref,
    value_output_ref,
    keep_ref,
    send_ref,
    input_grad_ref,
    modulation_grad_ref,
    first_t,
    first_grad,
    rows,
):
    images, positions = input_ref.shape[:2]
    tokens = images * positions
    flat = lambda ref: ref[...].reshape(tokens, D)
    step = pl.program_id(0)

    def product(grads):
        split_rows(dot(first_t[...], grads), rows, here_ref[0], keep_ref, send_ref, 0, slice(None))

    @pl.when(step == 0)
    def _():
        first_t[...] = flat(first_ref).T
        grads = grads_in_ref[0].reshape(tokens, D)
        product(grads)
        first_grad[...] = dot(grads, query_key_ref[:, :D], NT)

    @pl.when(step == 1)
    def _():
        grads = grads_in_ref[0].reshape(tokens, D)
        product(grads)
        first_grad[...] += dot(grads, query_key_ref[:, D:], NT)

    @pl.when(step == 2)
    def _():
        grads = grads_in_ref[0].reshape(tokens, D)
        product(grads)
        first_grad[...] += dot(grads, value_output_ref[:, :D], NT)

    @pl.when(step == 3)
    def _():
        first_t[...] = flat(attended_ref).T
        product(grads_in_ref[0].reshape(tokens, D))
        for image in range(images):
            at = slice(image * positions, (image + 1) * positions)
            normed, inverse = norm_of(input_ref[image].astype(F32))
            first = first_grad[at, :]
            scale_one = jnp.sum(first * normed, axis=0, keepdims=True)
            shift_one = jnp.sum(first, axis=0, keepdims=True)
            scaled = first * (1.0 + modulation_ref[image, 1:2, :])
            input_grad_ref[image] = stream_ref[image] + norm_back(scaled, normed, inverse)
            modulation_grad_ref[image] = jnp.concatenate(
                [
                    shift_one,
                    scale_one,
                    sums_ref[image, 2:6, :],
                    active_ref[image : image + 1, :].astype(F32),
                    jnp.zeros_like(shift_one),
                ],
                axis=0,
            ).astype(BF16)


BIG_VMEM = 58 * 1024 * 1024


def whole(array):
    return pl.BlockSpec(array.shape, lambda *_: (0,) * array.ndim)


def by_image(array):
    return pl.BlockSpec((1, *array.shape[1:]), lambda b: (b,) + (0,) * (array.ndim - 1))


def call(body, grid, ins, in_specs, outs, out_specs, scratch, flops, name):
    size = sum(a.size * a.dtype.itemsize for a in (*ins, *outs))
    return pl.pallas_call(
        body,
        grid=grid,
        out_shape=outs,
        in_specs=in_specs,
        out_specs=out_specs,
        scratch_shapes=scratch,
        compiler_params=pltpu.CompilerParams(vmem_limit_bytes=BIG_VMEM),
        cost_estimate=pl.CostEstimate(flops=flops, bytes_accessed=size, transcendentals=0),
        name=name,
    )(*ins)


def attention_forward(lengths, inputs, cotangent, modulation, cosine, sine, query_key, value_output):
    images, positions, _ = inputs.shape
    ins = (lengths, inputs, cotangent, modulation, cosine, sine, query_key, value_output)
    in_specs = [pl.BlockSpec(memory_space=pltpu.SMEM)]
    in_specs += [by_image(a) for a in ins[1:6]] + [whole(a) for a in ins[6:]]
    token = lambda dtype: jax.ShapeDtypeStruct((images, positions, D), dtype)
    outs = (
        token(BF16),
        token(BF16),
        token(BF16),
        token(BF16),
        jax.ShapeDtypeStruct((images, HEADS, positions, positions), F32),
        token(BF16),
        token(F32),
        token(F32),
        token(BF16),
        token(BF16),
    )
    flops = 2 * images * positions * D * (4 * D + 2 * positions)
    return call(
        attention_forward_kernel,
        (images,),
        ins,
        in_specs,
        outs,
        [by_image(a) for a in outs],
        [],
        flops,
        "attention_forward",
    )


def feed_forward(here, second, branch, weight):
    tokens = second.shape[0]
    units = weight.shape[1] // 3
    tile = 256
    steps = units // tile
    ins = (here.reshape(1).astype(jnp.int32), second, branch, weight, weight, weight)
    in_specs = [pl.BlockSpec(memory_space=pltpu.SMEM), whole(second), whole(branch)] + [
        pl.BlockSpec((D, tile), lambda t, which=which: (0, which * steps + t)) for which in range(3)
    ]
    outs = (
        jax.ShapeDtypeStruct((tokens, D), F32),
        jax.ShapeDtypeStruct((tokens, D), F32),
        jax.ShapeDtypeStruct((3, D // 48, 24, units), BF16),
        jax.ShapeDtypeStruct((3, D // 48, 24, units), BF16),
    )
    out_specs = [whole(outs[0]), whole(outs[1])]
    out_specs += [pl.BlockSpec((3, D // 48, 24, tile), lambda t: (0, 0, 0, t))] * 2
    scratch = [pltpu.VMEM((D, tokens), BF16), pltpu.VMEM((D, tokens), BF16), pltpu.VMEM((D, tile), F32)]
    flops = 2 * 9 * tokens * D * units
    return call(
        feed_forward_kernel, (steps,), ins, in_specs, outs, out_specs, scratch, flops, "feed_forward"
    )


def attention_backward(lengths, *ins):
    images, positions, _ = ins[0].shape
    shared = 8
    in_specs = [pl.BlockSpec(memory_space=pltpu.SMEM)]
    in_specs += [whole(a) if i == shared else by_image(a) for i, a in enumerate(ins)]
    outs = (
        jax.ShapeDtypeStruct((images, positions, D), BF16),
        jax.ShapeDtypeStruct((images, positions, D), F32),
        jax.ShapeDtypeStruct((4, images, positions, D), BF16),
        jax.ShapeDtypeStruct((images, 8, D), F32),
    )
    out_specs = [
        by_image(outs[0]),
        by_image(outs[1]),
        pl.BlockSpec((4, 1, positions, D), lambda b: (0, b, 0, 0)),
        by_image(outs[3]),
    ]
    flops = 2 * images * positions * D * (D + 5 * positions)
    return call(
        attention_backward_kernel,
        (images,),
        (lengths, *ins),
        in_specs,
        outs,
        out_specs,
        [pltpu.VMEM((positions, D), BF16)],
        flops,
        "attention_backward",
    )


def projection_backward(here, *ins):
    _, images, positions, _ = ins[0].shape
    tokens = images * positions
    in_specs = [pl.BlockSpec(memory_space=pltpu.SMEM)]
    in_specs += [pl.BlockSpec((1, images, positions, D), lambda k: (k, 0, 0, 0))]
    in_specs += [whole(a) for a in ins[1:]]
    ins = (here.reshape(1).astype(jnp.int32), *ins)
    outs = (
        jax.ShapeDtypeStruct((4, D // 48, 24, D), BF16),
        jax.ShapeDtypeStruct((4, D // 48, 24, D), BF16),
        jax.ShapeDtypeStruct((images, positions, D), F32),
        jax.ShapeDtypeStruct((images, 8, D), BF16),
    )
    out_specs = [pl.BlockSpec((1, D // 48, 24, D), lambda k: (k, 0, 0, 0))] * 2
    out_specs += [whole(outs[2]), whole(outs[3])]
    scratch = [pltpu.VMEM((D, tokens), BF16), pltpu.VMEM((tokens, D), F32), pltpu.VMEM((D, D), F32)]
    return call(
        projection_backward_kernel,
        (4,),
        ins,
        in_specs,
        outs,
        out_specs,
        scratch,
        2 * 7 * tokens * D * D,
        "projection_backward",
    )


def swish_value(values):
    return values / (1.0 + jnp.exp(-values))


def rope_tables(extents, positions):
    quarter = HDIM // 4
    places = jnp.arange(positions, dtype=jnp.int32)
    widths = extents[:, 1]
    row_place = (places[None, :] // widths[:, None]).astype(F32)
    col_place = (places[None, :] % widths[:, None]).astype(F32)
    lane = jnp.arange(2 * HDIM) % HDIM
    frequency = 10000.0 ** (-(lane % quarter).astype(F32) / quarter)
    by_row = lane < 2 * quarter
    angle = jnp.where(by_row, row_place[:, :, None], col_place[:, :, None]) * frequency
    return jnp.cos(angle), jnp.sin(angle)


def local(
    comm,
    inputs,
    cotangent,
    image_shape,
    time_bins,
    time_table,
    modulation_master,
    projection_master,
    output_master,
    expand_master,
    shrink_master,
    modulation_moment,
    projection_moment,
    output_moment,
    expand_moment,
    shrink_moment,
):
    masters = (modulation_master, projection_master, output_master, expand_master, shrink_master)
    moments = (modulation_moment, projection_moment, output_moment, expand_moment, shrink_moment)
    images, positions, features = inputs.shape
    tokens = images * positions
    rows = modulation_master.shape[1]
    row_index = comm.row_index()

    half = FF // 2
    shrink_low = shrink_master.astype(BF16).T
    packed_attention = jnp.concatenate(
        [projection_master[i].astype(BF16) for i in range(3)] + [output_master.astype(BF16)], axis=1
    )
    packed_units = jnp.concatenate(
        [
            part
            for cols in (slice(None, half), slice(half, None))
            for part in (
                expand_master[0, :, cols].astype(BF16),
                expand_master[1, :, cols].astype(BF16),
                shrink_low[:, cols],
            )
        ],
        axis=1,
    )
    selector = (
        time_bins[:, None] == jnp.arange(time_table.shape[0], dtype=jnp.int32)[None, :]
    ).astype(F32)
    active = swish_value(jnp.dot(selector, time_table, precision=HIGHEST)).astype(BF16)

    def group_rows():
        return comm.to_group(active.reshape(images, comm.row_shards, rows).transpose(1, 0, 2))

    def modulation_of(group):
        partial = jnp.einsum(
            "bd,kde->bke",
            group.reshape(-1, rows),
            modulation_master.astype(BF16),
            preferred_element_type=F32,
        )
        return jnp.sum(
            comm.to_group(partial.reshape(comm.row_shards, images, 6, features)), axis=0
        )

    cosine, sine = rope_tables(image_shape, positions)
    lengths = image_shape[:, 0] * image_shape[:, 1]

    def attend(weights, modulation):
        return attention_forward(
            lengths, inputs, cotangent, modulation, cosine, sine, weights[0], weights[1]
        )

    first, second, modulation, results = comm.gather_weights(
        packed_attention, packed_units, (group_rows, modulation_of), attend
    )
    query_key_weight, value_output_weight = first
    left_weight, right_weight = second
    (first_input, query, key, value, probs, attended, attention, middle, second_input, grad_branch) = (
        results
    )
    second_flat = second_input.reshape(tokens, D)
    branch_flat = grad_branch.reshape(tokens, D)
    shaped = lambda v: v.reshape(images, positions, D)
    here = comm.halves()
    branch_left, back_left, *grads = feed_forward(here, second_flat, branch_flat, left_weight)
    left_sum = comm.begin(*grads)
    second_flat, left_sum = meet(second_flat, left_sum)
    left_sum = comm.step(left_sum, "x", 0, 2), comm.step(left_sum, "y", 2, 1)
    branch_right, back_right, *grads = feed_forward(here, second_flat, branch_flat, right_weight)
    back_right, left_sum, grads = meet(back_right, left_sum, grads)
    right_sum = comm.begin(*grads)
    back_right, left_sum, right_sum = meet(back_right, left_sum, right_sum)
    left_sum = comm.step(left_sum[0], "y"), comm.step(left_sum[1], "x")
    right_sum = comm.step(right_sum, "x", 0, 2), comm.step(right_sum, "y", 2, 1)
    block_output, grad_stream, grads, sums = attention_backward(
        lengths,
        shaped(branch_left),
        shaped(branch_right),
        shaped(back_left),
        shaped(back_right),
        middle,
        cotangent,
        modulation,
        attention,
        value_output_weight,
        query,
        key,
        value,
        probs,
        cosine,
        sine,
    )
    left_sum, right_sum, grads = meet(left_sum, right_sum, grads)
    left_piece = comm.last(*left_sum)
    right_sum = comm.step(right_sum[0], "y"), comm.step(right_sum[1], "x")
    *grads, input_gradient, grad_modulation = projection_backward(
        here,
        grads,
        first_input,
        attended,
        inputs,
        modulation,
        grad_stream,
        sums,
        active,
        query_key_weight,
        value_output_weight,
    )
    left_piece, right_sum, grads, grad_modulation = meet(left_piece, right_sum, grads, grad_modulation)
    attention_sum = comm.begin(*grads)
    attention_sum, right_sum = meet(attention_sum, right_sum)
    first_sum = comm.step(attention_sum, "x", 0, 2)
    second_sum = comm.step(attention_sum, "y", 2, 2)
    right_piece = comm.last(*right_sum)
    gathered = comm.images_begin(grad_modulation)
    right_piece, *kept = meet(right_piece, first_sum[0], second_sum[0])
    first_sum, second_sum = (kept[0], *first_sum[1:]), (kept[1], *second_sum[1:])

    owner = comm.owner_index()
    own_expand = comm.own_rows(expand_moment)
    own_shrink = comm.own_rows(shrink_moment.T)
    wide_feed = [
        [
            (
                (piece, ((which,), 0, half)),
                (own_shrink, ((), side * half, half))
                if which == 2
                else (own_expand, ((which,), side * half, half)),
            )
            for side, piece in enumerate((left_piece, right_piece))
        ]
        for which in range(3)
    ]
    wide = comm.to_owners(comm.wide_slots_of(wide_feed))
    first_sum, second_sum, gathered = meet(first_sum, second_sum, gathered)
    gathered = comm.images_end(gathered)
    active_all = gathered[:, 6]
    first_sum = comm.step(first_sum, "y")
    second_sum = comm.step(second_sum, "x")
    first_sum, second_sum, wide, gathered = meet(first_sum, second_sum, wide, gathered)
    wide = comm.wide_halves(wide)
    attention_piece, wide = meet(comm.last(first_sum, second_sum), wide)
    wide = comm.wide_whole(wide)

    own_modulation = comm.own_rows(modulation_moment)
    own_projection = comm.own_rows(projection_moment)
    own_output = comm.own_rows(output_moment)
    square_feed = [[(None, (own_modulation, ((k,), 0, D)))] for k in range(6)]
    for k in range(3):
        square_feed.append(
            [((attention_piece, ((k,), 0, D)), (own_projection, ((k,), 0, D)))]
        )
    square_feed.append([((attention_piece, ((3,), 0, D)), (own_output, ((), 0, D)))])
    slots, wide = meet(comm.square_slots(square_feed), wide)
    active_wide = pick([0 if slot is None else 1 for slot in comm.wide_slots], owner)
    wide_done = newton_schulz(active_wide, wide)
    square, wide_done = comm.square_to_owners(slots, wide_done)
    item = pick([-1 if slot is None else slot for slot in comm.slots], owner)
    which = jnp.where((item >= 0) & (item < 6), item, 0)
    right = lax.dynamic_index_in_dim(gathered, which, 1, keepdims=False)
    right = jnp.where(item < 6, right, jnp.zeros_like(right))
    square_done = newton_schulz((item >= 0).astype(jnp.int32), square, active_all, right)
    size = FF // comm.wide_parts
    part = pick([0 if slot is None else slot[1] for slot in comm.wide_slots], owner)
    mine = lax.dynamic_slice_in_dim(wide_done, part * size, size, 1)
    mine = mine + jnp.pad(square_done, ((0, 0), (0, size - D)))
    back = comm.to_rows(mine)

    pieces = [(left_piece, (i,), half) for i in range(3)]
    pieces += [(right_piece, (i,), half) for i in range(3)]
    pieces += [(attention_piece, (i,), D) for i in range(4)]
    totals_low = comm.complete(pack(pieces)).astype(F32)
    by_unit = [
        jnp.concatenate(
            [totals_low[:, (side * 3 + i) * half : (side * 3 + i + 1) * half] for side in range(2)],
            axis=1,
        )
        for i in range(3)
    ]
    steps = [
        (back, (comm.wide_slots.index((i, p)),), size) for i in range(3) for p in range(comm.wide_parts)
    ]
    steps += [(back, (comm.slots.index(i),), D) for i in range(10)]
    updated = update(*comm.quarters(pack(steps)), masters)
    active_rows = lax.dynamic_slice_in_dim(active_all, row_index * rows, rows, 1)
    modulation_total = jnp.einsum(
        "bd,bke->kde",
        active_rows,
        gathered[:, :6],
        preferred_element_type=F32,
    )
    after = 3 * FF
    totals = (
        modulation_total,
        jnp.stack([totals_low[:, after + i * D : after + (i + 1) * D] for i in range(3)]),
        totals_low[:, after + 3 * D :],
        jnp.stack(by_unit[:2]),
        by_unit[2].T,
    )
    states = tuple((MOMENTUM_DECAY * moment + total for moment, total in zip(moments, totals)))
    return (block_output, input_gradient, *totals, *updated, *states)


def solution(mesh):
    if mesh.shape["dp"] == 4 and mesh.shape["fsdp"] == 8:
        comm = Torus(mesh)
    else:
        comm = Plain(mesh)
    images, rows = comm.images, comm.rows
    by_row = (
        P(None, rows, None),
        P(None, rows, None),
        P(rows, None),
        P(None, rows, None),
        P(None, rows),
    )
    return jax.shard_map(
        functools.partial(local, comm),
        mesh=comm.mesh,
        in_specs=(
            P(images, None, None),
            P(images, None, None),
            P(images, None),
            P(images),
            P(),
            *by_row,
            *by_row,
        ),
        out_specs=(P(images, None, None), P(images, None, None), *by_row, *by_row, *by_row),
        check_vma=False,
    )
```

```python
import functools
import itertools

import jax
import jax.numpy as jnp
from jax import lax
from jax.experimental import pallas as pl
from jax.experimental.pallas import tpu as pltpu
from jax.sharding import Mesh, PartitionSpec as P

D = 768
HEADS = 12
HDIM = 64
FF = 2048
NS_ITERS = 5
NORM_EPS = 1e-06
FROBENIUS_EPS = 1e-07
COEFF_FIRST = 3.4445
COEFF_SECOND = -4.775
COEFF_THIRD = 2.0315
MOMENTUM_DECAY = 0.9
LEARN_RATE = 1.0
HIGHEST = lax.Precision.HIGHEST
BF16 = jnp.bfloat16
F32 = jnp.float32
ITEMS = 13
NT = (((1,), (1,)), ((), ()))
NN = (((1,), (0,)), ((), ()))
TN = (((0,), (0,)), ((), ()))


def dot(a, b, dims=NN):
    return lax.dot_general(a, b, dims, preferred_element_type=F32)


def newton_schulz_kernel(width, active_ref, feed_ref, left_ref, right_ref, out_ref, x, xb, gram, low, poly):
    tile = 256
    tiles = D // tile
    blocks = width // tile
    spans = [slice(i * tile, (i + 1) * tile) for i in range(tiles)]

    def diagonal(part, other):
        rows = lax.broadcasted_iota(jnp.int32, (tile, tile), 0)
        cols = lax.broadcasted_iota(jnp.int32, (tile, tile), 1)
        return jnp.where(rows == cols, part, other)

    def block(b):
        return pl.ds(pl.multiple_of(b * tile, tile), tile)

    @pl.when(active_ref[0] != 0)
    def _():
        def load(b, acc):
            if len(feed_ref.shape) == 3:
                per = feed_ref.shape[2] // tile
                v = feed_ref[b // per, :, block(lax.rem(b, per))].astype(F32)
            else:
                v = feed_ref[:, block(b)].astype(F32)
            if right_ref is not None:
                v = v + (1.0 + MOMENTUM_DECAY) * dot(left_ref[...], right_ref[:, block(b)], TN)
            x[:, block(b)] = v
            return acc + jnp.sum(v * v, axis=0, keepdims=True)

        total = lax.fori_loop(0, blocks, load, jnp.zeros((1, tile), F32))
        total = jnp.sum(total, keepdims=True)
        inverse = 1.0 / (jnp.sqrt(total) + FROBENIUS_EPS)

        def scale_block(b, carry):
            v = x[:, block(b)] * inverse
            x[:, block(b)] = v
            xb[:, block(b)] = v.astype(BF16)
            return carry

        lax.fori_loop(0, blocks, scale_block, 0)

        def iterate(step, carry):
            trace = jnp.zeros((1, tile), F32)
            for i in range(tiles):
                for j in range(i + 1):
                    part = dot(xb[spans[i], :], xb[spans[j], :], NT)
                    gram[spans[i], spans[j]] = part
                    if i == j:
                        trace = trace + jnp.sum(diagonal(part, 0.0), axis=0, keepdims=True)
                    else:
                        lower = part.astype(BF16)
                        low[spans[i], spans[j]] = lower
                        low[spans[j], spans[i]] = lower.T
            shift = jnp.sum(trace, keepdims=True) / D
            for i in range(tiles):
                part = gram[spans[i], spans[i]]
                part = diagonal(part - shift, part)
                gram[spans[i], spans[i]] = part
                low[spans[i], spans[i]] = part.astype(BF16)
            linear = COEFF_SECOND + 2.0 * COEFF_THIRD * shift
            level = COEFF_SECOND * shift + COEFF_THIRD * shift * shift
            trace = jnp.zeros((1, tile), F32)
            for i in range(tiles):
                for j in range(i + 1):
                    part = linear * gram[spans[i], spans[j]] + COEFF_THIRD * dot(
                        low[spans[i], :], low[spans[j], :], NT
                    )
                    if i == j:
                        gram[spans[i], spans[j]] = part
                        trace = trace + jnp.sum(diagonal(part, 0.0), axis=0, keepdims=True)
                    else:
                        lower = part.astype(BF16)
                        poly[spans[i], spans[j]] = lower
                        poly[spans[j], spans[i]] = lower.T
            mean = jnp.sum(trace, keepdims=True) / D
            for i in range(tiles):
                part = gram[spans[i], spans[i]]
                poly[spans[i], spans[i]] = diagonal(part - mean, part).astype(BF16)
            scale = COEFF_FIRST + level + mean

            size = width // 2 if width > 1024 else width
            for b in range(width // size):
                cols = slice(b * size, (b + 1) * size)
                new = scale * x[:, cols] + dot(poly[...], xb[:, cols])
                x[:, cols] = new
                xb[:, cols] = new.astype(BF16)
            return carry

        lax.fori_loop(0, NS_ITERS, iterate, 0)
        out_ref[...] = xb[...]

    @pl.when(active_ref[0] == 0)
    def _():
        out_ref[...] = jnp.zeros_like(out_ref)


def newton_schulz(active, feed, left=None, right=None):
    width = feed.size // D
    operands = [active.reshape(1).astype(jnp.int32), feed]
    if left is None:

        def body(active_ref, feed_ref, *rest):
            newton_schulz_kernel(width, active_ref, feed_ref, None, None, *rest)

    else:
        body = functools.partial(newton_schulz_kernel, width)
        operands += [left, right]
    vmem = pl.BlockSpec(memory_space=pltpu.VMEM)
    return pl.pallas_call(
        body,
        out_shape=jax.ShapeDtypeStruct((D, width), BF16),
        in_specs=[pl.BlockSpec(memory_space=pltpu.SMEM)] + [vmem] * (len(operands) - 1),
        out_specs=vmem,
        scratch_shapes=[
            pltpu.VMEM((D, width), F32),
            pltpu.VMEM((D, width), BF16),
            pltpu.VMEM((D, D), F32),
            pltpu.VMEM((D, D), BF16),
            pltpu.VMEM((D, D), BF16),
        ],
        compiler_params=pltpu.CompilerParams(vmem_limit_bytes=40 * 1024 * 1024),
        cost_estimate=pl.CostEstimate(
            flops=NS_ITERS * 4 * D * D * (width + D), bytes_accessed=4 * D * width, transcendentals=0
        ),
        name="newton_schulz",
    )(*operands)


def tie(value, *others):
    return lax.optimization_barrier((value, *others))[0]


def meet(*values):
    flat, tree = jax.tree.flatten(values)
    return jax.tree.unflatten(tree, lax.optimization_barrier(tuple(flat)))


def fold(mine, other, here, view, start, count):
    before, after = view
    rows, cols = mine.shape[-2:]
    shape = (mine.shape[0], before, 2, after, rows, cols)
    block = pl.BlockSpec((1, *shape[1:]), lambda k: (start + k, 0, 0, 0, 0, 0))
    out = jax.ShapeDtypeStruct((count, before, after, rows, cols), BF16)
    out_block = pl.BlockSpec((1, *out.shape[1:]), lambda k: (k, 0, 0, 0, 0))

    def body(here_ref, mine_ref, other_ref, keep_ref, send_ref):
        here = here_ref[0]
        for ref, at in ((send_ref, 1 - here), (keep_ref, here)):
            ref[0] = (mine_ref[0, :, at].astype(F32) + other_ref[0, :, at].astype(F32)).astype(BF16)

    size = 6 * count * before * after * rows * cols * 2
    keep, send = pl.pallas_call(
        body,
        grid=(count,),
        out_shape=(out, out),
        in_specs=[pl.BlockSpec(memory_space=pltpu.SMEM), block, block],
        out_specs=(out_block, out_block),
        compiler_params=pltpu.CompilerParams(vmem_limit_bytes=24 * 1024 * 1024),
        cost_estimate=pl.CostEstimate(flops=0, bytes_accessed=size, transcendentals=0),
        name="fold",
    )(here.reshape(1).astype(jnp.int32), mine.reshape(shape), other.reshape(shape))
    flat = lambda v: v.reshape(count, before * after, rows, cols)
    return flat(keep), flat(send)


def fold_last(states, here):
    rows, cols = states[0][0].shape[-2:]
    counts = [mine.shape[0] for mine, _ in states]
    k = sum(counts)

    def body(here_ref, *refs):
        ins, outs = refs[: 2 * len(states)], refs[2 * len(states) :]
        for by, ref in enumerate(outs):
            at = lax.rem(here_ref[0] + by, 4)
            start = 0
            for i, count in enumerate(counts):
                total = ins[2 * i][:, at].astype(F32) + ins[2 * i + 1][:, at].astype(F32)
                ref[start : start + count] = total.astype(ref.dtype)
                start += count

    vmem = pl.BlockSpec(memory_space=pltpu.VMEM)
    return pl.pallas_call(
        body,
        out_shape=(jax.ShapeDtypeStruct((k, rows, cols), F32),)
        + (jax.ShapeDtypeStruct((k, rows, cols), BF16),) * 3,
        in_specs=[pl.BlockSpec(memory_space=pltpu.SMEM)] + [vmem] * (2 * len(states)),
        out_specs=(vmem,) * 4,
        compiler_params=pltpu.CompilerParams(vmem_limit_bytes=24 * 1024 * 1024),
        cost_estimate=pl.CostEstimate(
            flops=0, bytes_accessed=28 * k * rows * cols, transcendentals=0
        ),
        name="fold_last",
    )(here.reshape(1).astype(jnp.int32), *[part for state in states for part in state])


def place(parts, slots, lead=None, moves=None):
    count = len(parts)
    if lead is None:
        lead = (count, *parts[0].shape[:-2])
        moves = lambda slot: [(i, (), (slot[i],)) for i in range(count)]

    def body(slot_ref, *refs):
        ins, out = refs[:count], refs[count]
        for part, source, target in moves(slot_ref):
            out[target] = ins[part][source] if source else ins[part][...]

    size = count * parts[0].size * parts[0].dtype.itemsize
    vmem = pl.BlockSpec(memory_space=pltpu.VMEM)
    return pl.pallas_call(
        body,
        out_shape=jax.ShapeDtypeStruct((*lead, *parts[0].shape[-2:]), parts[0].dtype),
        in_specs=[pl.BlockSpec(memory_space=pltpu.SMEM)] + [vmem] * count,
        out_specs=vmem,
        cost_estimate=pl.CostEstimate(flops=0, bytes_accessed=2 * size, transcendentals=0),
        compiler_params=pltpu.CompilerParams(vmem_limit_bytes=24 * 1024 * 1024),
        name="place",
    )(jnp.stack(slots).astype(jnp.int32), *parts)


def place_halves(parts, slots):
    count = len(parts)
    rows, cols = parts[0].shape
    half = cols // 2

    def body(slot_ref, *refs):
        left, right = refs[count:]
        for i, ref in enumerate(refs[:count]):
            left[slot_ref[i]] = ref[:, :half]
            right[slot_ref[i]] = ref[:, half:]

    vmem = pl.BlockSpec(memory_space=pltpu.VMEM)
    shape = jax.ShapeDtypeStruct((count, rows, half), parts[0].dtype)
    return pl.pallas_call(
        body,
        out_shape=(shape, shape),
        in_specs=[pl.BlockSpec(memory_space=pltpu.SMEM)] + [vmem] * count,
        out_specs=(vmem, vmem),
        cost_estimate=pl.CostEstimate(flops=0, bytes_accessed=16 * rows * cols, transcendentals=0),
        compiler_params=pltpu.CompilerParams(vmem_limit_bytes=24 * 1024 * 1024),
        name="place_halves",
    )(jnp.stack(slots).astype(jnp.int32), *parts)


def slots_of(feeds, owners, width, quarter, extra=None):
    more = 0 if extra is None else extra.shape[0]
    arrays, index = [], {}

    def note(array):
        if array is None:
            return None
        source, columns = array
        if id(source) not in index:
            index[id(source)] = len(arrays)
            arrays.append(source)
        return (index[id(source)], columns)

    noted = [[(note(total), note(moment)) for total, moment in feed] for feed in feeds]
    rows = arrays[0].shape[-2]
    for total, _ in sum(feeds, []):
        if total is not None:
            rows = total[0].shape[-2]
    if all(total is None or total[0].shape[-2] == moment[0].shape[-2] for total, moment in sum(feeds, [])):
        quarter = jnp.int32(0)

    def block(array):
        shape = (*array.shape[:-2], rows, array.shape[-1])
        lead = (0,) * (array.ndim - 2)
        if array.shape[-2] == rows:
            return pl.BlockSpec(shape, lambda i, q: (*lead, 0, 0))
        return pl.BlockSpec(shape, lambda i, q: (*lead, q[0], 0))

    def body(_, *refs):
        out = refs[-1]
        if more:
            out = refs[-1].at[:, :rows]
            for slot in range(owners):
                refs[-1][slot, rows:] = refs[-2][...]

        def read(what):
            place_of, (lead, start, size) = what
            ref = refs[place_of]
            return ref[(*lead, slice(None), slice(start, start + size))].astype(F32)

        first = {}
        for slot in range(owners):
            if not noted[slot]:
                out[slot] = jnp.zeros((rows, width), BF16)
                continue
            key = str(noted[slot])
            if key in first:
                out[slot] = out[first[key]]
                continue
            first[key] = slot
            at = 0
            for total, moment in noted[slot]:
                value = MOMENTUM_DECAY * MOMENTUM_DECAY * read(moment)
                if total is not None:
                    value = value + (1.0 + MOMENTUM_DECAY) * read(total)
                out[slot, :, at : at + value.shape[1]] = value.astype(BF16)
                at += value.shape[1]

    return pl.pallas_call(
        body,
        out_shape=jax.ShapeDtypeStruct((owners, rows + more, width), BF16),
        grid_spec=pltpu.PrefetchScalarGridSpec(
            num_scalar_prefetch=1,
            grid=(1,),
            in_specs=[block(array) for array in arrays]
            + [pl.BlockSpec((more, width), lambda i, q: (0, 0))] * (more > 0),
            out_specs=pl.BlockSpec((owners, rows + more, width), lambda i, q: (0, 0, 0)),
        ),
        cost_estimate=pl.CostEstimate(
            flops=0, bytes_accessed=2 * owners * rows * width, transcendentals=0
        ),
        compiler_params=pltpu.CompilerParams(vmem_limit_bytes=24 * 1024 * 1024),
        name="slots",
    )(quarter.reshape(1).astype(jnp.int32), *arrays, *([extra] if more else []))


def pack(parts):
    arrays, index = [], {}
    for array, _, _ in parts:
        if id(array) not in index:
            index[id(array)] = len(arrays)
            arrays.append(array)
    rows = arrays[0].shape[-2]
    total = sum(cols for _, _, cols in parts)

    def body(*refs):
        at = 0
        for array, lead, cols in parts:
            value = refs[index[id(array)]][(*lead, slice(None), slice(0, cols))]
            refs[-1][:, at : at + cols] = value.astype(BF16)
            at += cols

    vmem = pl.BlockSpec(memory_space=pltpu.VMEM)
    return pl.pallas_call(
        body,
        out_shape=jax.ShapeDtypeStruct((rows, total), BF16),
        in_specs=[vmem] * len(arrays),
        out_specs=vmem,
        cost_estimate=pl.CostEstimate(flops=0, bytes_accessed=6 * rows * total, transcendentals=0),
        compiler_params=pltpu.CompilerParams(vmem_limit_bytes=24 * 1024 * 1024),
        name="pack",
    )(*arrays)


def pick(values, index):
    found = jnp.int32(values[0])
    for i, value in enumerate(values):
        if value != values[0]:
            found = jnp.where(index == i, jnp.int32(value), found)
    return found


def update_kernel(quarters, slot_ref, *refs):
    step_refs, refs = refs[:quarters], refs[quarters:]
    modulation, projection, output, expand, shrink = refs[:5]
    out_modulation, out_projection, out_output, out_expand, out_shrink = refs[5:10]
    quarter = pl.program_id(0)
    rows = step_refs[0].shape[0]
    ratio = LEARN_RATE * (FF / D) ** 0.5
    for which, steps in enumerate(step_refs):

        @pl.when(slot_ref[quarter] == which)
        def _(steps=steps):
            at = 3 * FF
            for k in range(2):
                step = steps[:, k * FF : (k + 1) * FF].astype(F32)
                out_expand[k] = expand[k] - ratio * step
            out_shrink[...] = shrink[...] - LEARN_RATE * steps[:, 2 * FF : at].astype(F32)
            for master, out, count in (
                (modulation, out_modulation, 6),
                (projection, out_projection, 3),
            ):
                for k in range(count):
                    out[k] = master[k] - LEARN_RATE * steps[:, at : at + D].astype(F32)
                    at += D
            out_output[...] = output[...] - LEARN_RATE * steps[:, at : at + D].astype(F32)


def update(slots, steps, masters):
    quarters = len(steps)
    rows = steps[0].shape[0]
    third = lambda a: pl.BlockSpec((a.shape[0], rows, a.shape[2]), lambda q: (0, q, 0))
    masters = (*masters[:4], masters[4].T)
    modulation, projection, output, expand, shrink = masters
    specs = [
        third(modulation),
        third(projection),
        pl.BlockSpec((rows, D), lambda q: (q, 0)),
        third(expand),
        pl.BlockSpec((rows, FF), lambda q: (q, 0)),
    ]
    updated = pl.pallas_call(
        functools.partial(update_kernel, quarters),
        grid=(quarters,),
        out_shape=tuple(jax.ShapeDtypeStruct(a.shape, F32) for a in masters),
        in_specs=[pl.BlockSpec(memory_space=pltpu.SMEM)] + [whole(a) for a in steps] + specs,
        out_specs=tuple(specs),
        cost_estimate=pl.CostEstimate(flops=0, bytes_accessed=14_000_000, transcendentals=0),
        compiler_params=pltpu.CompilerParams(vmem_limit_bytes=24 * 1024 * 1024),
        name="update",
    )(
        jnp.stack(slots).astype(jnp.int32),
        *steps,
        *[pltpu.with_memory_space_constraint(a, pltpu.HBM) for a in masters],
    )
    return (*updated[:4], updated[4].T)


def every(*sizes):
    return list(itertools.product(*[range(size) for size in sizes]))


class Plain:
    images = ("dp", "fsdp")
    rows = "fsdp"
    wide_parts = 1

    def __init__(self, mesh):
        self.mesh = mesh
        self.row_shards = mesh.shape["fsdp"]
        self.owners = mesh.shape["fsdp"]
        self.wide_slots = [(i, 0) for i in range(3)]
        self.wide_slots += [None] * (self.owners - 3)
        self.slots = [None] * 3 + list(range(10))
        self.slots += [None] * (self.owners - ITEMS)

    def row_index(self):
        return lax.axis_index("fsdp")

    def group_index(self):
        return lax.axis_index("dp")

    def owner_index(self):
        return lax.axis_index("fsdp")

    def gather_weights(self, first, second, modulate, attend):
        full = [lax.all_gather(chunk, "fsdp", axis=0, tiled=True) for chunk in (first, second)]
        first, second = [jnp.split(chunk, 2, axis=1) for chunk in full]
        modulation = modulate[1](modulate[0]())
        return first, second, modulation, attend(first, modulation)

    def to_group(self, value):
        return lax.all_to_all(value, "fsdp", split_axis=0, concat_axis=0, tiled=True)

    def halves(self):
        return jnp.int32(0)

    def begin(self, mine, send):
        k, n, rows, cols = mine.shape
        return (jnp.stack([mine, send], axis=2).reshape(k, 2 * n * rows, cols),)

    def step(self, state, axis, start=0, count=None):
        return (state[0][start : start + (count or state[0].shape[0])],)

    def last(self, *states):
        value = jnp.concatenate([state[0] for state in states], axis=0)
        shard = lax.psum_scatter(value, "fsdp", scatter_dimension=1, tiled=True)
        return lax.psum(shard.astype(F32), "dp")

    def own_rows(self, shard, dim=-2):
        return shard

    def complete_begin(self, piece):
        return piece

    def complete_end(self, piece):
        return piece

    def quarters(self, piece):
        return [jnp.int32(0)], [piece]

    def to_owners(self, pieces):
        got = lax.all_to_all(pieces, "fsdp", split_axis=0, concat_axis=0, tiled=True)
        return got.reshape(-1, got.shape[2])

    def wide_slots_of(self, feeds):
        return slots_of(
            [[] if slot is None else feeds[slot[0]] for slot in self.wide_slots],
            self.owners,
            FF,
            jnp.int32(0),
        )

    def wide_halves(self, got):
        return got

    def wide_whole(self, got):
        return jnp.stack(jnp.split(got, 2, axis=1))

    def square_slots(self, feeds, rows):
        return (
            slots_of(
                [[] if slot is None else feeds[slot] for slot in self.slots],
                self.owners,
                D,
                self.group_index(),
            ),
            rows,
        )

    def square_to_owners(self, slots, beside):
        pieces, rows = slots
        rows = lax.all_gather(rows, ("dp", "fsdp"), axis=0, tiled=True)
        return self.to_owners(pieces), rows, beside

    def to_rows(self, whole):
        blocks = whole.reshape(self.row_shards, -1, whole.shape[1])
        return lax.all_to_all(blocks, "fsdp", split_axis=0, concat_axis=0, tiled=True)


class Torus:
    images = ("x", "c", "z", "y")
    rows = ("z", "y")
    chips = ("x", "z", "y")
    wide_parts = 2

    def __init__(self, mesh):
        self.mesh = Mesh(mesh.devices.reshape(2, 2, 4, 2), ("x", "c", "z", "y"))
        self.row_shards = 8
        self.owners = 16
        wide_places = [(1, 0), (2, 1), (1, 1)]
        self.wide_slots = [None] * 16
        self.slots = [None] * 16
        for item, (z, y) in enumerate(wide_places):
            for part in range(2):
                self.wide_slots[(part * 4 + z) * 2 + y] = (item, part)
        free = [i for i in range(16) if self.wide_slots[i] is None]
        for item, slot in enumerate(free):
            self.slots[slot] = item

    def row_index(self):
        return lax.axis_index("z") * 2 + lax.axis_index("y")

    def group_index(self):
        return lax.axis_index("x") * 2 + lax.axis_index("c")

    def owner_index(self):
        return (lax.axis_index("x") * 4 + lax.axis_index("z")) * 2 + lax.axis_index("y")

    def swap(self, value, axis):
        return lax.ppermute(value, axis, [(0, 1), (1, 0)])

    def shift(self, value, by):
        return lax.ppermute(value, "z", [(i, (i + by) % 4) for i in range(4)])

    def exchange(self, value, axis):
        here = lax.axis_index(axis)
        return place([value, self.swap(value, axis)], [here, 1 - here])

    def spread_z(self, value):
        z = lax.axis_index("z")
        ring = [value] + [self.shift(value, by) for by in range(1, 4)]
        return place(ring, [(z - by) % 4 for by in range(4)])

    def gather_weights(self, first, second, modulate, attend):
        x, y, z, c = [lax.axis_index(axis) for axis in "xyzc"]
        slots = [(z - by) % 4 for by in range(4)]

        def ring_of(chunk, *others):
            piece = self.own_rows(chunk)
            if others:
                piece = tie(piece, *others)
            return [piece] + [self.shift(piece, by) for by in range(1, 4)]

        def one_hop(left, right):
            left_other, right_other = self.swap(left, "y"), self.swap(right, "x")
            left = place([left, left_other], [y, 1 - y])
            right = place([right, right_other], [x, 1 - x])
            return left, right

        def other_hop(left, right):
            left, right = meet(left, right)
            left_other, right_other = meet(self.swap(left, "x"), self.swap(right, "y"))
            left = place([left, left_other], [x, 1 - x])
            right = place([right, right_other], [y, 1 - y])
            return left, right

        def by_core(left, right):
            others = self.swap(left, "c"), self.swap(right, "c")
            pair = []
            for half, other, order in ((left, others[0], (2, 1, 0)), (right, others[1], (2, 0, 1))):

                def moves(slot, order=order):
                    found = []
                    for part in range(2):
                        for at in every(2, 2, 4):
                            found.append((part, at, (*[at[i] for i in order], slot[part])))
                    return found

                pair.append(place([half, other], [c, 1 - c], (4, 2, 2, 2), moves).reshape(D, -1))
            return pair

        group = modulate[0]()
        left, right = place_halves(ring_of(first), slots)
        left, right, group = meet(left, right, group)
        ring = ring_of(second, left, right)
        left, right = one_hop(left, right)
        left, right, ring[0], ring[1], ring[3] = meet(left, right, ring[0], ring[1], ring[3])
        left, right = other_hop(left, right)
        modulation = modulate[1](group)
        left, right, ring[2] = meet(left, right, ring[2])
        second_left, second_right = place_halves(ring, slots)
        others = self.swap(second_left, "y"), self.swap(second_right, "x")
        done = by_core(left, right)
        done, others, modulation = meet(done, others, modulation)
        left = place([second_left, others[0]], [y, 1 - y])
        right = place([second_right, others[1]], [x, 1 - x])
        left, right = meet(left, right)
        others = self.swap(left, "x"), self.swap(right, "y")
        done, left, right = meet(done, left, right)
        results = attend(done, modulation)
        left_other, right_other, results = meet(*others, results)
        left = place([left, left_other], [x, 1 - x])
        right = place([right, right_other], [y, 1 - y])
        return done, by_core(left, right), modulation, results

    def to_group(self, value):
        return lax.all_to_all(value, ("z", "y"), split_axis=0, concat_axis=0, tiled=True)

    def halves(self):
        return lax.axis_index("c")

    def begin(self, mine, send):
        return (mine, self.swap(send, "c"))

    def step(self, state, axis, start=0, count=None):
        mine, other = state
        parts = mine.shape[1]
        view = (4, 2) if (parts, axis) == (16, "y") else (parts // 2, 1)
        keep, send = fold(
            mine, other, lax.axis_index(axis), view, start, count or mine.shape[0]
        )
        return (keep, self.swap(send, axis))

    def last(self, *states):
        keep, *sends = fold_last(states, lax.axis_index("z"))
        got = [self.shift(send, by) for by, send in enumerate(sends, 1)]
        total = keep
        for part in got:
            total = total + part.astype(F32)
        return total

    def own_rows(self, shard, dim=-2):
        return lax.dynamic_slice_in_dim(
            shard, self.group_index() * (D // 32), D // 32, dim % shard.ndim
        )

    def quarters(self, piece):
        x, c = lax.axis_index("x"), lax.axis_index("c")
        by_x = self.swap(piece, "x")
        by_c = self.swap(piece, "c")
        by_both = self.swap(by_x, "c")
        slots = []
        for at_x, at_c in every(2, 2):
            slots.append(jnp.where(at_x == x, 0, 1) + jnp.where(at_c == c, 0, 2))
        return slots, [piece, by_x, by_c, by_both]

    def complete_begin(self, piece):
        return piece, self.swap(piece, "x")

    def complete_end(self, pair):
        x, c = lax.axis_index("x"), lax.axis_index("c")
        value = place(list(pair), [x, 1 - x])
        moves = lambda slot: [(part, (x,), (x, slot[part])) for part in range(2) for x in range(2)]
        value = place([value, self.swap(value, "c")], [c, 1 - c], (2, 2), moves)
        return value.reshape(D // 8, -1)

    def to_owners(self, pieces):
        return lax.all_to_all(pieces, self.chips, split_axis=0, concat_axis=0, tiled=True)

    def wide_slots_of(self, feeds):
        halved = []
        for slot in self.wide_slots:
            halved.append([] if slot is None else [feeds[slot[0]][slot[1]]])
        return slots_of(halved, self.owners, FF // 2, self.group_index())

    def wide_halves(self, got):
        return got, self.swap(got, "x")

    def wide_whole(self, got):
        half = FF // 2
        x, c = lax.axis_index("x"), lax.axis_index("c")
        both = place(list(got), [x, 1 - x])
        both = both.reshape(2, 2, 4, 2, D // 32, half)

        def moves(slot):
            return [
                (part, (p, x, z, y), (p, z, y, x, slot[part]))
                for part in range(2)
                for p, x, z, y in every(2, 2, 4, 2)
            ]

        whole = place([both, self.swap(both, "c")], [c, 1 - c], (2, 4, 2, 2, 2), moves)
        return whole.reshape(2, D, half)

    def square_slots(self, feeds, rows):
        return slots_of(
            [[] if slot is None else feeds[slot] for slot in self.slots],
            self.owners,
            D,
            self.group_index(),
            rows.reshape(-1, D),
        )

    def square_to_owners(self, slots, beside):
        quarter = D // 32
        got = self.to_owners(slots)
        got, beside = meet(got, beside)
        other = self.swap(got, "c")
        more = got.shape[1] - quarter

        def body(c_ref, mine_ref, other_ref, whole_ref, rows_ref):
            c = c_ref[0]
            for ref, at in ((mine_ref, c), (other_ref, 1 - c)):
                for chip, (x, z, y) in enumerate(every(2, 4, 2)):
                    whole_ref[z, y, x, at] = ref[chip, :quarter]
                    rows_ref[at, chip] = ref[chip, quarter:]

        vmem = pl.BlockSpec(memory_space=pltpu.VMEM)
        square, gathered = pl.pallas_call(
            body,
            out_shape=(
                jax.ShapeDtypeStruct((4, 2, 2, 2, quarter, D), BF16),
                jax.ShapeDtypeStruct((2, 16, more, D), BF16),
            ),
            in_specs=[pl.BlockSpec(memory_space=pltpu.SMEM), vmem, vmem],
            out_specs=(vmem, vmem),
            cost_estimate=pl.CostEstimate(
                flops=0, bytes_accessed=8 * got.size, transcendentals=0
            ),
            compiler_params=pltpu.CompilerParams(vmem_limit_bytes=24 * 1024 * 1024),
            name="place_square",
        )(lax.axis_index("c").reshape(1).astype(jnp.int32), got, other)
        return square.reshape(D, D), gathered.reshape(-1, 8, D), beside

    def to_rows(self, whole):
        cols = whole.shape[1]
        blocks = whole.reshape(4, 2, 2, 2, D // 32, cols)
        blocks = lax.dynamic_index_in_dim(blocks, lax.axis_index("c"), 3, keepdims=False)
        blocks = blocks.transpose(2, 0, 1, 3, 4).reshape(16, D // 32, cols)
        return lax.all_to_all(blocks, self.chips, split_axis=0, concat_axis=0, tiled=True)


def lanes(shape, dim):
    return lax.broadcasted_iota(jnp.int32, shape, dim)


def norm_of(values):
    centred = values - jnp.mean(values, axis=-1, keepdims=True)
    inverse = lax.rsqrt(jnp.mean(centred * centred, axis=-1, keepdims=True) + NORM_EPS)
    return centred * inverse, inverse


def norm_back(incoming, normed, inverse):
    return inverse * (
        incoming
        - jnp.mean(incoming, axis=-1, keepdims=True)
        - normed * jnp.mean(incoming * normed, axis=-1, keepdims=True)
    )


def rotate_pair(value):
    first = lanes(value.shape, 1) % 32 < 16
    return jnp.where(first, -pltpu.roll(value, 112, 1), pltpu.roll(value, 16, 1))


def two_heads(value):
    low = lanes(value.shape, 1) < HDIM
    zero = jnp.zeros_like(value)
    return jnp.where(low, value, zero), jnp.where(low, zero, value)


def pair_at(pair):
    return slice(pair * 2 * HDIM, (pair + 1) * 2 * HDIM)


def attention_forward_kernel(
    length_ref,
    input_ref,
    cotangent_ref,
    modulation_ref,
    cosine_ref,
    sine_ref,
    query_key_ref,
    value_output_ref,
    first_ref,
    query_ref,
    key_ref,
    value_ref,
    probs_ref,
    attended_ref,
    attention_ref,
    middle_ref,
    second_ref,
    branch_ref,
):
    length = length_ref[pl.program_id(0)]
    row = lambda which: modulation_ref[0, which : which + 1, :]
    stream = input_ref[0].astype(F32)
    positions = stream.shape[0]
    normed, _ = norm_of(stream)
    first = (normed * (1.0 + row(1)) + row(0)).astype(BF16)
    first_ref[0] = first
    inside = lanes((positions, D), 0) < length
    upstream = jnp.where(inside, cotangent_ref[0].astype(F32), 0.0)
    branch_ref[0] = (row(5) * upstream).astype(BF16)
    value_ref[0] = dot(first, value_output_ref[:, :D]).astype(BF16)
    cosine, sine = cosine_ref[0], sine_ref[0]
    keep = lanes((positions, positions), 1) < length
    for pair in range(HEADS // 2):
        at = pair_at(pair)
        query = dot(first, query_key_ref[:, at])
        key = dot(first, query_key_ref[:, D + pair * 128 : D + (pair + 1) * 128])
        query = (query * cosine + rotate_pair(query) * sine).astype(BF16)
        key = (key * cosine + rotate_pair(key) * sine).astype(BF16)
        query_ref[0, :, at] = query
        key_ref[0, :, at] = key
        low = []
        for head, masked in enumerate(two_heads(query)):
            scores = dot(masked, key, NT) * HDIM ** (-0.5)
            scores = jnp.where(keep, scores, -1000000000.0)
            exponent = jnp.exp(scores - jnp.max(scores, axis=-1, keepdims=True))
            probs = exponent * (1.0 / jnp.sum(exponent, axis=-1, keepdims=True))
            probs_ref[0, 2 * pair + head] = probs
            low.append(probs.astype(BF16))
        values = two_heads(value_ref[0, :, at])
        attended_ref[0, :, at] = dot(
            jnp.concatenate(low, axis=1), jnp.concatenate(values, axis=0)
        ).astype(BF16)
    attention = dot(attended_ref[0], value_output_ref[:, D:])
    attention_ref[0] = attention
    middle = stream + row(2) * attention
    middle_ref[0] = middle
    normed, _ = norm_of(middle)
    second_ref[0] = (normed * (1.0 + row(4)) + row(3)).astype(BF16)


def split_rows(value, scratch, here, keep_ref, send_ref, which, cols):
    scratch[...] = value
    rows = keep_ref.shape[2]
    for i in range(keep_ref.shape[1]):
        for ref, at in ((keep_ref, here), (send_ref, 1 - here)):
            start = pl.multiple_of((2 * i + at) * rows, 8)
            ref[which, i, :, cols] = scratch[pl.ds(start, rows), :].astype(BF16)


def feed_forward_kernel(
    here_ref,
    second_ref,
    branch_ref,
    gate_ref,
    up_ref,
    down_ref,
    out_ref,
    back_ref,
    keep_ref,
    send_ref,
    second_t,
    branch_t,
    rows,
):
    step = pl.program_id(0)

    @pl.when(step == 0)
    def _():
        second_t[...] = second_ref[...].T
        branch_t[...] = branch_ref[...].T
        out_ref[...] = jnp.zeros_like(out_ref)
        back_ref[...] = jnp.zeros_like(back_ref)

    gate, up, down = gate_ref[...], up_ref[...], down_ref[...]
    gate_pre = dot(second_ref[...], gate)
    up_pre = dot(second_ref[...], up)
    sigmoid = 1.0 / (1.0 + jnp.exp(-gate_pre))
    swish = gate_pre * sigmoid
    hidden = (swish * up_pre).astype(BF16)
    out_ref[...] += dot(hidden, down, NT)
    grad_hidden = dot(branch_ref[...], down)
    grad_gate = (grad_hidden * up_pre * sigmoid * (1.0 + gate_pre * (1.0 - sigmoid))).astype(BF16)
    grad_up = (grad_hidden * swish).astype(BF16)
    back_ref[...] += dot(grad_gate, gate, NT) + dot(grad_up, up, NT)
    everything = slice(None)
    products = ((second_t, grad_gate), (second_t, grad_up), (branch_t, hidden))
    for which, (left, right) in enumerate(products):
        split_rows(
            dot(left[...], right), rows, here_ref[0], keep_ref, send_ref, which, everything
        )


def attention_backward_kernel(
    length_ref,
    branch_left_ref,
    branch_right_ref,
    second_left_ref,
    second_right_ref,
    middle_ref,
    cotangent_ref,
    modulation_ref,
    attention_ref,
    value_output_ref,
    query_ref,
    key_ref,
    value_ref,
    probs_ref,
    cosine_ref,
    sine_ref,
    output_ref,
    stream_ref,
    grads_ref,
    sums_ref,
    attended_grad,
):
    length = length_ref[pl.program_id(0)]
    row = lambda which: modulation_ref[0, which : which + 1, :]
    middle = middle_ref[0]
    positions = middle.shape[0]
    inside = lanes((positions, D), 0) < length
    upstream = jnp.where(inside, cotangent_ref[0].astype(F32), 0.0)
    branch = branch_left_ref[0] + branch_right_ref[0]
    output_ref[0] = (middle + row(5) * branch).astype(BF16)
    total = lambda value: jnp.sum(value, axis=0, keepdims=True)
    gate_two = total(upstream * branch)
    second = second_left_ref[0] + second_right_ref[0]
    normed, inverse = norm_of(middle)
    scale_two = total(second * normed)
    shift_two = total(second)
    stream = upstream + norm_back(second * (1.0 + row(4)), normed, inverse)
    stream_ref[0] = stream
    gate_one = total(stream * attention_ref[0])
    blank = jnp.zeros_like(gate_one)
    sums_ref[0] = jnp.concatenate(
        [blank, blank, gate_one, shift_two, scale_two, gate_two, blank, blank], axis=0
    )
    grad_attention = (row(2) * stream).astype(BF16)
    grads_ref[3, 0] = grad_attention
    attended_grad[...] = dot(grad_attention, value_output_ref[:, D:], NT).astype(BF16)
    cosine, sine = cosine_ref[0], sine_ref[0]
    for pair in range(HEADS // 2):
        at = pair_at(pair)
        query, key, value = query_ref[0, :, at], key_ref[0, :, at], value_ref[0, :, at]
        attended = two_heads(attended_grad[:, at])
        low, scores = [], []
        for head in range(2):
            probs = probs_ref[0, 2 * pair + head]
            grad_probs = dot(attended[head], value, NT)
            inner = jnp.sum(grad_probs * probs, axis=-1, keepdims=True)
            scores.append((probs * (grad_probs - inner)).astype(BF16))
            low.append(probs.astype(BF16))
        grads_ref[2, 0, :, at] = dot(
            jnp.concatenate(low, axis=0), jnp.concatenate(attended, axis=0), TN
        ).astype(BF16)
        grad_query = dot(
            jnp.concatenate(scores, axis=1), jnp.concatenate(two_heads(key), axis=0)
        ) * HDIM ** (-0.5)
        grad_key = dot(
            jnp.concatenate(scores, axis=0), jnp.concatenate(two_heads(query), axis=0), TN
        ) * HDIM ** (-0.5)
        grads_ref[0, 0, :, at] = (grad_query * cosine - rotate_pair(grad_query * sine)).astype(BF16)
        grads_ref[1, 0, :, at] = (grad_key * cosine - rotate_pair(grad_key * sine)).astype(BF16)


def projection_backward_kernel(
    here_ref,
    grads_in_ref,
    first_ref,
    attended_ref,
    input_ref,
    modulation_ref,
    stream_ref,
    sums_ref,
    active_ref,
    query_key_ref,
    value_output_ref,
    keep_ref,
    send_ref,
    input_grad_ref,
    modulation_grad_ref,
    first_t,
    first_grad,
    rows,
):
    images, positions = input_ref.shape[:2]
    tokens = images * positions
    flat = lambda ref: ref[...].reshape(tokens, D)
    step = pl.program_id(0)

    def product(grads):
        split_rows(dot(first_t[...], grads), rows, here_ref[0], keep_ref, send_ref, 0, slice(None))

    @pl.when(step == 0)
    def _():
        first_t[...] = flat(first_ref).T
        grads = grads_in_ref[0].reshape(tokens, D)
        product(grads)
        first_grad[...] = dot(grads, query_key_ref[:, :D], NT)

    @pl.when(step == 1)
    def _():
        grads = grads_in_ref[0].reshape(tokens, D)
        product(grads)
        first_grad[...] += dot(grads, query_key_ref[:, D:], NT)

    @pl.when(step == 2)
    def _():
        grads = grads_in_ref[0].reshape(tokens, D)
        product(grads)
        first_grad[...] += dot(grads, value_output_ref[:, :D], NT)

    @pl.when(step == 3)
    def _():
        first_t[...] = flat(attended_ref).T
        product(grads_in_ref[0].reshape(tokens, D))
        for image in range(images):
            at = slice(image * positions, (image + 1) * positions)
            normed, inverse = norm_of(input_ref[image].astype(F32))
            first = first_grad[at, :]
            scale_one = jnp.sum(first * normed, axis=0, keepdims=True)
            shift_one = jnp.sum(first, axis=0, keepdims=True)
            scaled = first * (1.0 + modulation_ref[image, 1:2, :])
            input_grad_ref[image] = stream_ref[image] + norm_back(scaled, normed, inverse)
            modulation_grad_ref[image] = jnp.concatenate(
                [
                    shift_one,
                    scale_one,
                    sums_ref[image, 2:6, :],
                    active_ref[image : image + 1, :].astype(F32),
                    jnp.zeros_like(shift_one),
                ],
                axis=0,
            ).astype(BF16)


BIG_VMEM = 58 * 1024 * 1024


def whole(array):
    return pl.BlockSpec(array.shape, lambda *_: (0,) * array.ndim)


def by_image(array):
    return pl.BlockSpec((1, *array.shape[1:]), lambda b: (b,) + (0,) * (array.ndim - 1))


def call(body, grid, ins, in_specs, outs, out_specs, scratch, flops, name):
    size = sum(a.size * a.dtype.itemsize for a in (*ins, *outs))
    return pl.pallas_call(
        body,
        grid=grid,
        out_shape=outs,
        in_specs=in_specs,
        out_specs=out_specs,
        scratch_shapes=scratch,
        compiler_params=pltpu.CompilerParams(vmem_limit_bytes=BIG_VMEM),
        cost_estimate=pl.CostEstimate(flops=flops, bytes_accessed=size, transcendentals=0),
        name=name,
    )(*ins)


def attention_forward(lengths, inputs, cotangent, modulation, cosine, sine, query_key, value_output):
    images, positions, _ = inputs.shape
    ins = (lengths, inputs, cotangent, modulation, cosine, sine, query_key, value_output)
    in_specs = [pl.BlockSpec(memory_space=pltpu.SMEM)]
    in_specs += [by_image(a) for a in ins[1:6]] + [whole(a) for a in ins[6:]]
    token = lambda dtype: jax.ShapeDtypeStruct((images, positions, D), dtype)
    outs = (
        token(BF16),
        token(BF16),
        token(BF16),
        token(BF16),
        jax.ShapeDtypeStruct((images, HEADS, positions, positions), F32),
        token(BF16),
        token(F32),
        token(F32),
        token(BF16),
        token(BF16),
    )
    flops = 2 * images * positions * D * (4 * D + 2 * positions)
    return call(
        attention_forward_kernel,
        (images,),
        ins,
        in_specs,
        outs,
        [by_image(a) for a in outs],
        [],
        flops,
        "attention_forward",
    )


def feed_forward(here, second, branch, weight):
    tokens = second.shape[0]
    units = weight.shape[1] // 3
    tile = 256
    steps = units // tile
    ins = (here.reshape(1).astype(jnp.int32), second, branch, weight, weight, weight)
    in_specs = [pl.BlockSpec(memory_space=pltpu.SMEM), whole(second), whole(branch)] + [
        pl.BlockSpec((D, tile), lambda t, which=which: (0, which * steps + t)) for which in range(3)
    ]
    outs = (
        jax.ShapeDtypeStruct((tokens, D), F32),
        jax.ShapeDtypeStruct((tokens, D), F32),
        jax.ShapeDtypeStruct((3, D // 48, 24, units), BF16),
        jax.ShapeDtypeStruct((3, D // 48, 24, units), BF16),
    )
    out_specs = [whole(outs[0]), whole(outs[1])]
    out_specs += [pl.BlockSpec((3, D // 48, 24, tile), lambda t: (0, 0, 0, t))] * 2
    scratch = [pltpu.VMEM((D, tokens), BF16), pltpu.VMEM((D, tokens), BF16), pltpu.VMEM((D, tile), F32)]
    flops = 2 * 9 * tokens * D * units
    return call(
        feed_forward_kernel, (steps,), ins, in_specs, outs, out_specs, scratch, flops, "feed_forward"
    )


def attention_backward(lengths, *ins):
    images, positions, _ = ins[0].shape
    shared = 8
    in_specs = [pl.BlockSpec(memory_space=pltpu.SMEM)]
    in_specs += [whole(a) if i == shared else by_image(a) for i, a in enumerate(ins)]
    outs = (
        jax.ShapeDtypeStruct((images, positions, D), BF16),
        jax.ShapeDtypeStruct((images, positions, D), F32),
        jax.ShapeDtypeStruct((4, images, positions, D), BF16),
        jax.ShapeDtypeStruct((images, 8, D), F32),
    )
    out_specs = [
        by_image(outs[0]),
        by_image(outs[1]),
        pl.BlockSpec((4, 1, positions, D), lambda b: (0, b, 0, 0)),
        by_image(outs[3]),
    ]
    flops = 2 * images * positions * D * (D + 5 * positions)
    return call(
        attention_backward_kernel,
        (images,),
        (lengths, *ins),
        in_specs,
        outs,
        out_specs,
        [pltpu.VMEM((positions, D), BF16)],
        flops,
        "attention_backward",
    )


def projection_backward(here, *ins):
    _, images, positions, _ = ins[0].shape
    tokens = images * positions
    in_specs = [pl.BlockSpec(memory_space=pltpu.SMEM)]
    in_specs += [pl.BlockSpec((1, images, positions, D), lambda k: (k, 0, 0, 0))]
    in_specs += [whole(a) for a in ins[1:]]
    ins = (here.reshape(1).astype(jnp.int32), *ins)
    outs = (
        jax.ShapeDtypeStruct((4, D // 48, 24, D), BF16),
        jax.ShapeDtypeStruct((4, D // 48, 24, D), BF16),
        jax.ShapeDtypeStruct((images, positions, D), F32),
        jax.ShapeDtypeStruct((images, 8, D), BF16),
    )
    out_specs = [pl.BlockSpec((1, D // 48, 24, D), lambda k: (k, 0, 0, 0))] * 2
    out_specs += [whole(outs[2]), whole(outs[3])]
    scratch = [pltpu.VMEM((D, tokens), BF16), pltpu.VMEM((tokens, D), F32), pltpu.VMEM((D, D), F32)]
    return call(
        projection_backward_kernel,
        (4,),
        ins,
        in_specs,
        outs,
        out_specs,
        scratch,
        2 * 7 * tokens * D * D,
        "projection_backward",
    )


def swish_value(values):
    return values / (1.0 + jnp.exp(-values))


def rope_tables(extents, positions):
    quarter = HDIM // 4
    places = jnp.arange(positions, dtype=jnp.int32)
    widths = extents[:, 1]
    row_place = (places[None, :] // widths[:, None]).astype(F32)
    col_place = (places[None, :] % widths[:, None]).astype(F32)
    lane = jnp.arange(2 * HDIM) % HDIM
    frequency = 10000.0 ** (-(lane % quarter).astype(F32) / quarter)
    by_row = lane < 2 * quarter
    angle = jnp.where(by_row, row_place[:, :, None], col_place[:, :, None]) * frequency
    return jnp.cos(angle), jnp.sin(angle)


def local(
    comm,
    inputs,
    cotangent,
    image_shape,
    time_bins,
    time_table,
    modulation_master,
    projection_master,
    output_master,
    expand_master,
    shrink_master,
    modulation_moment,
    projection_moment,
    output_moment,
    expand_moment,
    shrink_moment,
):
    masters = (modulation_master, projection_master, output_master, expand_master, shrink_master)
    moments = (modulation_moment, projection_moment, output_moment, expand_moment, shrink_moment)
    images, positions, features = inputs.shape
    tokens = images * positions
    rows = modulation_master.shape[1]
    row_index = comm.row_index()

    half = FF // 2
    shrink_low = shrink_master.astype(BF16).T
    packed_attention = jnp.concatenate(
        [projection_master[i].astype(BF16) for i in range(3)] + [output_master.astype(BF16)], axis=1
    )
    packed_units = jnp.concatenate(
        [
            part
            for cols in (slice(None, half), slice(half, None))
            for part in (
                expand_master[0, :, cols].astype(BF16),
                expand_master[1, :, cols].astype(BF16),
                shrink_low[:, cols],
            )
        ],
        axis=1,
    )
    selector = (
        time_bins[:, None] == jnp.arange(time_table.shape[0], dtype=jnp.int32)[None, :]
    ).astype(F32)
    active = swish_value(jnp.dot(selector, time_table, precision=HIGHEST)).astype(BF16)

    def group_rows():
        return comm.to_group(active.reshape(images, comm.row_shards, rows).transpose(1, 0, 2))

    def modulation_of(group):
        partial = jnp.einsum(
            "bd,kde->bke",
            group.reshape(-1, rows),
            modulation_master.astype(BF16),
            preferred_element_type=F32,
        )
        return jnp.sum(
            comm.to_group(partial.reshape(comm.row_shards, images, 6, features)), axis=0
        )

    cosine, sine = rope_tables(image_shape, positions)
    lengths = image_shape[:, 0] * image_shape[:, 1]

    def attend(weights, modulation):
        return attention_forward(
            lengths, inputs, cotangent, modulation, cosine, sine, weights[0], weights[1]
        )

    first, second, modulation, results = comm.gather_weights(
        packed_attention, packed_units, (group_rows, modulation_of), attend
    )
    query_key_weight, value_output_weight = first
    left_weight, right_weight = second
    (first_input, query, key, value, probs, attended, attention, middle, second_input, grad_branch) = (
        results
    )
    second_flat = second_input.reshape(tokens, D)
    branch_flat = grad_branch.reshape(tokens, D)
    shaped = lambda v: v.reshape(images, positions, D)
    here = comm.halves()
    branch_left, back_left, *grads = feed_forward(here, second_flat, branch_flat, left_weight)
    left_sum = comm.begin(*grads)
    second_flat = tie(second_flat, back_left)
    branch_right, back_right, *grads = feed_forward(here, second_flat, branch_flat, right_weight)
    back_right, left_sum, grads = meet(back_right, left_sum, grads)
    left_sum = comm.step(left_sum, "x", 0, 2), comm.step(left_sum, "y", 2, 1)
    right_sum = comm.begin(*grads)
    block_output, grad_stream, grads, sums = attention_backward(
        lengths,
        shaped(branch_left),
        shaped(branch_right),
        shaped(back_left),
        shaped(back_right),
        middle,
        cotangent,
        modulation,
        attention,
        value_output_weight,
        query,
        key,
        value,
        probs,
        cosine,
        sine,
    )
    left_sum, right_sum, grads = meet(left_sum, right_sum, grads)
    left_sum = comm.step(left_sum[0], "y"), comm.step(left_sum[1], "x")
    right_sum = comm.step(right_sum, "x", 0, 2), comm.step(right_sum, "y", 2, 1)
    *grads, input_gradient, grad_modulation = projection_backward(
        here,
        grads,
        first_input,
        attended,
        inputs,
        modulation,
        grad_stream,
        sums,
        active,
        query_key_weight,
        value_output_weight,
    )
    left_sum, right_sum, grads, grad_modulation = meet(left_sum, right_sum, grads, grad_modulation)
    attention_sum = comm.begin(*grads)
    right_sum = comm.step(right_sum[0], "y"), comm.step(right_sum[1], "x")
    left_piece = comm.last(*left_sum)
    attention_sum, right_sum, left_piece = meet(attention_sum, right_sum, left_piece)
    right_piece = comm.last(*right_sum)
    first_sum = comm.step(attention_sum, "x", 0, 2)
    second_sum = comm.step(attention_sum, "y", 2, 2)
    first_sum, second_sum, right_piece = meet(first_sum, second_sum, right_piece)

    owner = comm.owner_index()
    own_expand, own_shrink = expand_moment, shrink_moment.T
    wide_feed = [
        [
            (
                (piece, ((which,), 0, half)),
                (own_shrink, ((), side * half, half))
                if which == 2
                else (own_expand, ((which,), side * half, half)),
            )
            for side, piece in enumerate((left_piece, right_piece))
        ]
        for which in range(3)
    ]
    wide = comm.to_owners(comm.wide_slots_of(wide_feed))
    first_sum = comm.step(first_sum, "y")
    second_sum = comm.step(second_sum, "x")
    first_sum, second_sum, wide = meet(first_sum, second_sum, wide)
    wide = comm.wide_halves(wide)
    attention_piece, wide = meet(comm.last(first_sum, second_sum), wide)
    own_modulation, own_projection, own_output = modulation_moment, projection_moment, output_moment
    square_feed = [[(None, (own_modulation, ((k,), 0, D)))] for k in range(6)]
    for k in range(3):
        square_feed.append(
            [((attention_piece, ((k,), 0, D)), (own_projection, ((k,), 0, D)))]
        )
    square_feed.append([((attention_piece, ((3,), 0, D)), (own_output, ((), 0, D)))])
    slots = comm.square_slots(square_feed, grad_modulation)
    wide = comm.wide_whole(wide)
    active_wide = pick([0 if slot is None else 1 for slot in comm.wide_slots], owner)
    wide_done = newton_schulz(active_wide, wide)
    slots, left_piece, right_piece, attention_piece = meet(
        slots, left_piece, right_piece, attention_piece
    )
    pieces = [(left_piece, (i,), half) for i in range(3)]
    pieces += [(right_piece, (i,), half) for i in range(3)]
    pieces += [(attention_piece, (i,), D) for i in range(4)]
    totals_low = comm.complete_begin(pack(pieces))
    square, gathered, (wide_done, totals_low) = comm.square_to_owners(slots, (wide_done, totals_low))
    active_all = gathered[:, 6]
    item = pick([-1 if slot is None else slot for slot in comm.slots], owner)
    which = jnp.where((item >= 0) & (item < 6), item, 0)
    right = lax.dynamic_index_in_dim(gathered, which, 1, keepdims=False)
    right = jnp.where(item < 6, right, jnp.zeros_like(right))
    square_done = newton_schulz((item >= 0).astype(jnp.int32), square, active_all, right)
    size = FF // comm.wide_parts
    part = pick([0 if slot is None else slot[1] for slot in comm.wide_slots], owner)
    mine = lax.dynamic_slice_in_dim(wide_done, part * size, size, 1)
    mine = mine + jnp.pad(square_done, ((0, 0), (0, size - D)))
    back = comm.to_rows(mine)

    totals_low = comm.complete_end(totals_low).astype(F32)
    by_unit = [
        jnp.concatenate(
            [totals_low[:, (side * 3 + i) * half : (side * 3 + i + 1) * half] for side in range(2)],
            axis=1,
        )
        for i in range(3)
    ]
    steps = [
        (back, (comm.wide_slots.index((i, p)),), size) for i in range(3) for p in range(comm.wide_parts)
    ]
    steps += [(back, (comm.slots.index(i),), D) for i in range(10)]
    updated = update(*comm.quarters(pack(steps)), masters)
    active_rows = lax.dynamic_slice_in_dim(active_all, row_index * rows, rows, 1)
    modulation_total = jnp.einsum(
        "bd,bke->kde",
        active_rows,
        gathered[:, :6],
        preferred_element_type=F32,
    )
    after = 3 * FF
    totals = (
        modulation_total,
        jnp.stack([totals_low[:, after + i * D : after + (i + 1) * D] for i in range(3)]),
        totals_low[:, after + 3 * D :],
        jnp.stack(by_unit[:2]),
        by_unit[2].T,
    )
    states = tuple((MOMENTUM_DECAY * moment + total for moment, total in zip(moments, totals)))
    return (block_output, input_gradient, *totals, *updated, *states)


def solution(mesh):
    if mesh.shape["dp"] == 4 and mesh.shape["fsdp"] == 8:
        comm = Torus(mesh)
    else:
        comm = Plain(mesh)
    images, rows = comm.images, comm.rows
    by_row = (
        P(None, rows, None),
        P(None, rows, None),
        P(rows, None),
        P(None, rows, None),
        P(None, rows),
    )
    return jax.shard_map(
        functools.partial(local, comm),
        mesh=comm.mesh,
        in_specs=(
            P(images, None, None),
            P(images, None, None),
            P(images, None),
            P(images),
            P(),
            *by_row,
            *by_row,
        ),
        out_specs=(P(images, None, None), P(images, None, None), *by_row, *by_row, *by_row),
        check_vma=False,
    )
```

```python
import functools
import itertools

import jax
import jax.numpy as jnp
from jax import lax
from jax.experimental import pallas as pl
from jax.experimental.pallas import tpu as pltpu
from jax.sharding import Mesh, PartitionSpec as P

D = 768
HEADS = 12
HDIM = 64
FF = 2048
NS_ITERS = 5
NORM_EPS = 1e-06
FROBENIUS_EPS = 1e-07
COEFF_FIRST = 3.4445
COEFF_SECOND = -4.775
COEFF_THIRD = 2.0315
MOMENTUM_DECAY = 0.9
LEARN_RATE = 1.0
HIGHEST = lax.Precision.HIGHEST
BF16 = jnp.bfloat16
F32 = jnp.float32
ITEMS = 13
NT = (((1,), (1,)), ((), ()))
NN = (((1,), (0,)), ((), ()))
TN = (((0,), (0,)), ((), ()))


def dot(a, b, dims=NN):
    return lax.dot_general(a, b, dims, preferred_element_type=F32)


def newton_schulz_kernel(width, active_ref, feed_ref, left_ref, right_ref, out_ref, x, xb, gram, low, poly):
    tile = 256
    tiles = D // tile
    blocks = width // tile
    spans = [slice(i * tile, (i + 1) * tile) for i in range(tiles)]

    def diagonal(part, other):
        rows = lax.broadcasted_iota(jnp.int32, (tile, tile), 0)
        cols = lax.broadcasted_iota(jnp.int32, (tile, tile), 1)
        return jnp.where(rows == cols, part, other)

    def block(b):
        return pl.ds(pl.multiple_of(b * tile, tile), tile)

    @pl.when(active_ref[0] != 0)
    def _():
        def load(b, acc):
            if len(feed_ref.shape) == 3:
                per = feed_ref.shape[2] // tile
                v = feed_ref[b // per, :, block(lax.rem(b, per))].astype(F32)
            else:
                v = feed_ref[:, block(b)].astype(F32)
            if right_ref is not None:
                v = v + (1.0 + MOMENTUM_DECAY) * dot(left_ref[...], right_ref[:, block(b)], TN)
            x[:, block(b)] = v
            return acc + jnp.sum(v * v, axis=0, keepdims=True)

        total = lax.fori_loop(0, blocks, load, jnp.zeros((1, tile), F32))
        total = jnp.sum(total, keepdims=True)
        inverse = 1.0 / (jnp.sqrt(total) + FROBENIUS_EPS)

        def scale_block(b, carry):
            v = x[:, block(b)] * inverse
            x[:, block(b)] = v
            xb[:, block(b)] = v.astype(BF16)
            return carry

        lax.fori_loop(0, blocks, scale_block, 0)

        def iterate(step, carry):
            trace = jnp.zeros((1, tile), F32)
            for i in range(tiles):
                for j in range(i + 1):
                    part = dot(xb[spans[i], :], xb[spans[j], :], NT)
                    gram[spans[i], spans[j]] = part
                    if i == j:
                        trace = trace + jnp.sum(diagonal(part, 0.0), axis=0, keepdims=True)
                    else:
                        lower = part.astype(BF16)
                        low[spans[i], spans[j]] = lower
                        low[spans[j], spans[i]] = lower.T
            shift = jnp.sum(trace, keepdims=True) / D
            for i in range(tiles):
                part = gram[spans[i], spans[i]]
                part = diagonal(part - shift, part)
                gram[spans[i], spans[i]] = part
                low[spans[i], spans[i]] = part.astype(BF16)
            linear = COEFF_SECOND + 2.0 * COEFF_THIRD * shift
            level = COEFF_SECOND * shift + COEFF_THIRD * shift * shift
            trace = jnp.zeros((1, tile), F32)
            for i in range(tiles):
                for j in range(i + 1):
                    part = linear * gram[spans[i], spans[j]] + COEFF_THIRD * dot(
                        low[spans[i], :], low[spans[j], :], NT
                    )
                    if i == j:
                        gram[spans[i], spans[j]] = part
                        trace = trace + jnp.sum(diagonal(part, 0.0), axis=0, keepdims=True)
                    else:
                        lower = part.astype(BF16)
                        poly[spans[i], spans[j]] = lower
                        poly[spans[j], spans[i]] = lower.T
            mean = jnp.sum(trace, keepdims=True) / D
            for i in range(tiles):
                part = gram[spans[i], spans[i]]
                poly[spans[i], spans[i]] = diagonal(part - mean, part).astype(BF16)
            scale = COEFF_FIRST + level + mean

            size = width // 2 if width > 1024 else width
            for b in range(width // size):
                cols = slice(b * size, (b + 1) * size)
                new = scale * x[:, cols] + dot(poly[...], xb[:, cols])
                x[:, cols] = new
                xb[:, cols] = new.astype(BF16)
            return carry

        lax.fori_loop(0, NS_ITERS, iterate, 0)
        out_ref[...] = xb[...]

    @pl.when(active_ref[0] == 0)
    def _():
        out_ref[...] = jnp.zeros_like(out_ref)


def newton_schulz(active, feed, left=None, right=None):
    width = feed.size // D
    operands = [active.reshape(1).astype(jnp.int32), feed]
    if left is None:

        def body(active_ref, feed_ref, *rest):
            newton_schulz_kernel(width, active_ref, feed_ref, None, None, *rest)

    else:
        body = functools.partial(newton_schulz_kernel, width)
        operands += [left, right]
    vmem = pl.BlockSpec(memory_space=pltpu.VMEM)
    return pl.pallas_call(
        body,
        out_shape=jax.ShapeDtypeStruct((D, width), BF16),
        in_specs=[pl.BlockSpec(memory_space=pltpu.SMEM)] + [vmem] * (len(operands) - 1),
        out_specs=vmem,
        scratch_shapes=[
            pltpu.VMEM((D, width), F32),
            pltpu.VMEM((D, width), BF16),
            pltpu.VMEM((D, D), F32),
            pltpu.VMEM((D, D), BF16),
            pltpu.VMEM((D, D), BF16),
        ],
        compiler_params=pltpu.CompilerParams(vmem_limit_bytes=40 * 1024 * 1024),
        cost_estimate=pl.CostEstimate(
            flops=NS_ITERS * 4 * D * D * (width + D), bytes_accessed=4 * D * width, transcendentals=0
        ),
        name="newton_schulz",
    )(*operands)


def tie(value, *others):
    return lax.optimization_barrier((value, *others))[0]


def meet(*values):
    flat, tree = jax.tree.flatten(values)
    return jax.tree.unflatten(tree, lax.optimization_barrier(tuple(flat)))


def fold(mine, other, here, view, start, count):
    before, after = view
    rows, cols = mine.shape[-2:]
    shape = (mine.shape[0], before, 2, after, rows, cols)
    block = pl.BlockSpec((1, *shape[1:]), lambda k: (start + k, 0, 0, 0, 0, 0))
    out = jax.ShapeDtypeStruct((count, before, after, rows, cols), BF16)
    out_block = pl.BlockSpec((1, *out.shape[1:]), lambda k: (k, 0, 0, 0, 0))

    def body(here_ref, mine_ref, other_ref, keep_ref, send_ref):
        here = here_ref[0]
        for ref, at in ((send_ref, 1 - here), (keep_ref, here)):
            ref[0] = (mine_ref[0, :, at].astype(F32) + other_ref[0, :, at].astype(F32)).astype(BF16)

    size = 6 * count * before * after * rows * cols * 2
    keep, send = pl.pallas_call(
        body,
        grid=(count,),
        out_shape=(out, out),
        in_specs=[pl.BlockSpec(memory_space=pltpu.SMEM), block, block],
        out_specs=(out_block, out_block),
        compiler_params=pltpu.CompilerParams(vmem_limit_bytes=24 * 1024 * 1024),
        cost_estimate=pl.CostEstimate(flops=0, bytes_accessed=size, transcendentals=0),
        name="fold",
    )(
        here.reshape(1).astype(jnp.int32),
        pltpu.with_memory_space_constraint(mine.reshape(shape), pltpu.HBM)
        if before * after > 4
        else mine.reshape(shape),
        other.reshape(shape),
    )
    flat = lambda v: v.reshape(count, before * after, rows, cols)
    return flat(keep), flat(send)


def fold_last(states, here):
    rows, cols = states[0][0].shape[-2:]
    counts = [mine.shape[0] for mine, _ in states]
    k = sum(counts)

    def body(here_ref, *refs):
        ins, outs = refs[: 2 * len(states)], refs[2 * len(states) :]
        for by, ref in enumerate(outs):
            at = lax.rem(here_ref[0] + by, 4)
            start = 0
            for i, count in enumerate(counts):
                total = ins[2 * i][:, at].astype(F32) + ins[2 * i + 1][:, at].astype(F32)
                ref[start : start + count] = total.astype(ref.dtype)
                start += count

    vmem = pl.BlockSpec(memory_space=pltpu.VMEM)
    return pl.pallas_call(
        body,
        out_shape=(jax.ShapeDtypeStruct((k, rows, cols), F32),)
        + (jax.ShapeDtypeStruct((k, rows, cols), BF16),) * 3,
        in_specs=[pl.BlockSpec(memory_space=pltpu.SMEM)] + [vmem] * (2 * len(states)),
        out_specs=(vmem,) * 4,
        compiler_params=pltpu.CompilerParams(vmem_limit_bytes=24 * 1024 * 1024),
        cost_estimate=pl.CostEstimate(
            flops=0, bytes_accessed=28 * k * rows * cols, transcendentals=0
        ),
        name="fold_last",
    )(here.reshape(1).astype(jnp.int32), *[part for state in states for part in state])


def place(parts, slots, lead=None, moves=None):
    count = len(parts)
    if lead is None:
        lead = (count, *parts[0].shape[:-2])
        moves = lambda slot: [(i, (), (slot[i],)) for i in range(count)]

    def body(slot_ref, *refs):
        ins, out = refs[:count], refs[count]
        for part, source, target in moves(slot_ref):
            out[target] = ins[part][source] if source else ins[part][...]

    size = count * parts[0].size * parts[0].dtype.itemsize
    vmem = pl.BlockSpec(memory_space=pltpu.VMEM)
    return pl.pallas_call(
        body,
        out_shape=jax.ShapeDtypeStruct((*lead, *parts[0].shape[-2:]), parts[0].dtype),
        in_specs=[pl.BlockSpec(memory_space=pltpu.SMEM)] + [vmem] * count,
        out_specs=vmem,
        cost_estimate=pl.CostEstimate(flops=0, bytes_accessed=2 * size, transcendentals=0),
        compiler_params=pltpu.CompilerParams(vmem_limit_bytes=24 * 1024 * 1024),
        name="place",
    )(jnp.stack(slots).astype(jnp.int32), *parts)


def place_halves(parts, slots):
    count = len(parts)
    rows, cols = parts[0].shape
    half = cols // 2

    def body(slot_ref, *refs):
        left, right = refs[count:]
        for i, ref in enumerate(refs[:count]):
            left[slot_ref[i]] = ref[:, :half]
            right[slot_ref[i]] = ref[:, half:]

    vmem = pl.BlockSpec(memory_space=pltpu.VMEM)
    shape = jax.ShapeDtypeStruct((count, rows, half), parts[0].dtype)
    return pl.pallas_call(
        body,
        out_shape=(shape, shape),
        in_specs=[pl.BlockSpec(memory_space=pltpu.SMEM)] + [vmem] * count,
        out_specs=(vmem, vmem),
        cost_estimate=pl.CostEstimate(flops=0, bytes_accessed=16 * rows * cols, transcendentals=0),
        compiler_params=pltpu.CompilerParams(vmem_limit_bytes=24 * 1024 * 1024),
        name="place_halves",
    )(jnp.stack(slots).astype(jnp.int32), *parts)


def slots_of(feeds, owners, width, quarter, extra=None):
    more = 0 if extra is None else extra.shape[0]
    arrays, index = [], {}

    def note(array):
        if array is None:
            return None
        source, columns = array
        if id(source) not in index:
            index[id(source)] = len(arrays)
            arrays.append(source)
        return (index[id(source)], columns)

    noted = [[(note(total), note(moment)) for total, moment in feed] for feed in feeds]
    rows = arrays[0].shape[-2]
    for total, _ in sum(feeds, []):
        if total is not None:
            rows = total[0].shape[-2]
    if all(total is None or total[0].shape[-2] == moment[0].shape[-2] for total, moment in sum(feeds, [])):
        quarter = jnp.int32(0)

    def block(array):
        shape = (*array.shape[:-2], rows, array.shape[-1])
        lead = (0,) * (array.ndim - 2)
        if array.shape[-2] == rows:
            return pl.BlockSpec(shape, lambda i, q: (*lead, 0, 0))
        return pl.BlockSpec(shape, lambda i, q: (*lead, q[0], 0))

    def body(_, *refs):
        out = refs[-1]
        if more:
            out = refs[-1].at[:, :rows]
            for slot in range(owners):
                refs[-1][slot, rows:] = refs[-2][...]

        def read(what):
            place_of, (lead, start, size) = what
            ref = refs[place_of]
            return ref[(*lead, slice(None), slice(start, start + size))].astype(F32)

        first = {}
        for slot in range(owners):
            if not noted[slot]:
                out[slot] = jnp.zeros((rows, width), BF16)
                continue
            key = str(noted[slot])
            if key in first:
                out[slot] = out[first[key]]
                continue
            first[key] = slot
            at = 0
            for total, moment in noted[slot]:
                value = MOMENTUM_DECAY * MOMENTUM_DECAY * read(moment)
                if total is not None:
                    value = value + (1.0 + MOMENTUM_DECAY) * read(total)
                out[slot, :, at : at + value.shape[1]] = value.astype(BF16)
                at += value.shape[1]

    return pl.pallas_call(
        body,
        out_shape=jax.ShapeDtypeStruct((owners, rows + more, width), BF16),
        grid_spec=pltpu.PrefetchScalarGridSpec(
            num_scalar_prefetch=1,
            grid=(1,),
            in_specs=[block(array) for array in arrays]
            + [pl.BlockSpec((more, width), lambda i, q: (0, 0))] * (more > 0),
            out_specs=pl.BlockSpec((owners, rows + more, width), lambda i, q: (0, 0, 0)),
        ),
        cost_estimate=pl.CostEstimate(
            flops=0, bytes_accessed=2 * owners * rows * width, transcendentals=0
        ),
        compiler_params=pltpu.CompilerParams(vmem_limit_bytes=24 * 1024 * 1024),
        name="slots",
    )(
        quarter.reshape(1).astype(jnp.int32),
        *[
            array
            if array.shape[-2] == rows
            else pltpu.with_memory_space_constraint(array, pltpu.HBM)
            for array in arrays
        ],
        *([extra] if more else []),
    )


def pack(parts):
    arrays, index = [], {}
    for array, _, _ in parts:
        if id(array) not in index:
            index[id(array)] = len(arrays)
            arrays.append(array)
    rows = arrays[0].shape[-2]
    total = sum(cols for _, _, cols in parts)

    def body(*refs):
        at = 0
        for array, lead, cols in parts:
            value = refs[index[id(array)]][(*lead, slice(None), slice(0, cols))]
            refs[-1][:, at : at + cols] = value.astype(BF16)
            at += cols

    vmem = pl.BlockSpec(memory_space=pltpu.VMEM)
    return pl.pallas_call(
        body,
        out_shape=jax.ShapeDtypeStruct((rows, total), BF16),
        in_specs=[vmem] * len(arrays),
        out_specs=vmem,
        cost_estimate=pl.CostEstimate(flops=0, bytes_accessed=6 * rows * total, transcendentals=0),
        compiler_params=pltpu.CompilerParams(vmem_limit_bytes=24 * 1024 * 1024),
        name="pack",
    )(*arrays)


def pick(values, index):
    found = jnp.int32(values[0])
    for i, value in enumerate(values):
        if value != values[0]:
            found = jnp.where(index == i, jnp.int32(value), found)
    return found


def update_kernel(quarters, slot_ref, *refs):
    step_refs, refs = refs[:quarters], refs[quarters:]
    modulation, projection, output, expand, shrink = refs[:5]
    out_modulation, out_projection, out_output, out_expand, out_shrink = refs[5:10]
    quarter = pl.program_id(0)
    rows = step_refs[0].shape[0]
    ratio = LEARN_RATE * (FF / D) ** 0.5
    for which, steps in enumerate(step_refs):

        @pl.when(slot_ref[quarter] == which)
        def _(steps=steps):
            at = 3 * FF
            for k in range(2):
                step = steps[:, k * FF : (k + 1) * FF].astype(F32)
                out_expand[k] = expand[k] - ratio * step
            out_shrink[...] = shrink[...] - LEARN_RATE * steps[:, 2 * FF : at].astype(F32)
            for master, out, count in (
                (modulation, out_modulation, 6),
                (projection, out_projection, 3),
            ):
                for k in range(count):
                    out[k] = master[k] - LEARN_RATE * steps[:, at : at + D].astype(F32)
                    at += D
            out_output[...] = output[...] - LEARN_RATE * steps[:, at : at + D].astype(F32)


def update(slots, steps, masters):
    quarters = len(steps)
    rows = steps[0].shape[0]
    third = lambda a: pl.BlockSpec((a.shape[0], rows, a.shape[2]), lambda q: (0, q, 0))
    masters = (*masters[:4], masters[4].T)
    modulation, projection, output, expand, shrink = masters
    specs = [
        third(modulation),
        third(projection),
        pl.BlockSpec((rows, D), lambda q: (q, 0)),
        third(expand),
        pl.BlockSpec((rows, FF), lambda q: (q, 0)),
    ]
    updated = pl.pallas_call(
        functools.partial(update_kernel, quarters),
        grid=(quarters,),
        out_shape=tuple(jax.ShapeDtypeStruct(a.shape, F32) for a in masters),
        in_specs=[pl.BlockSpec(memory_space=pltpu.SMEM)] + [whole(a) for a in steps] + specs,
        out_specs=tuple(specs),
        cost_estimate=pl.CostEstimate(flops=0, bytes_accessed=14_000_000, transcendentals=0),
        compiler_params=pltpu.CompilerParams(vmem_limit_bytes=24 * 1024 * 1024),
        name="update",
    )(
        jnp.stack(slots).astype(jnp.int32),
        *steps,
        *[pltpu.with_memory_space_constraint(a, pltpu.HBM) for a in masters],
    )
    return (*updated[:4], updated[4].T)


def every(*sizes):
    return list(itertools.product(*[range(size) for size in sizes]))


class Plain:
    images = ("dp", "fsdp")
    rows = "fsdp"
    wide_parts = 1

    def __init__(self, mesh):
        self.mesh = mesh
        self.row_shards = mesh.shape["fsdp"]
        self.owners = mesh.shape["fsdp"]
        self.wide_slots = [(i, 0) for i in range(3)]
        self.wide_slots += [None] * (self.owners - 3)
        self.slots = [None] * 3 + list(range(10))
        self.slots += [None] * (self.owners - ITEMS)

    def row_index(self):
        return lax.axis_index("fsdp")

    def group_index(self):
        return lax.axis_index("dp")

    def owner_index(self):
        return lax.axis_index("fsdp")

    def gather_weights(self, first, second, modulate, attend):
        full = [lax.all_gather(chunk, "fsdp", axis=0, tiled=True) for chunk in (first, second)]
        first, second = [jnp.split(chunk, 2, axis=1) for chunk in full]
        modulation = modulate[1](modulate[0]())
        return first, second, modulation, attend(first, modulation)

    def to_group(self, value):
        return lax.all_to_all(value, "fsdp", split_axis=0, concat_axis=0, tiled=True)

    def halves(self):
        return jnp.int32(0)

    def begin(self, mine, send):
        k, n, rows, cols = mine.shape
        return (jnp.stack([mine, send], axis=2).reshape(k, 2 * n * rows, cols),)

    def step(self, state, axis, start=0, count=None):
        return (state[0][start : start + (count or state[0].shape[0])],)

    def last_begin(self, *states):
        return states

    def last_end(self, states):
        return self.last(*states)

    def last(self, *states):
        value = jnp.concatenate([state[0] for state in states], axis=0)
        shard = lax.psum_scatter(value, "fsdp", scatter_dimension=1, tiled=True)
        return lax.psum(shard.astype(F32), "dp")

    def own_rows(self, shard, dim=-2):
        return shard

    def complete_begin(self, piece):
        return piece

    def complete_end(self, piece):
        return piece

    def quarters(self, piece):
        return [jnp.int32(0)], [piece]

    def to_owners(self, pieces):
        got = lax.all_to_all(pieces, "fsdp", split_axis=0, concat_axis=0, tiled=True)
        return got.reshape(-1, got.shape[2])

    def wide_slots_of(self, feeds):
        return slots_of(
            [[] if slot is None else feeds[slot[0]] for slot in self.wide_slots],
            self.owners,
            FF,
            jnp.int32(0),
        )

    def wide_halves(self, got):
        return got

    def wide_whole(self, got):
        return jnp.stack(jnp.split(got, 2, axis=1))

    def square_slots(self, feeds, rows):
        return (
            slots_of(
                [[] if slot is None else feeds[slot] for slot in self.slots],
                self.owners,
                D,
                self.group_index(),
            ),
            rows,
        )

    def square_to_owners(self, slots, beside):
        pieces, rows = slots
        rows = lax.all_gather(rows, ("dp", "fsdp"), axis=0, tiled=True)
        return self.to_owners(pieces), rows, beside

    def to_rows(self, whole):
        blocks = whole.reshape(self.row_shards, -1, whole.shape[1])
        return lax.all_to_all(blocks, "fsdp", split_axis=0, concat_axis=0, tiled=True)


class Torus:
    images = ("x", "c", "z", "y")
    rows = ("z", "y")
    chips = ("x", "z", "y")
    wide_parts = 2

    def __init__(self, mesh):
        self.mesh = Mesh(mesh.devices.reshape(2, 2, 4, 2), ("x", "c", "z", "y"))
        self.row_shards = 8
        self.owners = 16
        wide_places = [(1, 0), (2, 1), (1, 1)]
        self.wide_slots = [None] * 16
        self.slots = [None] * 16
        for item, (z, y) in enumerate(wide_places):
            for part in range(2):
                self.wide_slots[(part * 4 + z) * 2 + y] = (item, part)
        free = [i for i in range(16) if self.wide_slots[i] is None]
        for item, slot in enumerate(free):
            self.slots[slot] = item

    def row_index(self):
        return lax.axis_index("z") * 2 + lax.axis_index("y")

    def group_index(self):
        return lax.axis_index("x") * 2 + lax.axis_index("c")

    def owner_index(self):
        return (lax.axis_index("x") * 4 + lax.axis_index("z")) * 2 + lax.axis_index("y")

    def swap(self, value, axis):
        return lax.ppermute(value, axis, [(0, 1), (1, 0)])

    def shift(self, value, by):
        return lax.ppermute(value, "z", [(i, (i + by) % 4) for i in range(4)])

    def exchange(self, value, axis):
        here = lax.axis_index(axis)
        return place([value, self.swap(value, axis)], [here, 1 - here])

    def spread_z(self, value):
        z = lax.axis_index("z")
        ring = [value] + [self.shift(value, by) for by in range(1, 4)]
        return place(ring, [(z - by) % 4 for by in range(4)])

    def gather_weights(self, first, second, modulate, attend):
        x, y, z, c = [lax.axis_index(axis) for axis in "xyzc"]
        slots = [(z - by) % 4 for by in range(4)]

        def ring_of(chunk, *others):
            piece = self.own_rows(chunk)
            if others:
                piece = tie(piece, *others)
            return [piece] + [self.shift(piece, by) for by in range(1, 4)]

        def one_hop(left, right):
            left_other, right_other = self.swap(left, "y"), self.swap(right, "x")
            left = place([left, left_other], [y, 1 - y])
            right = place([right, right_other], [x, 1 - x])
            return left, right

        def other_hop(left, right):
            left, right = meet(left, right)
            left_other, right_other = meet(self.swap(left, "x"), self.swap(right, "y"))
            left = place([left, left_other], [x, 1 - x])
            right = place([right, right_other], [y, 1 - y])
            return left, right

        def by_core(left, right):
            others = self.swap(left, "c"), self.swap(right, "c")
            pair = []
            for half, other, order in ((left, others[0], (2, 1, 0)), (right, others[1], (2, 0, 1))):

                def moves(slot, order=order):
                    found = []
                    for part in range(2):
                        for at in every(2, 2, 4):
                            found.append((part, at, (*[at[i] for i in order], slot[part])))
                    return found

                pair.append(place([half, other], [c, 1 - c], (4, 2, 2, 2), moves).reshape(D, -1))
            return pair

        group = modulate[0]()
        left, right = place_halves(ring_of(first), slots)
        left, right, group = meet(left, right, group)
        ring = ring_of(second, left, right)
        left, right = one_hop(left, right)
        left, right, ring[0], ring[1], ring[3] = meet(left, right, ring[0], ring[1], ring[3])
        left, right = other_hop(left, right)
        modulation = modulate[1](group)
        left, right, ring[2] = meet(left, right, ring[2])
        second_left, second_right = place_halves(ring, slots)
        others = self.swap(second_left, "y"), self.swap(second_right, "x")
        done = by_core(left, right)
        done, others, modulation = meet(done, others, modulation)
        left = place([second_left, others[0]], [y, 1 - y])
        right = place([second_right, others[1]], [x, 1 - x])
        left, right = meet(left, right)
        others = self.swap(left, "x"), self.swap(right, "y")
        done, left, right = meet(done, left, right)
        results = attend(done, modulation)
        left_other, right_other, results = meet(*others, results)
        left = place([left, left_other], [x, 1 - x])
        right = place([right, right_other], [y, 1 - y])
        return done, by_core(left, right), modulation, results

    def to_group(self, value):
        return lax.all_to_all(value, ("z", "y"), split_axis=0, concat_axis=0, tiled=True)

    def halves(self):
        return lax.axis_index("c")

    def begin(self, mine, send):
        return (mine, self.swap(send, "c"))

    def step(self, state, axis, start=0, count=None):
        mine, other = state
        parts = mine.shape[1]
        view = (4, 2) if (parts, axis) == (16, "y") else (parts // 2, 1)
        keep, send = fold(
            mine, other, lax.axis_index(axis), view, start, count or mine.shape[0]
        )
        return (keep, self.swap(send, axis))

    def last(self, *states):
        return self.last_end(self.last_begin(*states))

    def last_begin(self, *states):
        return fold_last(states, lax.axis_index("z"))

    def last_end(self, folded):
        total, *sends = folded
        for by, send in enumerate(sends, 1):
            total = total + self.shift(send, by).astype(F32)
        return total

    def own_rows(self, shard, dim=-2):
        return lax.dynamic_slice_in_dim(
            shard, self.group_index() * (D // 32), D // 32, dim % shard.ndim
        )

    def quarters(self, piece):
        x, c = lax.axis_index("x"), lax.axis_index("c")
        by_x = self.swap(piece, "x")
        by_c = self.swap(piece, "c")
        by_both = self.swap(by_x, "c")
        slots = []
        for at_x, at_c in every(2, 2):
            slots.append(jnp.where(at_x == x, 0, 1) + jnp.where(at_c == c, 0, 2))
        return slots, [piece, by_x, by_c, by_both]

    def complete_begin(self, piece):
        return piece, self.swap(piece, "x")

    def complete_end(self, pair):
        x, c = lax.axis_index("x"), lax.axis_index("c")
        value = place(list(pair), [x, 1 - x])
        moves = lambda slot: [(part, (x,), (x, slot[part])) for part in range(2) for x in range(2)]
        value = place([value, self.swap(value, "c")], [c, 1 - c], (2, 2), moves)
        return value.reshape(D // 8, -1)

    def to_owners(self, pieces):
        return lax.all_to_all(pieces, self.chips, split_axis=0, concat_axis=0, tiled=True)

    def wide_slots_of(self, feeds):
        halved = []
        for slot in self.wide_slots:
            halved.append([] if slot is None else [feeds[slot[0]][slot[1]]])
        return slots_of(halved, self.owners, FF // 2, self.group_index())

    def wide_halves(self, got):
        return got, self.swap(got, "x")

    def wide_whole(self, got):
        half = FF // 2
        x, c = lax.axis_index("x"), lax.axis_index("c")
        both = place(list(got), [x, 1 - x])
        both = both.reshape(2, 2, 4, 2, D // 32, half)

        def moves(slot):
            return [
                (part, (p, x, z, y), (p, z, y, x, slot[part]))
                for part in range(2)
                for p, x, z, y in every(2, 2, 4, 2)
            ]

        whole = place([both, self.swap(both, "c")], [c, 1 - c], (2, 4, 2, 2, 2), moves)
        return whole.reshape(2, D, half)

    def square_slots(self, feeds, rows):
        return slots_of(
            [[] if slot is None else feeds[slot] for slot in self.slots],
            self.owners,
            D,
            self.group_index(),
            rows.reshape(-1, D),
        )

    def square_to_owners(self, slots, beside):
        quarter = D // 32
        got = self.to_owners(slots)
        got, beside = meet(got, beside)
        other = self.swap(got, "c")
        more = got.shape[1] - quarter

        def body(c_ref, mine_ref, other_ref, whole_ref, rows_ref):
            c = c_ref[0]
            for ref, at in ((mine_ref, c), (other_ref, 1 - c)):
                for chip, (x, z, y) in enumerate(every(2, 4, 2)):
                    whole_ref[z, y, x, at] = ref[chip, :quarter]
                    rows_ref[at, chip] = ref[chip, quarter:]

        vmem = pl.BlockSpec(memory_space=pltpu.VMEM)
        square, gathered = pl.pallas_call(
            body,
            out_shape=(
                jax.ShapeDtypeStruct((4, 2, 2, 2, quarter, D), BF16),
                jax.ShapeDtypeStruct((2, 16, more, D), BF16),
            ),
            in_specs=[pl.BlockSpec(memory_space=pltpu.SMEM), vmem, vmem],
            out_specs=(vmem, vmem),
            cost_estimate=pl.CostEstimate(
                flops=0, bytes_accessed=8 * got.size, transcendentals=0
            ),
            compiler_params=pltpu.CompilerParams(vmem_limit_bytes=24 * 1024 * 1024),
            name="place_square",
        )(lax.axis_index("c").reshape(1).astype(jnp.int32), got, other)
        return square.reshape(D, D), gathered.reshape(-1, 8, D), beside

    def to_rows(self, whole):
        cols = whole.shape[1]
        blocks = whole.reshape(4, 2, 2, 2, D // 32, cols)
        blocks = lax.dynamic_index_in_dim(blocks, lax.axis_index("c"), 3, keepdims=False)
        blocks = blocks.transpose(2, 0, 1, 3, 4).reshape(16, D // 32, cols)
        return lax.all_to_all(blocks, self.chips, split_axis=0, concat_axis=0, tiled=True)


def lanes(shape, dim):
    return lax.broadcasted_iota(jnp.int32, shape, dim)


def norm_of(values):
    centred = values - jnp.mean(values, axis=-1, keepdims=True)
    inverse = lax.rsqrt(jnp.mean(centred * centred, axis=-1, keepdims=True) + NORM_EPS)
    return centred * inverse, inverse


def norm_back(incoming, normed, inverse):
    return inverse * (
        incoming
        - jnp.mean(incoming, axis=-1, keepdims=True)
        - normed * jnp.mean(incoming * normed, axis=-1, keepdims=True)
    )


def rotate_pair(value):
    first = lanes(value.shape, 1) % 32 < 16
    return jnp.where(first, -pltpu.roll(value, 112, 1), pltpu.roll(value, 16, 1))


def two_heads(value):
    low = lanes(value.shape, 1) < HDIM
    zero = jnp.zeros_like(value)
    return jnp.where(low, value, zero), jnp.where(low, zero, value)


def pair_at(pair):
    return pl.ds(pl.multiple_of(pair * 2 * HDIM, 2 * HDIM), 2 * HDIM)


def attention_forward_kernel(
    length_ref,
    input_ref,
    cotangent_ref,
    modulation_ref,
    cosine_ref,
    sine_ref,
    query_key_ref,
    value_output_ref,
    first_ref,
    query_ref,
    key_ref,
    value_ref,
    probs_ref,
    attended_ref,
    attention_ref,
    middle_ref,
    second_ref,
    branch_ref,
):
    length = length_ref[pl.program_id(0)]
    row = lambda which: modulation_ref[0, which : which + 1, :]
    stream = input_ref[0].astype(F32)
    positions = stream.shape[0]
    normed, _ = norm_of(stream)
    first = (normed * (1.0 + row(1)) + row(0)).astype(BF16)
    first_ref[0] = first
    inside = lanes((positions, D), 0) < length
    upstream = jnp.where(inside, cotangent_ref[0].astype(F32), 0.0)
    branch_ref[0] = (row(5) * upstream).astype(BF16)
    value_ref[0] = dot(first, value_output_ref[:, :D]).astype(BF16)
    cosine, sine = cosine_ref[0], sine_ref[0]
    keep = lanes((positions, positions), 1) < length

    @pl.loop(0, HEADS // 2)
    def _(pair):
        at = pair_at(pair)
        query = dot(first, query_key_ref[:, at])
        key = dot(first, query_key_ref[:, pair_at(HEADS // 2 + pair)])
        query = (query * cosine + rotate_pair(query) * sine).astype(BF16)
        key = (key * cosine + rotate_pair(key) * sine).astype(BF16)
        query_ref[0, :, at] = query
        key_ref[0, :, at] = key
        low = []
        for head, masked in enumerate(two_heads(query)):
            scores = dot(masked, key, NT) * HDIM ** (-0.5)
            scores = jnp.where(keep, scores, -1000000000.0)
            exponent = jnp.exp(scores - jnp.max(scores, axis=-1, keepdims=True))
            probs = exponent * (1.0 / jnp.sum(exponent, axis=-1, keepdims=True))
            probs_ref[0, 2 * pair + head] = probs
            low.append(probs.astype(BF16))
        values = two_heads(value_ref[0, :, at])
        attended_ref[0, :, at] = dot(
            jnp.concatenate(low, axis=1), jnp.concatenate(values, axis=0)
        ).astype(BF16)

    attention = dot(attended_ref[0], value_output_ref[:, D:])
    attention_ref[0] = attention
    middle = stream + row(2) * attention
    middle_ref[0] = middle
    normed, _ = norm_of(middle)
    second_ref[0] = (normed * (1.0 + row(4)) + row(3)).astype(BF16)


def split_rows(value, scratch, here, keep_ref, send_ref, which, cols):
    scratch[...] = value
    rows = keep_ref.shape[2]
    for i in range(keep_ref.shape[1]):
        for ref, at in ((keep_ref, here), (send_ref, 1 - here)):
            start = pl.multiple_of((2 * i + at) * rows, 8)
            ref[which, i, :, cols] = scratch[pl.ds(start, rows), :].astype(BF16)


def feed_forward_kernel(
    here_ref,
    second_ref,
    branch_ref,
    gate_ref,
    up_ref,
    down_ref,
    out_ref,
    back_ref,
    keep_ref,
    send_ref,
    second_t,
    branch_t,
    rows,
):
    step = pl.program_id(0)

    @pl.when(step == 0)
    def _():
        second_t[...] = second_ref[...].T
        branch_t[...] = branch_ref[...].T
        out_ref[...] = jnp.zeros_like(out_ref)
        back_ref[...] = jnp.zeros_like(back_ref)

    gate, up, down = gate_ref[...], up_ref[...], down_ref[...]
    gate_pre = dot(second_ref[...], gate)
    up_pre = dot(second_ref[...], up)
    sigmoid = 1.0 / (1.0 + jnp.exp(-gate_pre))
    swish = gate_pre * sigmoid
    hidden = (swish * up_pre).astype(BF16)
    out_ref[...] += dot(hidden, down, NT)
    grad_hidden = dot(branch_ref[...], down)
    grad_gate = (grad_hidden * up_pre * sigmoid * (1.0 + gate_pre * (1.0 - sigmoid))).astype(BF16)
    grad_up = (grad_hidden * swish).astype(BF16)
    back_ref[...] += dot(grad_gate, gate, NT) + dot(grad_up, up, NT)
    everything = slice(None)
    products = ((second_t, grad_gate), (second_t, grad_up), (branch_t, hidden))
    for which, (left, right) in enumerate(products):
        split_rows(
            dot(left[...], right), rows, here_ref[0], keep_ref, send_ref, which, everything
        )


def attention_backward_kernel(
    length_ref,
    branch_left_ref,
    branch_right_ref,
    second_left_ref,
    second_right_ref,
    middle_ref,
    cotangent_ref,
    modulation_ref,
    attention_ref,
    value_output_ref,
    query_ref,
    key_ref,
    value_ref,
    probs_ref,
    cosine_ref,
    sine_ref,
    output_ref,
    stream_ref,
    grads_ref,
    sums_ref,
    attended_grad,
):
    length = length_ref[pl.program_id(0)]
    row = lambda which: modulation_ref[0, which : which + 1, :]
    middle = middle_ref[0]
    positions = middle.shape[0]
    inside = lanes((positions, D), 0) < length
    upstream = jnp.where(inside, cotangent_ref[0].astype(F32), 0.0)
    branch = branch_left_ref[0] + branch_right_ref[0]
    output_ref[0] = (middle + row(5) * branch).astype(BF16)
    total = lambda value: jnp.sum(value, axis=0, keepdims=True)
    gate_two = total(upstream * branch)
    second = second_left_ref[0] + second_right_ref[0]
    normed, inverse = norm_of(middle)
    scale_two = total(second * normed)
    shift_two = total(second)
    stream = upstream + norm_back(second * (1.0 + row(4)), normed, inverse)
    stream_ref[0] = stream
    gate_one = total(stream * attention_ref[0])
    blank = jnp.zeros_like(gate_one)
    sums_ref[0] = jnp.concatenate(
        [blank, blank, gate_one, shift_two, scale_two, gate_two, blank, blank], axis=0
    )
    grad_attention = (row(2) * stream).astype(BF16)
    grads_ref[3, 0] = grad_attention
    attended_grad[...] = dot(grad_attention, value_output_ref[:, D:], NT).astype(BF16)
    cosine, sine = cosine_ref[0], sine_ref[0]

    @pl.loop(0, HEADS // 2)
    def _(pair):
        at = pair_at(pair)
        query, key, value = query_ref[0, :, at], key_ref[0, :, at], value_ref[0, :, at]
        attended = two_heads(attended_grad[:, at])
        low, scores = [], []
        for head in range(2):
            probs = probs_ref[0, 2 * pair + head]
            grad_probs = dot(attended[head], value, NT)
            inner = jnp.sum(grad_probs * probs, axis=-1, keepdims=True)
            scores.append((probs * (grad_probs - inner)).astype(BF16))
            low.append(probs.astype(BF16))
        grads_ref[2, 0, :, at] = dot(
            jnp.concatenate(low, axis=0), jnp.concatenate(attended, axis=0), TN
        ).astype(BF16)
        grad_query = dot(
            jnp.concatenate(scores, axis=1), jnp.concatenate(two_heads(key), axis=0)
        ) * HDIM ** (-0.5)
        grad_key = dot(
            jnp.concatenate(scores, axis=0), jnp.concatenate(two_heads(query), axis=0), TN
        ) * HDIM ** (-0.5)
        grads_ref[0, 0, :, at] = (grad_query * cosine - rotate_pair(grad_query * sine)).astype(BF16)
        grads_ref[1, 0, :, at] = (grad_key * cosine - rotate_pair(grad_key * sine)).astype(BF16)


def projection_backward_kernel(
    here_ref,
    grads_in_ref,
    first_ref,
    attended_ref,
    input_ref,
    modulation_ref,
    stream_ref,
    sums_ref,
    active_ref,
    query_key_ref,
    value_output_ref,
    keep_ref,
    send_ref,
    input_grad_ref,
    modulation_grad_ref,
    first_t,
    first_grad,
    rows,
):
    images, positions = input_ref.shape[:2]
    tokens = images * positions
    flat = lambda ref: ref[...].reshape(tokens, D)
    step = pl.program_id(0)

    def product(grads):
        split_rows(dot(first_t[...], grads), rows, here_ref[0], keep_ref, send_ref, 0, slice(None))

    @pl.when(step == 0)
    def _():
        first_t[...] = flat(first_ref).T
        grads = grads_in_ref[0].reshape(tokens, D)
        product(grads)
        first_grad[...] = dot(grads, query_key_ref[:, :D], NT)

    @pl.when(step == 1)
    def _():
        grads = grads_in_ref[0].reshape(tokens, D)
        product(grads)
        first_grad[...] += dot(grads, query_key_ref[:, D:], NT)

    @pl.when(step == 2)
    def _():
        grads = grads_in_ref[0].reshape(tokens, D)
        product(grads)
        first_grad[...] += dot(grads, value_output_ref[:, :D], NT)

    @pl.when(step == 3)
    def _():
        first_t[...] = flat(attended_ref).T
        product(grads_in_ref[0].reshape(tokens, D))
        for image in range(images):
            at = slice(image * positions, (image + 1) * positions)
            normed, inverse = norm_of(input_ref[image].astype(F32))
            first = first_grad[at, :]
            scale_one = jnp.sum(first * normed, axis=0, keepdims=True)
            shift_one = jnp.sum(first, axis=0, keepdims=True)
            scaled = first * (1.0 + modulation_ref[image, 1:2, :])
            input_grad_ref[image] = stream_ref[image] + norm_back(scaled, normed, inverse)
            modulation_grad_ref[image] = jnp.concatenate(
                [
                    shift_one,
                    scale_one,
                    sums_ref[image, 2:6, :],
                    active_ref[image : image + 1, :].astype(F32),
                    jnp.zeros_like(shift_one),
                ],
                axis=0,
            ).astype(BF16)


BIG_VMEM = 58 * 1024 * 1024


def whole(array):
    return pl.BlockSpec(array.shape, lambda *_: (0,) * array.ndim)


def by_image(array):
    return pl.BlockSpec((1, *array.shape[1:]), lambda b: (b,) + (0,) * (array.ndim - 1))


def call(body, grid, ins, in_specs, outs, out_specs, scratch, flops, name):
    size = sum(a.size * a.dtype.itemsize for a in (*ins, *outs))
    return pl.pallas_call(
        body,
        grid=grid,
        out_shape=outs,
        in_specs=in_specs,
        out_specs=out_specs,
        scratch_shapes=scratch,
        compiler_params=pltpu.CompilerParams(vmem_limit_bytes=BIG_VMEM),
        cost_estimate=pl.CostEstimate(flops=flops, bytes_accessed=size, transcendentals=0),
        name=name,
    )(*ins)


def attention_forward(lengths, inputs, cotangent, modulation, cosine, sine, query_key, value_output):
    images, positions, _ = inputs.shape
    ins = (lengths, inputs, cotangent, modulation, cosine, sine, query_key, value_output)
    in_specs = [pl.BlockSpec(memory_space=pltpu.SMEM)]
    in_specs += [by_image(a) for a in ins[1:6]] + [whole(a) for a in ins[6:]]
    token = lambda dtype: jax.ShapeDtypeStruct((images, positions, D), dtype)
    outs = (
        token(BF16),
        token(BF16),
        token(BF16),
        token(BF16),
        jax.ShapeDtypeStruct((images, HEADS, positions, positions), F32),
        token(BF16),
        token(F32),
        token(F32),
        token(BF16),
        token(BF16),
    )
    flops = 2 * images * positions * D * (4 * D + 2 * positions)
    return call(
        attention_forward_kernel,
        (images,),
        ins,
        in_specs,
        outs,
        [by_image(a) for a in outs],
        [],
        flops,
        "attention_forward",
    )


def feed_forward(here, second, branch, weight):
    tokens = second.shape[0]
    units = weight.shape[1] // 3
    tile = 256
    steps = units // tile
    weight = pltpu.with_memory_space_constraint(weight, pltpu.HBM)
    ins = (here.reshape(1).astype(jnp.int32), second, branch, weight, weight, weight)
    in_specs = [pl.BlockSpec(memory_space=pltpu.SMEM), whole(second), whole(branch)] + [
        pl.BlockSpec((D, tile), lambda t, which=which: (0, which * steps + t)) for which in range(3)
    ]
    outs = (
        jax.ShapeDtypeStruct((tokens, D), F32),
        jax.ShapeDtypeStruct((tokens, D), F32),
        jax.ShapeDtypeStruct((3, D // 48, 24, units), BF16),
        jax.ShapeDtypeStruct((3, D // 48, 24, units), BF16),
    )
    out_specs = [whole(outs[0]), whole(outs[1])]
    out_specs += [pl.BlockSpec((3, D // 48, 24, tile), lambda t: (0, 0, 0, t))] * 2
    scratch = [pltpu.VMEM((D, tokens), BF16), pltpu.VMEM((D, tokens), BF16), pltpu.VMEM((D, tile), F32)]
    flops = 2 * 9 * tokens * D * units
    return call(
        feed_forward_kernel, (steps,), ins, in_specs, outs, out_specs, scratch, flops, "feed_forward"
    )


def attention_backward(lengths, *ins):
    images, positions, _ = ins[0].shape
    shared = 8
    in_specs = [pl.BlockSpec(memory_space=pltpu.SMEM)]
    in_specs += [whole(a) if i == shared else by_image(a) for i, a in enumerate(ins)]
    outs = (
        jax.ShapeDtypeStruct((images, positions, D), BF16),
        jax.ShapeDtypeStruct((images, positions, D), F32),
        jax.ShapeDtypeStruct((4, images, positions, D), BF16),
        jax.ShapeDtypeStruct((images, 8, D), F32),
    )
    out_specs = [
        by_image(outs[0]),
        by_image(outs[1]),
        pl.BlockSpec((4, 1, positions, D), lambda b: (0, b, 0, 0)),
        by_image(outs[3]),
    ]
    flops = 2 * images * positions * D * (D + 5 * positions)
    return call(
        attention_backward_kernel,
        (images,),
        (lengths, *ins),
        in_specs,
        outs,
        out_specs,
        [pltpu.VMEM((positions, D), BF16)],
        flops,
        "attention_backward",
    )


def projection_backward(here, *ins):
    _, images, positions, _ = ins[0].shape
    tokens = images * positions
    in_specs = [pl.BlockSpec(memory_space=pltpu.SMEM)]
    in_specs += [pl.BlockSpec((1, images, positions, D), lambda k: (k, 0, 0, 0))]
    in_specs += [whole(a) for a in ins[1:]]
    ins = (here.reshape(1).astype(jnp.int32), *ins)
    outs = (
        jax.ShapeDtypeStruct((4, D // 48, 24, D), BF16),
        jax.ShapeDtypeStruct((4, D // 48, 24, D), BF16),
        jax.ShapeDtypeStruct((images, positions, D), F32),
        jax.ShapeDtypeStruct((images, 8, D), BF16),
    )
    out_specs = [pl.BlockSpec((1, D // 48, 24, D), lambda k: (k, 0, 0, 0))] * 2
    out_specs += [whole(outs[2]), whole(outs[3])]
    scratch = [pltpu.VMEM((D, tokens), BF16), pltpu.VMEM((tokens, D), F32), pltpu.VMEM((D, D), F32)]
    return call(
        projection_backward_kernel,
        (4,),
        ins,
        in_specs,
        outs,
        out_specs,
        scratch,
        2 * 7 * tokens * D * D,
        "projection_backward",
    )


def swish_value(values):
    return values / (1.0 + jnp.exp(-values))


def rope_tables(extents, positions):
    quarter = HDIM // 4
    places = jnp.arange(positions, dtype=jnp.int32)
    widths = extents[:, 1]
    row_place = (places[None, :] // widths[:, None]).astype(F32)
    col_place = (places[None, :] % widths[:, None]).astype(F32)
    lane = jnp.arange(2 * HDIM) % HDIM
    frequency = 10000.0 ** (-(lane % quarter).astype(F32) / quarter)
    by_row = lane < 2 * quarter
    angle = jnp.where(by_row, row_place[:, :, None], col_place[:, :, None]) * frequency
    return jnp.cos(angle), jnp.sin(angle)


def local(
    comm,
    inputs,
    cotangent,
    image_shape,
    time_bins,
    time_table,
    modulation_master,
    projection_master,
    output_master,
    expand_master,
    shrink_master,
    modulation_moment,
    projection_moment,
    output_moment,
    expand_moment,
    shrink_moment,
):
    masters = (modulation_master, projection_master, output_master, expand_master, shrink_master)
    moments = (modulation_moment, projection_moment, output_moment, expand_moment, shrink_moment)
    images, positions, features = inputs.shape
    tokens = images * positions
    rows = modulation_master.shape[1]
    row_index = comm.row_index()

    half = FF // 2
    shrink_low = shrink_master.astype(BF16).T
    packed_attention = jnp.concatenate(
        [projection_master[i].astype(BF16) for i in range(3)] + [output_master.astype(BF16)], axis=1
    )
    packed_units = jnp.concatenate(
        [
            part
            for cols in (slice(None, half), slice(half, None))
            for part in (
                expand_master[0, :, cols].astype(BF16),
                expand_master[1, :, cols].astype(BF16),
                shrink_low[:, cols],
            )
        ],
        axis=1,
    )
    selector = (
        time_bins[:, None] == jnp.arange(time_table.shape[0], dtype=jnp.int32)[None, :]
    ).astype(F32)
    active = swish_value(jnp.dot(selector, time_table, precision=HIGHEST)).astype(BF16)

    def group_rows():
        return comm.to_group(active.reshape(images, comm.row_shards, rows).transpose(1, 0, 2))

    def modulation_of(group):
        partial = jnp.einsum(
            "bd,kde->bke",
            group.reshape(-1, rows),
            modulation_master.astype(BF16),
            preferred_element_type=F32,
        )
        return jnp.sum(
            comm.to_group(partial.reshape(comm.row_shards, images, 6, features)), axis=0
        )

    cosine, sine = rope_tables(image_shape, positions)
    lengths = image_shape[:, 0] * image_shape[:, 1]

    def attend(weights, modulation):
        return attention_forward(
            lengths, inputs, cotangent, modulation, cosine, sine, weights[0], weights[1]
        )

    first, second, modulation, results = comm.gather_weights(
        packed_attention, packed_units, (group_rows, modulation_of), attend
    )
    query_key_weight, value_output_weight = first
    left_weight, right_weight = second
    (first_input, query, key, value, probs, attended, attention, middle, second_input, grad_branch) = (
        results
    )
    second_flat = second_input.reshape(tokens, D)
    branch_flat = grad_branch.reshape(tokens, D)
    shaped = lambda v: v.reshape(images, positions, D)
    here = comm.halves()
    branch_left, back_left, *grads = feed_forward(here, second_flat, branch_flat, left_weight)
    left_sum = comm.begin(*grads)
    second_flat = tie(second_flat, back_left)
    branch_right, back_right, *grads = feed_forward(here, second_flat, branch_flat, right_weight)
    back_right, left_sum, grads = meet(back_right, left_sum, grads)
    left_sum = comm.step(left_sum, "x", 0, 2), comm.step(left_sum, "y", 2, 1)
    right_sum = comm.begin(*grads)
    block_output, grad_stream, grads, sums = attention_backward(
        lengths,
        shaped(branch_left),
        shaped(branch_right),
        shaped(back_left),
        shaped(back_right),
        middle,
        cotangent,
        modulation,
        attention,
        value_output_weight,
        query,
        key,
        value,
        probs,
        cosine,
        sine,
    )
    left_sum, right_sum, grads = meet(left_sum, right_sum, grads)
    left_sum = comm.step(left_sum[0], "y"), comm.step(left_sum[1], "x")
    right_sum = comm.step(right_sum, "x", 0, 2), comm.step(right_sum, "y", 2, 1)
    *grads, input_gradient, grad_modulation = projection_backward(
        here,
        grads,
        first_input,
        attended,
        inputs,
        modulation,
        grad_stream,
        sums,
        active,
        query_key_weight,
        value_output_weight,
    )
    left_sum, right_sum, grads, grad_modulation = meet(left_sum, right_sum, grads, grad_modulation)
    attention_sum = comm.begin(*grads)
    right_sum = comm.step(right_sum[0], "y"), comm.step(right_sum[1], "x")
    left_piece = comm.last(*left_sum)
    attention_sum, right_sum, left_piece = meet(attention_sum, right_sum, left_piece)
    right_begun, attention_sum = meet(comm.last_begin(*right_sum), attention_sum)
    right_piece = comm.last_end(right_begun)
    first_sum = comm.step(attention_sum, "x", 0, 2)
    second_sum = comm.step(attention_sum, "y", 2, 2)
    first_sum, second_sum, right_piece = meet(first_sum, second_sum, right_piece)

    owner = comm.owner_index()
    own_expand, own_shrink = expand_moment, shrink_moment.T
    wide_feed = [
        [
            (
                (piece, ((which,), 0, half)),
                (own_shrink, ((), side * half, half))
                if which == 2
                else (own_expand, ((which,), side * half, half)),
            )
            for side, piece in enumerate((left_piece, right_piece))
        ]
        for which in range(3)
    ]
    wide = comm.to_owners(comm.wide_slots_of(wide_feed))
    first_sum = comm.step(first_sum, "y")
    second_sum = comm.step(second_sum, "x")
    first_sum, second_sum, wide = meet(first_sum, second_sum, wide)
    wide = comm.wide_halves(wide)
    attention_piece, wide = meet(comm.last(first_sum, second_sum), wide)
    own_modulation, own_projection, own_output = modulation_moment, projection_moment, output_moment
    square_feed = [[(None, (own_modulation, ((k,), 0, D)))] for k in range(6)]
    for k in range(3):
        square_feed.append(
            [((attention_piece, ((k,), 0, D)), (own_projection, ((k,), 0, D)))]
        )
    square_feed.append([((attention_piece, ((3,), 0, D)), (own_output, ((), 0, D)))])
    slots = comm.square_slots(square_feed, grad_modulation)
    wide = comm.wide_whole(wide)
    active_wide = pick([0 if slot is None else 1 for slot in comm.wide_slots], owner)
    wide_done = newton_schulz(active_wide, wide)
    slots, left_piece, right_piece, attention_piece = meet(
        slots, left_piece, right_piece, attention_piece
    )
    pieces = [(left_piece, (i,), half) for i in range(3)]
    pieces += [(right_piece, (i,), half) for i in range(3)]
    pieces += [(attention_piece, (i,), D) for i in range(4)]
    totals_low = comm.complete_begin(pack(pieces))
    square, gathered, (wide_done, totals_low) = comm.square_to_owners(slots, (wide_done, totals_low))
    active_all = gathered[:, 6]
    item = pick([-1 if slot is None else slot for slot in comm.slots], owner)
    which = jnp.where((item >= 0) & (item < 6), item, 0)
    right = lax.dynamic_index_in_dim(gathered, which, 1, keepdims=False)
    right = jnp.where(item < 6, right, jnp.zeros_like(right))
    square_done = newton_schulz((item >= 0).astype(jnp.int32), square, active_all, right)
    size = FF // comm.wide_parts
    part = pick([0 if slot is None else slot[1] for slot in comm.wide_slots], owner)
    mine = lax.dynamic_slice_in_dim(wide_done, part * size, size, 1)
    mine = mine + jnp.pad(square_done, ((0, 0), (0, size - D)))
    back = comm.to_rows(mine)

    totals_low = comm.complete_end(totals_low).astype(F32)
    by_unit = [
        jnp.concatenate(
            [totals_low[:, (side * 3 + i) * half : (side * 3 + i + 1) * half] for side in range(2)],
            axis=1,
        )
        for i in range(3)
    ]
    steps = [
        (back, (comm.wide_slots.index((i, p)),), size) for i in range(3) for p in range(comm.wide_parts)
    ]
    steps += [(back, (comm.slots.index(i),), D) for i in range(10)]
    updated = update(*comm.quarters(pack(steps)), masters)
    active_rows = lax.dynamic_slice_in_dim(active_all, row_index * rows, rows, 1)
    modulation_total = jnp.einsum(
        "bd,bke->kde",
        active_rows,
        gathered[:, :6],
        preferred_element_type=F32,
    )
    after = 3 * FF
    totals = (
        modulation_total,
        jnp.stack([totals_low[:, after + i * D : after + (i + 1) * D] for i in range(3)]),
        totals_low[:, after + 3 * D :],
        jnp.stack(by_unit[:2]),
        by_unit[2].T,
    )
    states = tuple((MOMENTUM_DECAY * moment + total for moment, total in zip(moments, totals)))
    return (block_output, input_gradient, *totals, *updated, *states)


def solution(mesh):
    if mesh.shape["dp"] == 4 and mesh.shape["fsdp"] == 8:
        comm = Torus(mesh)
    else:
        comm = Plain(mesh)
    images, rows = comm.images, comm.rows
    by_row = (
        P(None, rows, None),
        P(None, rows, None),
        P(rows, None),
        P(None, rows, None),
        P(None, rows),
    )
    return jax.shard_map(
        functools.partial(local, comm),
        mesh=comm.mesh,
        in_specs=(
            P(images, None, None),
            P(images, None, None),
            P(images, None),
            P(images),
            P(),
            *by_row,
            *by_row,
        ),
        out_specs=(P(images, None, None), P(images, None, None), *by_row, *by_row, *by_row),
        check_vma=False,
    )
```

```python
import functools
import itertools

import jax
import jax.numpy as jnp
from jax import lax
from jax.experimental import pallas as pl
from jax.experimental.pallas import tpu as pltpu
from jax.sharding import Mesh, PartitionSpec as P

D = 768
HEADS = 12
HDIM = 64
FF = 2048
NS_ITERS = 5
NORM_EPS = 1e-06
FROBENIUS_EPS = 1e-07
COEFF_FIRST = 3.4445
COEFF_SECOND = -4.775
COEFF_THIRD = 2.0315
MOMENTUM_DECAY = 0.9
LEARN_RATE = 1.0
HIGHEST = lax.Precision.HIGHEST
BF16 = jnp.bfloat16
F32 = jnp.float32
ITEMS = 13
NT = (((1,), (1,)), ((), ()))
NN = (((1,), (0,)), ((), ()))
TN = (((0,), (0,)), ((), ()))


def dot(a, b, dims=NN):
    return lax.dot_general(a, b, dims, preferred_element_type=F32)


def newton_schulz_kernel(width, active_ref, feed_ref, left_ref, right_ref, out_ref, x, xb, gram, low, poly):
    tile = 256
    tiles = D // tile
    blocks = width // tile
    spans = [slice(i * tile, (i + 1) * tile) for i in range(tiles)]

    def diagonal(part, other):
        rows = lax.broadcasted_iota(jnp.int32, (tile, tile), 0)
        cols = lax.broadcasted_iota(jnp.int32, (tile, tile), 1)
        return jnp.where(rows == cols, part, other)

    def block(b):
        return pl.ds(pl.multiple_of(b * tile, tile), tile)

    @pl.when(active_ref[0] != 0)
    def _():
        def load(b, acc):
            if len(feed_ref.shape) == 3:
                per = feed_ref.shape[2] // tile
                v = feed_ref[b // per, :, block(lax.rem(b, per))].astype(F32)
            else:
                v = feed_ref[:, block(b)].astype(F32)
            if right_ref is not None:
                v = v + (1.0 + MOMENTUM_DECAY) * dot(left_ref[...], right_ref[:, block(b)], TN)
            x[:, block(b)] = v
            return acc + jnp.sum(v * v, axis=0, keepdims=True)

        total = lax.fori_loop(0, blocks, load, jnp.zeros((1, tile), F32))
        total = jnp.sum(total, keepdims=True)
        inverse = 1.0 / (jnp.sqrt(total) + FROBENIUS_EPS)

        def scale_block(b, carry):
            v = x[:, block(b)] * inverse
            x[:, block(b)] = v
            xb[:, block(b)] = v.astype(BF16)
            return carry

        lax.fori_loop(0, blocks, scale_block, 0)

        def iterate(step, carry):
            trace = jnp.zeros((1, tile), F32)
            for i in range(tiles):
                for j in range(i + 1):
                    part = dot(xb[spans[i], :], xb[spans[j], :], NT)
                    gram[spans[i], spans[j]] = part
                    if i == j:
                        trace = trace + jnp.sum(diagonal(part, 0.0), axis=0, keepdims=True)
                    else:
                        lower = part.astype(BF16)
                        low[spans[i], spans[j]] = lower
                        low[spans[j], spans[i]] = lower.T
            shift = jnp.sum(trace, keepdims=True) / D
            for i in range(tiles):
                part = gram[spans[i], spans[i]]
                part = diagonal(part - shift, part)
                gram[spans[i], spans[i]] = part
                low[spans[i], spans[i]] = part.astype(BF16)
            linear = COEFF_SECOND + 2.0 * COEFF_THIRD * shift
            level = COEFF_SECOND * shift + COEFF_THIRD * shift * shift
            trace = jnp.zeros((1, tile), F32)
            for i in range(tiles):
                for j in range(i + 1):
                    part = linear * gram[spans[i], spans[j]] + COEFF_THIRD * dot(
                        low[spans[i], :], low[spans[j], :], NT
                    )
                    if i == j:
                        gram[spans[i], spans[j]] = part
                        trace = trace + jnp.sum(diagonal(part, 0.0), axis=0, keepdims=True)
                    else:
                        lower = part.astype(BF16)
                        poly[spans[i], spans[j]] = lower
                        poly[spans[j], spans[i]] = lower.T
            mean = jnp.sum(trace, keepdims=True) / D
            for i in range(tiles):
                part = gram[spans[i], spans[i]]
                poly[spans[i], spans[i]] = diagonal(part - mean, part).astype(BF16)
            scale = COEFF_FIRST + level + mean

            size = width // 2 if width > 1024 else width
            for b in range(width // size):
                cols = slice(b * size, (b + 1) * size)
                new = scale * x[:, cols] + dot(poly[...], xb[:, cols])
                x[:, cols] = new
                xb[:, cols] = new.astype(BF16)
            return carry

        lax.fori_loop(0, NS_ITERS, iterate, 0)
        out_ref[...] = xb[...]

    @pl.when(active_ref[0] == 0)
    def _():
        out_ref[...] = jnp.zeros_like(out_ref)


def newton_schulz(active, feed, left=None, right=None):
    width = feed.size // D
    operands = [active.reshape(1).astype(jnp.int32), feed]
    if left is None:

        def body(active_ref, feed_ref, *rest):
            newton_schulz_kernel(width, active_ref, feed_ref, None, None, *rest)

    else:
        body = functools.partial(newton_schulz_kernel, width)
        operands += [left, right]
    vmem = pl.BlockSpec(memory_space=pltpu.VMEM)
    return pl.pallas_call(
        body,
        out_shape=jax.ShapeDtypeStruct((D, width), BF16),
        in_specs=[pl.BlockSpec(memory_space=pltpu.SMEM)] + [vmem] * (len(operands) - 1),
        out_specs=vmem,
        scratch_shapes=[
            pltpu.VMEM((D, width), F32),
            pltpu.VMEM((D, width), BF16),
            pltpu.VMEM((D, D), F32),
            pltpu.VMEM((D, D), BF16),
            pltpu.VMEM((D, D), BF16),
        ],
        compiler_params=pltpu.CompilerParams(vmem_limit_bytes=40 * 1024 * 1024),
        cost_estimate=pl.CostEstimate(
            flops=NS_ITERS * 4 * D * D * (width + D), bytes_accessed=4 * D * width, transcendentals=0
        ),
        name="newton_schulz",
    )(*operands)


def tie(value, *others):
    return lax.optimization_barrier((value, *others))[0]


def meet(*values):
    flat, tree = jax.tree.flatten(values)
    return jax.tree.unflatten(tree, lax.optimization_barrier(tuple(flat)))


def fold(mine, other, here, view, start, count):
    before, after = view
    rows, cols = mine.shape[-2:]
    shape = (mine.shape[0], before, 2, after, rows, cols)
    block = pl.BlockSpec((1, *shape[1:]), lambda k: (start + k, 0, 0, 0, 0, 0))
    out = jax.ShapeDtypeStruct((count, before, after, rows, cols), BF16)
    out_block = pl.BlockSpec((1, *out.shape[1:]), lambda k: (k, 0, 0, 0, 0))

    def body(here_ref, mine_ref, other_ref, keep_ref, send_ref):
        here = here_ref[0]
        for ref, at in ((send_ref, 1 - here), (keep_ref, here)):
            ref[0] = (mine_ref[0, :, at].astype(F32) + other_ref[0, :, at].astype(F32)).astype(BF16)

    size = 6 * count * before * after * rows * cols * 2
    keep, send = pl.pallas_call(
        body,
        grid=(count,),
        out_shape=(out, out),
        in_specs=[pl.BlockSpec(memory_space=pltpu.SMEM), block, block],
        out_specs=(out_block, out_block),
        compiler_params=pltpu.CompilerParams(vmem_limit_bytes=24 * 1024 * 1024),
        cost_estimate=pl.CostEstimate(flops=0, bytes_accessed=size, transcendentals=0),
        name="fold",
    )(
        here.reshape(1).astype(jnp.int32),
        pltpu.with_memory_space_constraint(mine.reshape(shape), pltpu.HBM)
        if before * after > 4
        else mine.reshape(shape),
        other.reshape(shape),
    )
    flat = lambda v: v.reshape(count, before * after, rows, cols)
    return flat(keep), flat(send)


def fold_last(states, here):
    rows, cols = states[0][0].shape[-2:]
    counts = [mine.shape[0] for mine, _ in states]
    k = sum(counts)

    def body(here_ref, *refs):
        ins, outs = refs[: 2 * len(states)], refs[2 * len(states) :]
        for by, ref in enumerate(outs):
            at = lax.rem(here_ref[0] + by, 4)
            start = 0
            for i, count in enumerate(counts):
                total = ins[2 * i][:, at].astype(F32) + ins[2 * i + 1][:, at].astype(F32)
                ref[start : start + count] = total.astype(ref.dtype)
                start += count

    vmem = pl.BlockSpec(memory_space=pltpu.VMEM)
    return pl.pallas_call(
        body,
        out_shape=(jax.ShapeDtypeStruct((k, rows, cols), F32),)
        + (jax.ShapeDtypeStruct((k, rows, cols), BF16),) * 3,
        in_specs=[pl.BlockSpec(memory_space=pltpu.SMEM)] + [vmem] * (2 * len(states)),
        out_specs=(vmem,) * 4,
        compiler_params=pltpu.CompilerParams(vmem_limit_bytes=24 * 1024 * 1024),
        cost_estimate=pl.CostEstimate(
            flops=0, bytes_accessed=28 * k * rows * cols, transcendentals=0
        ),
        name="fold_last",
    )(here.reshape(1).astype(jnp.int32), *[part for state in states for part in state])


def place(parts, slots, lead=None, moves=None):
    count = len(parts)
    if lead is None:
        lead = (count, *parts[0].shape[:-2])
        moves = lambda slot: [(i, (), (slot[i],)) for i in range(count)]

    def body(slot_ref, *refs):
        ins, out = refs[:count], refs[count]
        for part, source, target in moves(slot_ref):
            out[target] = ins[part][source] if source else ins[part][...]

    size = count * parts[0].size * parts[0].dtype.itemsize
    vmem = pl.BlockSpec(memory_space=pltpu.VMEM)
    return pl.pallas_call(
        body,
        out_shape=jax.ShapeDtypeStruct((*lead, *parts[0].shape[-2:]), parts[0].dtype),
        in_specs=[pl.BlockSpec(memory_space=pltpu.SMEM)] + [vmem] * count,
        out_specs=vmem,
        cost_estimate=pl.CostEstimate(flops=0, bytes_accessed=2 * size, transcendentals=0),
        compiler_params=pltpu.CompilerParams(vmem_limit_bytes=24 * 1024 * 1024),
        name="place",
    )(jnp.stack(slots).astype(jnp.int32), *parts)


def place_halves(parts, slots):
    count = len(parts)
    rows, cols = parts[0].shape
    half = cols // 2

    def body(slot_ref, *refs):
        left, right = refs[count:]
        for i, ref in enumerate(refs[:count]):
            left[slot_ref[i]] = ref[:, :half]
            right[slot_ref[i]] = ref[:, half:]

    vmem = pl.BlockSpec(memory_space=pltpu.VMEM)
    shape = jax.ShapeDtypeStruct((count, rows, half), parts[0].dtype)
    return pl.pallas_call(
        body,
        out_shape=(shape, shape),
        in_specs=[pl.BlockSpec(memory_space=pltpu.SMEM)] + [vmem] * count,
        out_specs=(vmem, vmem),
        cost_estimate=pl.CostEstimate(flops=0, bytes_accessed=16 * rows * cols, transcendentals=0),
        compiler_params=pltpu.CompilerParams(vmem_limit_bytes=24 * 1024 * 1024),
        name="place_halves",
    )(jnp.stack(slots).astype(jnp.int32), *parts)


def slots_of(feeds, owners, width, quarter, extra=None):
    more = 0 if extra is None else extra.shape[0]
    arrays, index = [], {}

    def note(array):
        if array is None:
            return None
        source, columns = array
        if id(source) not in index:
            index[id(source)] = len(arrays)
            arrays.append(source)
        return (index[id(source)], columns)

    noted = [[(note(total), note(moment)) for total, moment in feed] for feed in feeds]
    rows = arrays[0].shape[-2]
    for total, _ in sum(feeds, []):
        if total is not None:
            rows = total[0].shape[-2]
    if all(total is None or total[0].shape[-2] == moment[0].shape[-2] for total, moment in sum(feeds, [])):
        quarter = jnp.int32(0)

    def block(array):
        shape = (*array.shape[:-2], rows, array.shape[-1])
        lead = (0,) * (array.ndim - 2)
        if array.shape[-2] == rows:
            return pl.BlockSpec(shape, lambda i, q: (*lead, 0, 0))
        return pl.BlockSpec(shape, lambda i, q: (*lead, q[0], 0))

    def body(_, *refs):
        out = refs[-1]
        if more:
            out = refs[-1].at[:, :rows]
            for slot in range(owners):
                refs[-1][slot, rows:] = refs[-2][...]

        def read(what):
            place_of, (lead, start, size) = what
            ref = refs[place_of]
            return ref[(*lead, slice(None), slice(start, start + size))].astype(F32)

        first = {}
        for slot in range(owners):
            if not noted[slot]:
                out[slot] = jnp.zeros((rows, width), BF16)
                continue
            key = str(noted[slot])
            if key in first:
                out[slot] = out[first[key]]
                continue
            first[key] = slot
            at = 0
            for total, moment in noted[slot]:
                value = MOMENTUM_DECAY * MOMENTUM_DECAY * read(moment)
                if total is not None:
                    value = value + (1.0 + MOMENTUM_DECAY) * read(total)
                out[slot, :, at : at + value.shape[1]] = value.astype(BF16)
                at += value.shape[1]

    return pl.pallas_call(
        body,
        out_shape=jax.ShapeDtypeStruct((owners, rows + more, width), BF16),
        grid_spec=pltpu.PrefetchScalarGridSpec(
            num_scalar_prefetch=1,
            grid=(1,),
            in_specs=[block(array) for array in arrays]
            + [pl.BlockSpec((more, width), lambda i, q: (0, 0))] * (more > 0),
            out_specs=pl.BlockSpec((owners, rows + more, width), lambda i, q: (0, 0, 0)),
        ),
        cost_estimate=pl.CostEstimate(
            flops=0, bytes_accessed=2 * owners * rows * width, transcendentals=0
        ),
        compiler_params=pltpu.CompilerParams(vmem_limit_bytes=24 * 1024 * 1024),
        name="slots",
    )(
        quarter.reshape(1).astype(jnp.int32),
        *[
            array
            if array.shape[-2] == rows
            else pltpu.with_memory_space_constraint(array, pltpu.HBM)
            for array in arrays
        ],
        *([extra] if more else []),
    )


def pack(parts):
    arrays, index = [], {}
    for array, _, _ in parts:
        if id(array) not in index:
            index[id(array)] = len(arrays)
            arrays.append(array)
    rows = arrays[0].shape[-2]
    total = sum(cols for _, _, cols in parts)

    def body(*refs):
        at = 0
        for array, lead, cols in parts:
            value = refs[index[id(array)]][(*lead, slice(None), slice(0, cols))]
            refs[-1][:, at : at + cols] = value.astype(BF16)
            at += cols

    vmem = pl.BlockSpec(memory_space=pltpu.VMEM)
    return pl.pallas_call(
        body,
        out_shape=jax.ShapeDtypeStruct((rows, total), BF16),
        in_specs=[vmem] * len(arrays),
        out_specs=vmem,
        cost_estimate=pl.CostEstimate(flops=0, bytes_accessed=6 * rows * total, transcendentals=0),
        compiler_params=pltpu.CompilerParams(vmem_limit_bytes=24 * 1024 * 1024),
        name="pack",
    )(*arrays)


def pick(values, index):
    found = jnp.int32(values[0])
    for i, value in enumerate(values):
        if value != values[0]:
            found = jnp.where(index == i, jnp.int32(value), found)
    return found


def update_kernel(quarters, slot_ref, *refs):
    step_refs, refs = refs[:quarters], refs[quarters:]
    modulation, projection, output, expand, shrink = refs[:5]
    out_modulation, out_projection, out_output, out_expand, out_shrink = refs[5:10]
    quarter = pl.program_id(0)
    rows = step_refs[0].shape[0]
    ratio = LEARN_RATE * (FF / D) ** 0.5
    for which, steps in enumerate(step_refs):

        @pl.when(slot_ref[quarter] == which)
        def _(steps=steps):
            at = 3 * FF
            for k in range(2):
                step = steps[:, k * FF : (k + 1) * FF].astype(F32)
                out_expand[k] = expand[k] - ratio * step
            out_shrink[...] = shrink[...] - LEARN_RATE * steps[:, 2 * FF : at].astype(F32)
            for master, out, count in (
                (modulation, out_modulation, 6),
                (projection, out_projection, 3),
            ):
                for k in range(count):
                    out[k] = master[k] - LEARN_RATE * steps[:, at : at + D].astype(F32)
                    at += D
            out_output[...] = output[...] - LEARN_RATE * steps[:, at : at + D].astype(F32)


def update(slots, steps, masters):
    quarters = len(steps)
    rows = steps[0].shape[0]
    third = lambda a: pl.BlockSpec((a.shape[0], rows, a.shape[2]), lambda q: (0, q, 0))
    masters = (*masters[:4], masters[4].T)
    modulation, projection, output, expand, shrink = masters
    specs = [
        third(modulation),
        third(projection),
        pl.BlockSpec((rows, D), lambda q: (q, 0)),
        third(expand),
        pl.BlockSpec((rows, FF), lambda q: (q, 0)),
    ]
    updated = pl.pallas_call(
        functools.partial(update_kernel, quarters),
        grid=(quarters,),
        out_shape=tuple(jax.ShapeDtypeStruct(a.shape, F32) for a in masters),
        in_specs=[pl.BlockSpec(memory_space=pltpu.SMEM)] + [whole(a) for a in steps] + specs,
        out_specs=tuple(specs),
        cost_estimate=pl.CostEstimate(flops=0, bytes_accessed=14_000_000, transcendentals=0),
        compiler_params=pltpu.CompilerParams(vmem_limit_bytes=24 * 1024 * 1024),
        name="update",
    )(
        jnp.stack(slots).astype(jnp.int32),
        *steps,
        *[pltpu.with_memory_space_constraint(a, pltpu.HBM) for a in masters],
    )
    return (*updated[:4], updated[4].T)


def every(*sizes):
    return list(itertools.product(*[range(size) for size in sizes]))


class Plain:
    images = ("dp", "fsdp")
    rows = "fsdp"
    wide_parts = 1

    def __init__(self, mesh):
        self.mesh = mesh
        self.row_shards = mesh.shape["fsdp"]
        self.owners = mesh.shape["fsdp"]
        self.wide_slots = [(i, 0) for i in range(3)]
        self.wide_slots += [None] * (self.owners - 3)
        self.slots = [None] * 3 + list(range(10))
        self.slots += [None] * (self.owners - ITEMS)

    def row_index(self):
        return lax.axis_index("fsdp")

    def group_index(self):
        return lax.axis_index("dp")

    def owner_index(self):
        return lax.axis_index("fsdp")

    def gather_weights(self, first, second, modulate, attend):
        full = [lax.all_gather(chunk, "fsdp", axis=0, tiled=True) for chunk in (first, second)]
        first, second = [jnp.split(chunk, 2, axis=1) for chunk in full]
        modulation = modulate[1](modulate[0]())
        return first, second, modulation, attend(first, modulation)

    def to_group(self, value):
        return lax.all_to_all(value, "fsdp", split_axis=0, concat_axis=0, tiled=True)

    def halves(self):
        return jnp.int32(0)

    def begin(self, mine, send):
        k, n, rows, cols = mine.shape
        return (jnp.stack([mine, send], axis=2).reshape(k, 2 * n * rows, cols),)

    def step(self, state, axis, start=0, count=None):
        return (state[0][start : start + (count or state[0].shape[0])],)

    def last_begin(self, *states):
        return states

    def last_end(self, states):
        return self.last(*states)

    def last(self, *states):
        value = jnp.concatenate([state[0] for state in states], axis=0)
        shard = lax.psum_scatter(value, "fsdp", scatter_dimension=1, tiled=True)
        return lax.psum(shard.astype(F32), "dp")

    def own_rows(self, shard, dim=-2):
        return shard

    def complete_begin(self, piece):
        return piece

    def complete_end(self, piece):
        return piece

    def quarters(self, piece):
        return [jnp.int32(0)], [piece]

    def to_owners(self, pieces):
        got = lax.all_to_all(pieces, "fsdp", split_axis=0, concat_axis=0, tiled=True)
        return got.reshape(-1, got.shape[2])

    def wide_slots_of(self, feeds):
        return slots_of(
            [[] if slot is None else feeds[slot[0]] for slot in self.wide_slots],
            self.owners,
            FF,
            jnp.int32(0),
        )

    def wide_halves(self, got):
        return got

    def wide_whole(self, got):
        return jnp.stack(jnp.split(got, 2, axis=1))

    def square_slots(self, feeds, rows):
        return (
            slots_of(
                [[] if slot is None else feeds[slot] for slot in self.slots],
                self.owners,
                D,
                self.group_index(),
            ),
            rows,
        )

    def square_to_owners(self, slots, beside):
        pieces, rows = slots
        rows = lax.all_gather(rows, ("dp", "fsdp"), axis=0, tiled=True)
        return self.to_owners(pieces), rows, beside

    def to_rows(self, whole):
        blocks = whole.reshape(self.row_shards, -1, whole.shape[1])
        return lax.all_to_all(blocks, "fsdp", split_axis=0, concat_axis=0, tiled=True)


class Torus:
    images = ("x", "c", "z", "y")
    rows = ("z", "y")
    chips = ("x", "z", "y")
    wide_parts = 2

    def __init__(self, mesh):
        self.mesh = Mesh(mesh.devices.reshape(2, 2, 4, 2), ("x", "c", "z", "y"))
        self.row_shards = 8
        self.owners = 16
        wide_places = [(1, 0), (2, 1), (1, 1)]
        self.wide_slots = [None] * 16
        self.slots = [None] * 16
        for item, (z, y) in enumerate(wide_places):
            for part in range(2):
                self.wide_slots[(part * 4 + z) * 2 + y] = (item, part)
        free = [i for i in range(16) if self.wide_slots[i] is None]
        for item, slot in enumerate(free):
            self.slots[slot] = item

    def row_index(self):
        return lax.axis_index("z") * 2 + lax.axis_index("y")

    def group_index(self):
        return lax.axis_index("x") * 2 + lax.axis_index("c")

    def owner_index(self):
        return (lax.axis_index("x") * 4 + lax.axis_index("z")) * 2 + lax.axis_index("y")

    def swap(self, value, axis):
        return lax.ppermute(value, axis, [(0, 1), (1, 0)])

    def shift(self, value, by):
        return lax.ppermute(value, "z", [(i, (i + by) % 4) for i in range(4)])

    def exchange(self, value, axis):
        here = lax.axis_index(axis)
        return place([value, self.swap(value, axis)], [here, 1 - here])

    def spread_z(self, value):
        z = lax.axis_index("z")
        ring = [value] + [self.shift(value, by) for by in range(1, 4)]
        return place(ring, [(z - by) % 4 for by in range(4)])

    def gather_weights(self, first, second, modulate, attend):
        x, y, z, c = [lax.axis_index(axis) for axis in "xyzc"]
        slots = [(z - by) % 4 for by in range(4)]

        def ring_of(chunk, *others):
            piece = self.own_rows(chunk)
            if others:
                piece = tie(piece, *others)
            return [piece] + [self.shift(piece, by) for by in range(1, 4)]

        def one_hop(left, right):
            left_other, right_other = self.swap(left, "y"), self.swap(right, "x")
            left = place([left, left_other], [y, 1 - y])
            right = place([right, right_other], [x, 1 - x])
            return left, right

        def other_hop(left, right):
            left, right = meet(left, right)
            left_other, right_other = meet(self.swap(left, "x"), self.swap(right, "y"))
            left = place([left, left_other], [x, 1 - x])
            right = place([right, right_other], [y, 1 - y])
            return left, right

        def by_core(left, right):
            others = self.swap(left, "c"), self.swap(right, "c")
            pair = []
            for half, other, order in ((left, others[0], (2, 1, 0)), (right, others[1], (2, 0, 1))):

                def moves(slot, order=order):
                    found = []
                    for part in range(2):
                        for at in every(2, 2, 4):
                            found.append((part, at, (*[at[i] for i in order], slot[part])))
                    return found

                pair.append(place([half, other], [c, 1 - c], (4, 2, 2, 2), moves).reshape(D, -1))
            return pair

        group = modulate[0]()
        left, right = place_halves(ring_of(first), slots)
        left, right, group = meet(left, right, group)
        ring = ring_of(second, left, right)
        left, right = one_hop(left, right)
        left, right, ring[0], ring[1], ring[3] = meet(left, right, ring[0], ring[1], ring[3])
        left, right = other_hop(left, right)
        modulation = modulate[1](group)
        left, right, ring[2] = meet(left, right, ring[2])
        second_left, second_right = place_halves(ring, slots)
        others = self.swap(second_left, "y"), self.swap(second_right, "x")
        done = by_core(left, right)
        done, others, modulation = meet(done, others, modulation)
        left = place([second_left, others[0]], [y, 1 - y])
        right = place([second_right, others[1]], [x, 1 - x])
        left, right = meet(left, right)
        others = self.swap(left, "x"), self.swap(right, "y")
        done, left, right = meet(done, left, right)
        results = attend(done, modulation)
        left_other, right_other, results = meet(*others, results)
        left = place([left, left_other], [x, 1 - x])
        right = place([right, right_other], [y, 1 - y])
        return done, by_core(left, right), modulation, results

    def to_group(self, value):
        return lax.all_to_all(value, ("z", "y"), split_axis=0, concat_axis=0, tiled=True)

    def halves(self):
        return lax.axis_index("c")

    def begin(self, mine, send):
        return (mine, self.swap(send, "c"))

    def step(self, state, axis, start=0, count=None):
        mine, other = state
        parts = mine.shape[1]
        view = (4, 2) if (parts, axis) == (16, "y") else (parts // 2, 1)
        keep, send = fold(
            mine, other, lax.axis_index(axis), view, start, count or mine.shape[0]
        )
        return (keep, self.swap(send, axis))

    def last(self, *states):
        return self.last_end(self.last_begin(*states))

    def last_begin(self, *states):
        return fold_last(states, lax.axis_index("z"))

    def last_end(self, folded):
        total, *sends = folded
        for by, send in enumerate(sends, 1):
            total = total + self.shift(send, by).astype(F32)
        return total

    def own_rows(self, shard, dim=-2):
        return lax.dynamic_slice_in_dim(
            shard, self.group_index() * (D // 32), D // 32, dim % shard.ndim
        )

    def quarters(self, piece):
        x, c = lax.axis_index("x"), lax.axis_index("c")
        by_x = self.swap(piece, "x")
        by_c = self.swap(piece, "c")
        by_both = self.swap(by_x, "c")
        slots = []
        for at_x, at_c in every(2, 2):
            slots.append(jnp.where(at_x == x, 0, 1) + jnp.where(at_c == c, 0, 2))
        return slots, [piece, by_x, by_c, by_both]

    def complete_begin(self, piece):
        return piece, self.swap(piece, "x")

    def complete_end(self, pair):
        x, c = lax.axis_index("x"), lax.axis_index("c")
        value = place(list(pair), [x, 1 - x])
        moves = lambda slot: [(part, (x,), (x, slot[part])) for part in range(2) for x in range(2)]
        value = place([value, self.swap(value, "c")], [c, 1 - c], (2, 2), moves)
        return value.reshape(D // 8, -1)

    def to_owners(self, pieces):
        return lax.all_to_all(pieces, self.chips, split_axis=0, concat_axis=0, tiled=True)

    def wide_slots_of(self, feeds):
        halved = []
        for slot in self.wide_slots:
            halved.append([] if slot is None else [feeds[slot[0]][slot[1]]])
        return slots_of(halved, self.owners, FF // 2, self.group_index())

    def wide_halves(self, got):
        return got, self.swap(got, "x")

    def wide_whole(self, got):
        half = FF // 2
        x, c = lax.axis_index("x"), lax.axis_index("c")
        both = place(list(got), [x, 1 - x])
        both = both.reshape(2, 2, 4, 2, D // 32, half)

        def moves(slot):
            return [
                (part, (p, x, z, y), (p, z, y, x, slot[part]))
                for part in range(2)
                for p, x, z, y in every(2, 2, 4, 2)
            ]

        whole = place([both, self.swap(both, "c")], [c, 1 - c], (2, 4, 2, 2, 2), moves)
        return whole.reshape(2, D, half)

    def square_slots(self, feeds, rows):
        return slots_of(
            [[] if slot is None else feeds[slot] for slot in self.slots],
            self.owners,
            D,
            self.group_index(),
            rows.reshape(-1, D),
        )

    def square_to_owners(self, slots, beside):
        quarter = D // 32
        got = self.to_owners(slots)
        got, beside = meet(got, beside)
        other = self.swap(got, "c")
        more = got.shape[1] - quarter

        def body(c_ref, mine_ref, other_ref, whole_ref, rows_ref):
            c = c_ref[0]
            for ref, at in ((mine_ref, c), (other_ref, 1 - c)):
                for chip, (x, z, y) in enumerate(every(2, 4, 2)):
                    whole_ref[z, y, x, at] = ref[chip, :quarter]
                    rows_ref[at, chip] = ref[chip, quarter:]

        vmem = pl.BlockSpec(memory_space=pltpu.VMEM)
        square, gathered = pl.pallas_call(
            body,
            out_shape=(
                jax.ShapeDtypeStruct((4, 2, 2, 2, quarter, D), BF16),
                jax.ShapeDtypeStruct((2, 16, more, D), BF16),
            ),
            in_specs=[pl.BlockSpec(memory_space=pltpu.SMEM), vmem, vmem],
            out_specs=(vmem, vmem),
            cost_estimate=pl.CostEstimate(
                flops=0, bytes_accessed=8 * got.size, transcendentals=0
            ),
            compiler_params=pltpu.CompilerParams(vmem_limit_bytes=24 * 1024 * 1024),
            name="place_square",
        )(lax.axis_index("c").reshape(1).astype(jnp.int32), got, other)
        return square.reshape(D, D), gathered.reshape(-1, 8, D), beside

    def to_rows(self, whole):
        cols = whole.shape[1]
        blocks = whole.reshape(4, 2, 2, 2, D // 32, cols)
        blocks = lax.dynamic_index_in_dim(blocks, lax.axis_index("c"), 3, keepdims=False)
        blocks = blocks.transpose(2, 0, 1, 3, 4).reshape(16, D // 32, cols)
        return lax.all_to_all(blocks, self.chips, split_axis=0, concat_axis=0, tiled=True)


def lanes(shape, dim):
    return lax.broadcasted_iota(jnp.int32, shape, dim)


def norm_of(values):
    centred = values - jnp.mean(values, axis=-1, keepdims=True)
    inverse = lax.rsqrt(jnp.mean(centred * centred, axis=-1, keepdims=True) + NORM_EPS)
    return centred * inverse, inverse


def norm_back(incoming, normed, inverse):
    return inverse * (
        incoming
        - jnp.mean(incoming, axis=-1, keepdims=True)
        - normed * jnp.mean(incoming * normed, axis=-1, keepdims=True)
    )


def rotate_pair(value):
    first = lanes(value.shape, 1) % 32 < 16
    return jnp.where(first, -pltpu.roll(value, 112, 1), pltpu.roll(value, 16, 1))


def two_heads(value):
    low = lanes(value.shape, 1) < HDIM
    zero = jnp.zeros_like(value)
    return jnp.where(low, value, zero), jnp.where(low, zero, value)


def pair_at(pair):
    return pl.ds(pl.multiple_of(pair * 2 * HDIM, 2 * HDIM), 2 * HDIM)


def attention_forward_kernel(
    length_ref,
    input_ref,
    cotangent_ref,
    modulation_ref,
    cosine_ref,
    sine_ref,
    query_key_ref,
    value_output_ref,
    first_ref,
    query_ref,
    key_ref,
    value_ref,
    probs_ref,
    attended_ref,
    attention_ref,
    middle_ref,
    second_ref,
    branch_ref,
):
    length = length_ref[pl.program_id(0)]
    row = lambda which: modulation_ref[0, which : which + 1, :]
    stream = input_ref[0].astype(F32)
    positions = stream.shape[0]
    normed, _ = norm_of(stream)
    first = (normed * (1.0 + row(1)) + row(0)).astype(BF16)
    first_ref[0] = first
    inside = lanes((positions, D), 0) < length
    upstream = jnp.where(inside, cotangent_ref[0].astype(F32), 0.0)
    branch_ref[0] = (row(5) * upstream).astype(BF16)
    value_ref[0] = dot(first, value_output_ref[:, :D]).astype(BF16)
    cosine, sine = cosine_ref[0], sine_ref[0]
    keep = lanes((positions, positions), 1) < length

    @pl.loop(0, HEADS // 2)
    def _(pair):
        at = pair_at(pair)
        query = dot(first, query_key_ref[:, at])
        key = dot(first, query_key_ref[:, pair_at(HEADS // 2 + pair)])
        query = (query * cosine + rotate_pair(query) * sine).astype(BF16)
        key = (key * cosine + rotate_pair(key) * sine).astype(BF16)
        query_ref[0, :, at] = query
        key_ref[0, :, at] = key
        low = []
        for head, masked in enumerate(two_heads(query)):
            scores = dot(masked, key, NT) * HDIM ** (-0.5)
            scores = jnp.where(keep, scores, -1000000000.0)
            exponent = jnp.exp(scores - jnp.max(scores, axis=-1, keepdims=True))
            probs = exponent * (1.0 / jnp.sum(exponent, axis=-1, keepdims=True))
            probs_ref[0, 2 * pair + head] = probs
            low.append(probs.astype(BF16))
        values = two_heads(value_ref[0, :, at])
        attended_ref[0, :, at] = dot(
            jnp.concatenate(low, axis=1), jnp.concatenate(values, axis=0)
        ).astype(BF16)

    attention = dot(attended_ref[0], value_output_ref[:, D:])
    attention_ref[0] = attention
    middle = stream + row(2) * attention
    middle_ref[0] = middle
    normed, _ = norm_of(middle)
    second_ref[0] = (normed * (1.0 + row(4)) + row(3)).astype(BF16)


def split_rows(value, scratch, here, keep_ref, send_ref, which, cols):
    scratch[...] = value
    rows = keep_ref.shape[2]
    for i in range(keep_ref.shape[1]):
        for ref, at in ((keep_ref, here), (send_ref, 1 - here)):
            start = pl.multiple_of((2 * i + at) * rows, 8)
            ref[which, i, :, cols] = scratch[pl.ds(start, rows), :].astype(BF16)


def feed_forward_kernel(
    here_ref,
    second_ref,
    branch_ref,
    gate_ref,
    up_ref,
    down_ref,
    out_ref,
    back_ref,
    keep_ref,
    send_ref,
    second_t,
    branch_t,
    rows,
):
    step = pl.program_id(0)

    @pl.when(step == 0)
    def _():
        second_t[...] = second_ref[...].T
        branch_t[...] = branch_ref[...].T
        out_ref[...] = jnp.zeros_like(out_ref)
        back_ref[...] = jnp.zeros_like(back_ref)

    gate, up, down = gate_ref[...], up_ref[...], down_ref[...]
    gate_pre = dot(second_ref[...], gate)
    up_pre = dot(second_ref[...], up)
    sigmoid = 1.0 / (1.0 + jnp.exp(-gate_pre))
    swish = gate_pre * sigmoid
    hidden = (swish * up_pre).astype(BF16)
    out_ref[...] += dot(hidden, down, NT)
    grad_hidden = dot(branch_ref[...], down)
    grad_gate = (grad_hidden * up_pre * sigmoid * (1.0 + gate_pre * (1.0 - sigmoid))).astype(BF16)
    grad_up = (grad_hidden * swish).astype(BF16)
    back_ref[...] += dot(grad_gate, gate, NT) + dot(grad_up, up, NT)
    everything = slice(None)
    products = ((second_t, grad_gate), (second_t, grad_up), (branch_t, hidden))
    for which, (left, right) in enumerate(products):
        split_rows(
            dot(left[...], right), rows, here_ref[0], keep_ref, send_ref, which, everything
        )


def attention_backward_kernel(
    length_ref,
    branch_left_ref,
    branch_right_ref,
    second_left_ref,
    second_right_ref,
    middle_ref,
    cotangent_ref,
    modulation_ref,
    attention_ref,
    value_output_ref,
    query_ref,
    key_ref,
    value_ref,
    probs_ref,
    cosine_ref,
    sine_ref,
    output_ref,
    stream_ref,
    grads_ref,
    sums_ref,
    attended_grad,
):
    length = length_ref[pl.program_id(0)]
    row = lambda which: modulation_ref[0, which : which + 1, :]
    middle = middle_ref[0]
    positions = middle.shape[0]
    inside = lanes((positions, D), 0) < length
    upstream = jnp.where(inside, cotangent_ref[0].astype(F32), 0.0)
    branch = branch_left_ref[0] + branch_right_ref[0]
    output_ref[0] = (middle + row(5) * branch).astype(BF16)
    total = lambda value: jnp.sum(value, axis=0, keepdims=True)
    gate_two = total(upstream * branch)
    second = second_left_ref[0] + second_right_ref[0]
    normed, inverse = norm_of(middle)
    scale_two = total(second * normed)
    shift_two = total(second)
    stream = upstream + norm_back(second * (1.0 + row(4)), normed, inverse)
    stream_ref[0] = stream
    gate_one = total(stream * attention_ref[0])
    blank = jnp.zeros_like(gate_one)
    sums_ref[0] = jnp.concatenate(
        [blank, blank, gate_one, shift_two, scale_two, gate_two, blank, blank], axis=0
    )
    grad_attention = (row(2) * stream).astype(BF16)
    grads_ref[3, 0] = grad_attention
    attended_grad[...] = dot(grad_attention, value_output_ref[:, D:], NT).astype(BF16)
    cosine, sine = cosine_ref[0], sine_ref[0]

    @pl.loop(0, HEADS // 2)
    def _(pair):
        at = pair_at(pair)
        query, key, value = query_ref[0, :, at], key_ref[0, :, at], value_ref[0, :, at]
        attended = two_heads(attended_grad[:, at])
        low, scores = [], []
        for head in range(2):
            probs = probs_ref[0, 2 * pair + head]
            grad_probs = dot(attended[head], value, NT)
            inner = jnp.sum(grad_probs * probs, axis=-1, keepdims=True)
            scores.append((probs * (grad_probs - inner)).astype(BF16))
            low.append(probs.astype(BF16))
        grads_ref[2, 0, :, at] = dot(
            jnp.concatenate(low, axis=0), jnp.concatenate(attended, axis=0), TN
        ).astype(BF16)
        grad_query = dot(
            jnp.concatenate(scores, axis=1), jnp.concatenate(two_heads(key), axis=0)
        ) * HDIM ** (-0.5)
        grad_key = dot(
            jnp.concatenate(scores, axis=0), jnp.concatenate(two_heads(query), axis=0), TN
        ) * HDIM ** (-0.5)
        grads_ref[0, 0, :, at] = (grad_query * cosine - rotate_pair(grad_query * sine)).astype(BF16)
        grads_ref[1, 0, :, at] = (grad_key * cosine - rotate_pair(grad_key * sine)).astype(BF16)


def projection_backward_kernel(
    here_ref,
    grads_in_ref,
    first_ref,
    attended_ref,
    input_ref,
    modulation_ref,
    stream_ref,
    sums_ref,
    active_ref,
    query_key_ref,
    value_output_ref,
    keep_ref,
    send_ref,
    input_grad_ref,
    modulation_grad_ref,
    first_t,
    first_grad,
    rows,
):
    images, positions = input_ref.shape[:2]
    tokens = images * positions
    flat = lambda ref: ref[...].reshape(tokens, D)
    step = pl.program_id(0)

    def product(grads):
        split_rows(dot(first_t[...], grads), rows, here_ref[0], keep_ref, send_ref, 0, slice(None))

    @pl.when(step == 0)
    def _():
        first_t[...] = flat(first_ref).T
        grads = grads_in_ref[0].reshape(tokens, D)
        product(grads)
        first_grad[...] = dot(grads, query_key_ref[:, :D], NT)

    @pl.when(step == 1)
    def _():
        grads = grads_in_ref[0].reshape(tokens, D)
        product(grads)
        first_grad[...] += dot(grads, query_key_ref[:, D:], NT)

    @pl.when(step == 2)
    def _():
        grads = grads_in_ref[0].reshape(tokens, D)
        product(grads)
        first_grad[...] += dot(grads, value_output_ref[:, :D], NT)

    @pl.when(step == 3)
    def _():
        first_t[...] = flat(attended_ref).T
        product(grads_in_ref[0].reshape(tokens, D))
        for image in range(images):
            at = slice(image * positions, (image + 1) * positions)
            normed, inverse = norm_of(input_ref[image].astype(F32))
            first = first_grad[at, :]
            scale_one = jnp.sum(first * normed, axis=0, keepdims=True)
            shift_one = jnp.sum(first, axis=0, keepdims=True)
            scaled = first * (1.0 + modulation_ref[image, 1:2, :])
            input_grad_ref[image] = stream_ref[image] + norm_back(scaled, normed, inverse)
            modulation_grad_ref[image] = jnp.concatenate(
                [
                    shift_one,
                    scale_one,
                    sums_ref[image, 2:6, :],
                    active_ref[image : image + 1, :].astype(F32),
                    jnp.zeros_like(shift_one),
                ],
                axis=0,
            ).astype(BF16)


BIG_VMEM = 58 * 1024 * 1024


def whole(array):
    return pl.BlockSpec(array.shape, lambda *_: (0,) * array.ndim)


def by_image(array):
    return pl.BlockSpec((1, *array.shape[1:]), lambda b: (b,) + (0,) * (array.ndim - 1))


def call(body, grid, ins, in_specs, outs, out_specs, scratch, flops, name):
    size = sum(a.size * a.dtype.itemsize for a in (*ins, *outs))
    return pl.pallas_call(
        body,
        grid=grid,
        out_shape=outs,
        in_specs=in_specs,
        out_specs=out_specs,
        scratch_shapes=scratch,
        compiler_params=pltpu.CompilerParams(vmem_limit_bytes=BIG_VMEM),
        cost_estimate=pl.CostEstimate(flops=flops, bytes_accessed=size, transcendentals=0),
        name=name,
    )(*ins)


def attention_forward(lengths, inputs, cotangent, modulation, cosine, sine, query_key, value_output):
    images, positions, _ = inputs.shape
    ins = (lengths, inputs, cotangent, modulation, cosine, sine, query_key, value_output)
    in_specs = [pl.BlockSpec(memory_space=pltpu.SMEM)]
    in_specs += [by_image(a) for a in ins[1:6]] + [whole(a) for a in ins[6:]]
    token = lambda dtype: jax.ShapeDtypeStruct((images, positions, D), dtype)
    outs = (
        token(BF16),
        token(BF16),
        token(BF16),
        token(BF16),
        jax.ShapeDtypeStruct((images, HEADS, positions, positions), F32),
        token(BF16),
        token(F32),
        token(F32),
        token(BF16),
        token(BF16),
    )
    flops = 2 * images * positions * D * (4 * D + 2 * positions)
    return call(
        attention_forward_kernel,
        (images,),
        ins,
        in_specs,
        outs,
        [by_image(a) for a in outs],
        [],
        flops,
        "attention_forward",
    )


def feed_forward(here, second, branch, weight):
    tokens = second.shape[0]
    units = weight.shape[1] // 3
    tile = 256
    steps = units // tile
    weight = pltpu.with_memory_space_constraint(weight, pltpu.HBM)
    ins = (here.reshape(1).astype(jnp.int32), second, branch, weight, weight, weight)
    in_specs = [pl.BlockSpec(memory_space=pltpu.SMEM), whole(second), whole(branch)] + [
        pl.BlockSpec((D, tile), lambda t, which=which: (0, which * steps + t)) for which in range(3)
    ]
    outs = (
        jax.ShapeDtypeStruct((tokens, D), F32),
        jax.ShapeDtypeStruct((tokens, D), F32),
        jax.ShapeDtypeStruct((3, D // 48, 24, units), BF16),
        jax.ShapeDtypeStruct((3, D // 48, 24, units), BF16),
    )
    out_specs = [whole(outs[0]), whole(outs[1])]
    out_specs += [pl.BlockSpec((3, D // 48, 24, tile), lambda t: (0, 0, 0, t))] * 2
    scratch = [pltpu.VMEM((D, tokens), BF16), pltpu.VMEM((D, tokens), BF16), pltpu.VMEM((D, tile), F32)]
    flops = 2 * 9 * tokens * D * units
    return call(
        feed_forward_kernel, (steps,), ins, in_specs, outs, out_specs, scratch, flops, "feed_forward"
    )


def attention_backward(lengths, *ins):
    images, positions, _ = ins[0].shape
    shared = 8
    in_specs = [pl.BlockSpec(memory_space=pltpu.SMEM)]
    in_specs += [whole(a) if i == shared else by_image(a) for i, a in enumerate(ins)]
    outs = (
        jax.ShapeDtypeStruct((images, positions, D), BF16),
        jax.ShapeDtypeStruct((images, positions, D), F32),
        jax.ShapeDtypeStruct((4, images, positions, D), BF16),
        jax.ShapeDtypeStruct((images, 8, D), F32),
    )
    out_specs = [
        by_image(outs[0]),
        by_image(outs[1]),
        pl.BlockSpec((4, 1, positions, D), lambda b: (0, b, 0, 0)),
        by_image(outs[3]),
    ]
    flops = 2 * images * positions * D * (D + 5 * positions)
    return call(
        attention_backward_kernel,
        (images,),
        (lengths, *ins),
        in_specs,
        outs,
        out_specs,
        [pltpu.VMEM((positions, D), BF16)],
        flops,
        "attention_backward",
    )


def projection_backward(here, *ins):
    _, images, positions, _ = ins[0].shape
    tokens = images * positions
    in_specs = [pl.BlockSpec(memory_space=pltpu.SMEM)]
    in_specs += [pl.BlockSpec((1, images, positions, D), lambda k: (k, 0, 0, 0))]
    in_specs += [whole(a) for a in ins[1:]]
    ins = (here.reshape(1).astype(jnp.int32), *ins)
    outs = (
        jax.ShapeDtypeStruct((4, D // 48, 24, D), BF16),
        jax.ShapeDtypeStruct((4, D // 48, 24, D), BF16),
        jax.ShapeDtypeStruct((images, positions, D), F32),
        jax.ShapeDtypeStruct((images, 8, D), BF16),
    )
    out_specs = [pl.BlockSpec((1, D // 48, 24, D), lambda k: (k, 0, 0, 0))] * 2
    out_specs += [whole(outs[2]), whole(outs[3])]
    scratch = [pltpu.VMEM((D, tokens), BF16), pltpu.VMEM((tokens, D), F32), pltpu.VMEM((D, D), F32)]
    return call(
        projection_backward_kernel,
        (4,),
        ins,
        in_specs,
        outs,
        out_specs,
        scratch,
        2 * 7 * tokens * D * D,
        "projection_backward",
    )


def swish_value(values):
    return values / (1.0 + jnp.exp(-values))


def rope_tables(extents, positions):
    quarter = HDIM // 4
    places = jnp.arange(positions, dtype=jnp.int32)
    widths = extents[:, 1]
    row_place = (places[None, :] // widths[:, None]).astype(F32)
    col_place = (places[None, :] % widths[:, None]).astype(F32)
    lane = jnp.arange(2 * HDIM) % HDIM
    frequency = 10000.0 ** (-(lane % quarter).astype(F32) / quarter)
    by_row = lane < 2 * quarter
    angle = jnp.where(by_row, row_place[:, :, None], col_place[:, :, None]) * frequency
    return jnp.cos(angle), jnp.sin(angle)


def local(
    comm,
    inputs,
    cotangent,
    image_shape,
    time_bins,
    time_table,
    modulation_master,
    projection_master,
    output_master,
    expand_master,
    shrink_master,
    modulation_moment,
    projection_moment,
    output_moment,
    expand_moment,
    shrink_moment,
):
    masters = (modulation_master, projection_master, output_master, expand_master, shrink_master)
    moments = (modulation_moment, projection_moment, output_moment, expand_moment, shrink_moment)
    images, positions, features = inputs.shape
    tokens = images * positions
    rows = modulation_master.shape[1]
    row_index = comm.row_index()

    half = FF // 2
    shrink_low = shrink_master.astype(BF16).T
    packed_attention = jnp.concatenate(
        [projection_master[i].astype(BF16) for i in range(3)] + [output_master.astype(BF16)], axis=1
    )
    packed_units = jnp.concatenate(
        [
            part
            for cols in (slice(None, half), slice(half, None))
            for part in (
                expand_master[0, :, cols].astype(BF16),
                expand_master[1, :, cols].astype(BF16),
                shrink_low[:, cols],
            )
        ],
        axis=1,
    )
    selector = (
        time_bins[:, None] == jnp.arange(time_table.shape[0], dtype=jnp.int32)[None, :]
    ).astype(F32)
    active = swish_value(jnp.dot(selector, time_table, precision=HIGHEST)).astype(BF16)

    def group_rows():
        return comm.to_group(active.reshape(images, comm.row_shards, rows).transpose(1, 0, 2))

    def modulation_of(group):
        partial = jnp.einsum(
            "bd,kde->bke",
            group.reshape(-1, rows),
            modulation_master.astype(BF16),
            preferred_element_type=F32,
        )
        return jnp.sum(
            comm.to_group(partial.reshape(comm.row_shards, images, 6, features)), axis=0
        )

    cosine, sine = rope_tables(image_shape, positions)
    lengths = image_shape[:, 0] * image_shape[:, 1]

    def attend(weights, modulation):
        return attention_forward(
            lengths, inputs, cotangent, modulation, cosine, sine, weights[0], weights[1]
        )

    first, second, modulation, results = comm.gather_weights(
        packed_attention, packed_units, (group_rows, modulation_of), attend
    )
    query_key_weight, value_output_weight = first
    left_weight, right_weight = second
    (first_input, query, key, value, probs, attended, attention, middle, second_input, grad_branch) = (
        results
    )
    second_flat = second_input.reshape(tokens, D)
    branch_flat = grad_branch.reshape(tokens, D)
    shaped = lambda v: v.reshape(images, positions, D)
    here = comm.halves()
    branch_left, back_left, *grads = feed_forward(here, second_flat, branch_flat, left_weight)
    left_sum = comm.begin(*grads)
    second_flat = tie(second_flat, back_left)
    branch_right, back_right, *grads = feed_forward(here, second_flat, branch_flat, right_weight)
    back_right, left_sum, grads = meet(back_right, left_sum, grads)
    left_sum = comm.step(left_sum, "x", 0, 2), comm.step(left_sum, "y", 2, 1)
    right_sum = comm.begin(*grads)
    block_output, grad_stream, grads, sums = attention_backward(
        lengths,
        shaped(branch_left),
        shaped(branch_right),
        shaped(back_left),
        shaped(back_right),
        middle,
        cotangent,
        modulation,
        attention,
        value_output_weight,
        query,
        key,
        value,
        probs,
        cosine,
        sine,
    )
    left_sum, right_sum, grads = meet(left_sum, right_sum, grads)
    left_sum = comm.step(left_sum[0], "y"), comm.step(left_sum[1], "x")
    right_sum = comm.step(right_sum, "x", 0, 2), comm.step(right_sum, "y", 2, 1)
    *grads, input_gradient, grad_modulation = projection_backward(
        here,
        grads,
        first_input,
        attended,
        inputs,
        modulation,
        grad_stream,
        sums,
        active,
        query_key_weight,
        value_output_weight,
    )
    left_sum, right_sum, grads, grad_modulation = meet(left_sum, right_sum, grads, grad_modulation)
    attention_sum = comm.begin(*grads)
    right_sum = comm.step(right_sum[0], "y"), comm.step(right_sum[1], "x")
    left_piece = comm.last(*left_sum)
    attention_sum, right_sum, left_piece = meet(attention_sum, right_sum, left_piece)
    right_begun, attention_sum = meet(comm.last_begin(*right_sum), attention_sum)
    right_piece = comm.last_end(right_begun)
    first_sum = comm.step(attention_sum, "x", 0, 2)
    second_sum = comm.step(attention_sum, "y", 2, 2)
    first_sum, second_sum, right_piece = meet(first_sum, second_sum, right_piece)

    owner = comm.owner_index()
    own_expand, own_shrink = expand_moment, shrink_moment.T
    wide_feed = [
        [
            (
                (piece, ((which,), 0, half)),
                (own_shrink, ((), side * half, half))
                if which == 2
                else (own_expand, ((which,), side * half, half)),
            )
            for side, piece in enumerate((left_piece, right_piece))
        ]
        for which in range(3)
    ]
    wide = comm.to_owners(comm.wide_slots_of(wide_feed))
    first_sum = comm.step(first_sum, "y")
    second_sum = comm.step(second_sum, "x")
    first_sum, second_sum, wide = meet(first_sum, second_sum, wide)
    wide = comm.wide_halves(wide)
    attention_piece, wide = meet(comm.last(first_sum, second_sum), wide)
    own_modulation, own_projection, own_output = modulation_moment, projection_moment, output_moment
    square_feed = [[(None, (own_modulation, ((k,), 0, D)))] for k in range(6)]
    for k in range(3):
        square_feed.append(
            [((attention_piece, ((k,), 0, D)), (own_projection, ((k,), 0, D)))]
        )
    square_feed.append([((attention_piece, ((3,), 0, D)), (own_output, ((), 0, D)))])
    slots = comm.square_slots(square_feed, grad_modulation)
    wide = comm.wide_whole(wide)
    active_wide = pick([0 if slot is None else 1 for slot in comm.wide_slots], owner)
    wide_done = newton_schulz(active_wide, wide)
    slots, left_piece, right_piece, attention_piece = meet(
        slots, left_piece, right_piece, attention_piece
    )
    pieces = [(left_piece, (i,), half) for i in range(3)]
    pieces += [(right_piece, (i,), half) for i in range(3)]
    pieces += [(attention_piece, (i,), D) for i in range(4)]
    totals_low = comm.complete_begin(pack(pieces))
    square, gathered, (wide_done, totals_low) = comm.square_to_owners(slots, (wide_done, totals_low))
    active_all = gathered[:, 6]
    item = pick([-1 if slot is None else slot for slot in comm.slots], owner)
    which = jnp.where((item >= 0) & (item < 6), item, 0)
    right = lax.dynamic_index_in_dim(gathered, which, 1, keepdims=False)
    right = jnp.where(item < 6, right, jnp.zeros_like(right))
    square_done = newton_schulz((item >= 0).astype(jnp.int32), square, active_all, right)
    size = FF // comm.wide_parts
    part = pick([0 if slot is None else slot[1] for slot in comm.wide_slots], owner)
    mine = lax.dynamic_slice_in_dim(wide_done, part * size, size, 1)
    mine = mine + jnp.pad(square_done, ((0, 0), (0, size - D)))
    mine, totals_low = meet(mine, totals_low)
    back = comm.to_rows(mine)

    totals_low = comm.complete_end(totals_low).astype(F32)
    by_unit = [
        jnp.concatenate(
            [totals_low[:, (side * 3 + i) * half : (side * 3 + i + 1) * half] for side in range(2)],
            axis=1,
        )
        for i in range(3)
    ]
    steps = [
        (back, (comm.wide_slots.index((i, p)),), size) for i in range(3) for p in range(comm.wide_parts)
    ]
    steps += [(back, (comm.slots.index(i),), D) for i in range(10)]
    updated = update(*comm.quarters(pack(steps)), masters)
    active_rows = lax.dynamic_slice_in_dim(active_all, row_index * rows, rows, 1)
    modulation_total = jnp.einsum(
        "bd,bke->kde",
        active_rows,
        gathered[:, :6],
        preferred_element_type=F32,
    )
    after = 3 * FF
    totals = (
        modulation_total,
        jnp.stack([totals_low[:, after + i * D : after + (i + 1) * D] for i in range(3)]),
        totals_low[:, after + 3 * D :],
        jnp.stack(by_unit[:2]),
        by_unit[2].T,
    )
    states = tuple((MOMENTUM_DECAY * moment + total for moment, total in zip(moments, totals)))
    return (block_output, input_gradient, *totals, *updated, *states)


def solution(mesh):
    if mesh.shape["dp"] == 4 and mesh.shape["fsdp"] == 8:
        comm = Torus(mesh)
    else:
        comm = Plain(mesh)
    images, rows = comm.images, comm.rows
    by_row = (
        P(None, rows, None),
        P(None, rows, None),
        P(rows, None),
        P(None, rows, None),
        P(None, rows),
    )
    return jax.shard_map(
        functools.partial(local, comm),
        mesh=comm.mesh,
        in_specs=(
            P(images, None, None),
            P(images, None, None),
            P(images, None),
            P(images),
            P(),
            *by_row,
            *by_row,
        ),
        out_specs=(P(images, None, None), P(images, None, None), *by_row, *by_row, *by_row),
        check_vma=False,
    )
```

```python
import functools
import itertools

import jax
import jax.numpy as jnp
from jax import lax
from jax.experimental import pallas as pl
from jax.experimental.pallas import tpu as pltpu
from jax.sharding import Mesh, PartitionSpec as P

D = 768
HEADS = 12
HDIM = 64
FF = 2048
NS_ITERS = 5
NORM_EPS = 1e-06
FROBENIUS_EPS = 1e-07
COEFF_FIRST = 3.4445
COEFF_SECOND = -4.775
COEFF_THIRD = 2.0315
MOMENTUM_DECAY = 0.9
LEARN_RATE = 1.0
HIGHEST = lax.Precision.HIGHEST
BF16 = jnp.bfloat16
F32 = jnp.float32
ITEMS = 13
NT = (((1,), (1,)), ((), ()))
NN = (((1,), (0,)), ((), ()))
TN = (((0,), (0,)), ((), ()))


def dot(a, b, dims=NN):
    return lax.dot_general(a, b, dims, preferred_element_type=F32)


def newton_schulz_kernel(width, active_ref, feed_ref, left_ref, right_ref, out_ref, x, xb, gram, low, poly):
    tile = 256
    tiles = D // tile
    blocks = width // tile
    spans = [slice(i * tile, (i + 1) * tile) for i in range(tiles)]

    def diagonal(part, other):
        rows = lax.broadcasted_iota(jnp.int32, (tile, tile), 0)
        cols = lax.broadcasted_iota(jnp.int32, (tile, tile), 1)
        return jnp.where(rows == cols, part, other)

    def block(b):
        return pl.ds(pl.multiple_of(b * tile, tile), tile)

    @pl.when(active_ref[0] != 0)
    def _():
        def load(b, acc):
            if len(feed_ref.shape) == 3:
                per = feed_ref.shape[2] // tile
                v = feed_ref[b // per, :, block(lax.rem(b, per))].astype(F32)
            else:
                v = feed_ref[:, block(b)].astype(F32)
            if right_ref is not None:
                v = v + (1.0 + MOMENTUM_DECAY) * dot(left_ref[...], right_ref[:, block(b)], TN)
            x[:, block(b)] = v
            return acc + jnp.sum(v * v, axis=0, keepdims=True)

        total = lax.fori_loop(0, blocks, load, jnp.zeros((1, tile), F32))
        total = jnp.sum(total, keepdims=True)
        inverse = 1.0 / (jnp.sqrt(total) + FROBENIUS_EPS)

        def scale_block(b, carry):
            v = x[:, block(b)] * inverse
            x[:, block(b)] = v
            xb[:, block(b)] = v.astype(BF16)
            return carry

        lax.fori_loop(0, blocks, scale_block, 0)

        def iterate(step, carry):
            trace = jnp.zeros((1, tile), F32)
            for i in range(tiles):
                for j in range(i + 1):
                    part = dot(xb[spans[i], :], xb[spans[j], :], NT)
                    gram[spans[i], spans[j]] = part
                    if i == j:
                        trace = trace + jnp.sum(diagonal(part, 0.0), axis=0, keepdims=True)
                    else:
                        lower = part.astype(BF16)
                        low[spans[i], spans[j]] = lower
                        low[spans[j], spans[i]] = lower.T
            shift = jnp.sum(trace, keepdims=True) / D
            for i in range(tiles):
                part = gram[spans[i], spans[i]]
                part = diagonal(part - shift, part)
                gram[spans[i], spans[i]] = part
                low[spans[i], spans[i]] = part.astype(BF16)
            linear = COEFF_SECOND + 2.0 * COEFF_THIRD * shift
            level = COEFF_SECOND * shift + COEFF_THIRD * shift * shift
            trace = jnp.zeros((1, tile), F32)
            for i in range(tiles):
                for j in range(i + 1):
                    part = linear * gram[spans[i], spans[j]] + COEFF_THIRD * dot(
                        low[spans[i], :], low[spans[j], :], NT
                    )
                    if i == j:
                        gram[spans[i], spans[j]] = part
                        trace = trace + jnp.sum(diagonal(part, 0.0), axis=0, keepdims=True)
                    else:
                        lower = part.astype(BF16)
                        poly[spans[i], spans[j]] = lower
                        poly[spans[j], spans[i]] = lower.T
            mean = jnp.sum(trace, keepdims=True) / D
            for i in range(tiles):
                part = gram[spans[i], spans[i]]
                poly[spans[i], spans[i]] = diagonal(part - mean, part).astype(BF16)
            scale = COEFF_FIRST + level + mean

            size = width // 2 if width > 1024 else width
            for b in range(width // size):
                cols = slice(b * size, (b + 1) * size)
                new = scale * x[:, cols] + dot(poly[...], xb[:, cols])
                x[:, cols] = new
                xb[:, cols] = new.astype(BF16)
            return carry

        lax.fori_loop(0, NS_ITERS, iterate, 0)
        out_ref[...] = xb[...]

    @pl.when(active_ref[0] == 0)
    def _():
        out_ref[...] = jnp.zeros_like(out_ref)


def newton_schulz(active, feed, left=None, right=None):
    width = feed.size // D
    operands = [active.reshape(1).astype(jnp.int32), feed]
    if left is None:

        def body(active_ref, feed_ref, *rest):
            newton_schulz_kernel(width, active_ref, feed_ref, None, None, *rest)

    else:
        body = functools.partial(newton_schulz_kernel, width)
        operands += [left, right]
    vmem = pl.BlockSpec(memory_space=pltpu.VMEM)
    return pl.pallas_call(
        body,
        out_shape=jax.ShapeDtypeStruct((D, width), BF16),
        in_specs=[pl.BlockSpec(memory_space=pltpu.SMEM)] + [vmem] * (len(operands) - 1),
        out_specs=vmem,
        scratch_shapes=[
            pltpu.VMEM((D, width), F32),
            pltpu.VMEM((D, width), BF16),
            pltpu.VMEM((D, D), F32),
            pltpu.VMEM((D, D), BF16),
            pltpu.VMEM((D, D), BF16),
        ],
        compiler_params=pltpu.CompilerParams(vmem_limit_bytes=32 * 1024 * 1024),
        cost_estimate=pl.CostEstimate(
            flops=NS_ITERS * 4 * D * D * (width + D), bytes_accessed=4 * D * width, transcendentals=0
        ),
        name="newton_schulz",
    )(*operands)


def tie(value, *others):
    return lax.optimization_barrier((value, *others))[0]


def meet(*values):
    flat, tree = jax.tree.flatten(values)
    return jax.tree.unflatten(tree, lax.optimization_barrier(tuple(flat)))


def fold(mine, other, here, view, start, count):
    before, after = view
    rows, cols = mine.shape[-2:]
    shape = (mine.shape[0], before, 2, after, rows, cols)
    block = pl.BlockSpec((1, *shape[1:]), lambda k: (start + k, 0, 0, 0, 0, 0))
    out = jax.ShapeDtypeStruct((count, before, after, rows, cols), BF16)
    out_block = pl.BlockSpec((1, *out.shape[1:]), lambda k: (k, 0, 0, 0, 0))

    def body(here_ref, mine_ref, other_ref, keep_ref, send_ref):
        here = here_ref[0]
        for ref, at in ((send_ref, 1 - here), (keep_ref, here)):
            ref[0] = (mine_ref[0, :, at].astype(F32) + other_ref[0, :, at].astype(F32)).astype(BF16)

    size = 6 * count * before * after * rows * cols * 2
    keep, send = pl.pallas_call(
        body,
        grid=(count,),
        out_shape=(out, out),
        in_specs=[pl.BlockSpec(memory_space=pltpu.SMEM), block, block],
        out_specs=(out_block, out_block),
        compiler_params=pltpu.CompilerParams(vmem_limit_bytes=24 * 1024 * 1024),
        cost_estimate=pl.CostEstimate(flops=0, bytes_accessed=size, transcendentals=0),
        name="fold",
    )(
        here.reshape(1).astype(jnp.int32),
        pltpu.with_memory_space_constraint(mine.reshape(shape), pltpu.HBM)
        if before * after > 4
        else mine.reshape(shape),
        other.reshape(shape),
    )
    flat = lambda v: v.reshape(count, before * after, rows, cols)
    return flat(keep), flat(send)


def fold_last(states, here):
    rows, cols = states[0][0].shape[-2:]
    counts = [mine.shape[0] for mine, _ in states]
    k = sum(counts)

    def body(here_ref, *refs):
        ins, outs = refs[: 2 * len(states)], refs[2 * len(states) :]
        for by, ref in enumerate(outs):
            at = lax.rem(here_ref[0] + by, 4)
            start = 0
            for i, count in enumerate(counts):
                total = ins[2 * i][:, at].astype(F32) + ins[2 * i + 1][:, at].astype(F32)
                ref[start : start + count] = total.astype(ref.dtype)
                start += count

    vmem = pl.BlockSpec(memory_space=pltpu.VMEM)
    return pl.pallas_call(
        body,
        out_shape=(jax.ShapeDtypeStruct((k, rows, cols), F32),)
        + (jax.ShapeDtypeStruct((k, rows, cols), BF16),) * 3,
        in_specs=[pl.BlockSpec(memory_space=pltpu.SMEM)] + [vmem] * (2 * len(states)),
        out_specs=(vmem,) * 4,
        compiler_params=pltpu.CompilerParams(vmem_limit_bytes=24 * 1024 * 1024),
        cost_estimate=pl.CostEstimate(
            flops=0, bytes_accessed=28 * k * rows * cols, transcendentals=0
        ),
        name="fold_last",
    )(here.reshape(1).astype(jnp.int32), *[part for state in states for part in state])


def place(parts, slots, lead=None, moves=None):
    count = len(parts)
    if lead is None:
        lead = (count, *parts[0].shape[:-2])
        moves = lambda slot: [(i, (), (slot[i],)) for i in range(count)]

    def body(slot_ref, *refs):
        ins, out = refs[:count], refs[count]
        for part, source, target in moves(slot_ref):
            out[target] = ins[part][source] if source else ins[part][...]

    size = count * parts[0].size * parts[0].dtype.itemsize
    vmem = pl.BlockSpec(memory_space=pltpu.VMEM)
    return pl.pallas_call(
        body,
        out_shape=jax.ShapeDtypeStruct((*lead, *parts[0].shape[-2:]), parts[0].dtype),
        in_specs=[pl.BlockSpec(memory_space=pltpu.SMEM)] + [vmem] * count,
        out_specs=vmem,
        cost_estimate=pl.CostEstimate(flops=0, bytes_accessed=2 * size, transcendentals=0),
        compiler_params=pltpu.CompilerParams(vmem_limit_bytes=24 * 1024 * 1024),
        name="place",
    )(jnp.stack(slots).astype(jnp.int32), *parts)


def place_halves(parts, slots):
    count = len(parts)
    rows, cols = parts[0].shape
    half = cols // 2

    def body(slot_ref, *refs):
        left, right = refs[count:]
        for i, ref in enumerate(refs[:count]):
            left[slot_ref[i]] = ref[:, :half]
            right[slot_ref[i]] = ref[:, half:]

    vmem = pl.BlockSpec(memory_space=pltpu.VMEM)
    shape = jax.ShapeDtypeStruct((count, rows, half), parts[0].dtype)
    return pl.pallas_call(
        body,
        out_shape=(shape, shape),
        in_specs=[pl.BlockSpec(memory_space=pltpu.SMEM)] + [vmem] * count,
        out_specs=(vmem, vmem),
        cost_estimate=pl.CostEstimate(flops=0, bytes_accessed=16 * rows * cols, transcendentals=0),
        compiler_params=pltpu.CompilerParams(vmem_limit_bytes=24 * 1024 * 1024),
        name="place_halves",
    )(jnp.stack(slots).astype(jnp.int32), *parts)


def slots_of(feeds, owners, width, quarter, extra=None):
    more = 0 if extra is None else extra.shape[0]
    arrays, index = [], {}

    def note(array):
        if array is None:
            return None
        source, columns = array
        if id(source) not in index:
            index[id(source)] = len(arrays)
            arrays.append(source)
        return (index[id(source)], columns)

    noted = [[(note(total), note(moment)) for total, moment in feed] for feed in feeds]
    rows = arrays[0].shape[-2]
    for total, _ in sum(feeds, []):
        if total is not None:
            rows = total[0].shape[-2]
    if all(total is None or total[0].shape[-2] == moment[0].shape[-2] for total, moment in sum(feeds, [])):
        quarter = jnp.int32(0)

    def block(array):
        shape = (*array.shape[:-2], rows, array.shape[-1])
        lead = (0,) * (array.ndim - 2)
        if array.shape[-2] == rows:
            return pl.BlockSpec(shape, lambda i, q: (*lead, 0, 0))
        return pl.BlockSpec(shape, lambda i, q: (*lead, q[0], 0))

    def body(_, *refs):
        out = refs[-1]
        if more:
            out = refs[-1].at[:, :rows]
            for slot in range(owners):
                refs[-1][slot, rows:] = refs[-2][...]

        def read(what):
            place_of, (lead, start, size) = what
            ref = refs[place_of]
            return ref[(*lead, slice(None), slice(start, start + size))].astype(F32)

        first = {}
        for slot in range(owners):
            if not noted[slot]:
                out[slot] = jnp.zeros((rows, width), BF16)
                continue
            key = str(noted[slot])
            if key in first:
                out[slot] = out[first[key]]
                continue
            first[key] = slot
            at = 0
            for total, moment in noted[slot]:
                value = MOMENTUM_DECAY * MOMENTUM_DECAY * read(moment)
                if total is not None:
                    value = value + (1.0 + MOMENTUM_DECAY) * read(total)
                out[slot, :, at : at + value.shape[1]] = value.astype(BF16)
                at += value.shape[1]

    return pl.pallas_call(
        body,
        out_shape=jax.ShapeDtypeStruct((owners, rows + more, width), BF16),
        grid_spec=pltpu.PrefetchScalarGridSpec(
            num_scalar_prefetch=1,
            grid=(1,),
            in_specs=[block(array) for array in arrays]
            + [pl.BlockSpec((more, width), lambda i, q: (0, 0))] * (more > 0),
            out_specs=pl.BlockSpec((owners, rows + more, width), lambda i, q: (0, 0, 0)),
        ),
        cost_estimate=pl.CostEstimate(
            flops=0, bytes_accessed=2 * owners * rows * width, transcendentals=0
        ),
        compiler_params=pltpu.CompilerParams(vmem_limit_bytes=24 * 1024 * 1024),
        name="slots",
    )(
        quarter.reshape(1).astype(jnp.int32),
        *[
            array
            if array.shape[-2] == rows
            else pltpu.with_memory_space_constraint(array, pltpu.HBM)
            for array in arrays
        ],
        *([extra] if more else []),
    )


def pack(parts):
    arrays, index = [], {}
    for array, _, _ in parts:
        if id(array) not in index:
            index[id(array)] = len(arrays)
            arrays.append(array)
    rows = arrays[0].shape[-2]
    total = sum(cols for _, _, cols in parts)

    def body(*refs):
        at = 0
        for array, lead, cols in parts:
            value = refs[index[id(array)]][(*lead, slice(None), slice(0, cols))]
            refs[-1][:, at : at + cols] = value.astype(BF16)
            at += cols

    vmem = pl.BlockSpec(memory_space=pltpu.VMEM)
    return pl.pallas_call(
        body,
        out_shape=jax.ShapeDtypeStruct((rows, total), BF16),
        in_specs=[vmem] * len(arrays),
        out_specs=vmem,
        cost_estimate=pl.CostEstimate(flops=0, bytes_accessed=6 * rows * total, transcendentals=0),
        compiler_params=pltpu.CompilerParams(vmem_limit_bytes=24 * 1024 * 1024),
        name="pack",
    )(*arrays)


def pick(values, index):
    found = jnp.int32(values[0])
    for i, value in enumerate(values):
        if value != values[0]:
            found = jnp.where(index == i, jnp.int32(value), found)
    return found


def update_kernel(quarters, slot_ref, *refs):
    step_refs, refs = refs[:quarters], refs[quarters:]
    modulation, projection, output, expand, shrink = refs[:5]
    out_modulation, out_projection, out_output, out_expand, out_shrink = refs[5:10]
    quarter = pl.program_id(0)
    rows = step_refs[0].shape[0]
    ratio = LEARN_RATE * (FF / D) ** 0.5
    for which, steps in enumerate(step_refs):

        @pl.when(slot_ref[quarter] == which)
        def _(steps=steps):
            at = 3 * FF
            for k in range(2):
                step = steps[:, k * FF : (k + 1) * FF].astype(F32)
                out_expand[k] = expand[k] - ratio * step
            out_shrink[...] = shrink[...] - LEARN_RATE * steps[:, 2 * FF : at].astype(F32)
            for master, out, count in (
                (modulation, out_modulation, 6),
                (projection, out_projection, 3),
            ):
                for k in range(count):
                    out[k] = master[k] - LEARN_RATE * steps[:, at : at + D].astype(F32)
                    at += D
            out_output[...] = output[...] - LEARN_RATE * steps[:, at : at + D].astype(F32)


def update(slots, steps, masters):
    quarters = len(steps)
    rows = steps[0].shape[0]
    third = lambda a: pl.BlockSpec((a.shape[0], rows, a.shape[2]), lambda q: (0, q, 0))
    masters = (*masters[:4], masters[4].T)
    modulation, projection, output, expand, shrink = masters
    specs = [
        third(modulation),
        third(projection),
        pl.BlockSpec((rows, D), lambda q: (q, 0)),
        third(expand),
        pl.BlockSpec((rows, FF), lambda q: (q, 0)),
    ]
    updated = pl.pallas_call(
        functools.partial(update_kernel, quarters),
        grid=(quarters,),
        out_shape=tuple(jax.ShapeDtypeStruct(a.shape, F32) for a in masters),
        in_specs=[pl.BlockSpec(memory_space=pltpu.SMEM)] + [whole(a) for a in steps] + specs,
        out_specs=tuple(specs),
        cost_estimate=pl.CostEstimate(flops=0, bytes_accessed=14_000_000, transcendentals=0),
        compiler_params=pltpu.CompilerParams(vmem_limit_bytes=24 * 1024 * 1024),
        name="update",
    )(
        jnp.stack(slots).astype(jnp.int32),
        *steps,
        *[pltpu.with_memory_space_constraint(a, pltpu.HBM) for a in masters],
    )
    return (*updated[:4], updated[4].T)


def every(*sizes):
    return list(itertools.product(*[range(size) for size in sizes]))


class Plain:
    images = ("dp", "fsdp")
    rows = "fsdp"
    wide_parts = 1

    def __init__(self, mesh):
        self.mesh = mesh
        self.row_shards = mesh.shape["fsdp"]
        self.owners = mesh.shape["fsdp"]
        self.wide_slots = [(i, 0) for i in range(3)]
        self.wide_slots += [None] * (self.owners - 3)
        self.slots = [None] * 3 + list(range(10))
        self.slots += [None] * (self.owners - ITEMS)

    def row_index(self):
        return lax.axis_index("fsdp")

    def group_index(self):
        return lax.axis_index("dp")

    def owner_index(self):
        return lax.axis_index("fsdp")

    def gather_weights(self, first, second, modulate, attend):
        full = [lax.all_gather(chunk, "fsdp", axis=0, tiled=True) for chunk in (first, second)]
        first, second = [jnp.split(chunk, 2, axis=1) for chunk in full]
        modulation = modulate[1](modulate[0]())
        return first, second, modulation, attend(first, modulation)

    def to_group(self, value):
        return lax.all_to_all(value, "fsdp", split_axis=0, concat_axis=0, tiled=True)

    def halves(self):
        return jnp.int32(0)

    def begin(self, mine, send):
        k, n, rows, cols = mine.shape
        return (jnp.stack([mine, send], axis=2).reshape(k, 2 * n * rows, cols),)

    def step(self, state, axis, start=0, count=None):
        return (state[0][start : start + (count or state[0].shape[0])],)

    def last_begin(self, *states):
        return states

    def last_end(self, states):
        return self.last(*states)

    def last(self, *states):
        value = jnp.concatenate([state[0] for state in states], axis=0)
        shard = lax.psum_scatter(value, "fsdp", scatter_dimension=1, tiled=True)
        return lax.psum(shard.astype(F32), "dp")

    def own_rows(self, shard, dim=-2):
        return shard

    def complete_begin(self, piece):
        return piece

    def complete_end(self, piece):
        return piece

    def quarters(self, piece):
        return [jnp.int32(0)], [piece]

    def to_owners(self, pieces):
        got = lax.all_to_all(pieces, "fsdp", split_axis=0, concat_axis=0, tiled=True)
        return got.reshape(-1, got.shape[2])

    def wide_slots_of(self, feeds):
        return slots_of(
            [[] if slot is None else feeds[slot[0]] for slot in self.wide_slots],
            self.owners,
            FF,
            jnp.int32(0),
        )

    def wide_halves(self, got):
        return got

    def wide_whole(self, got):
        return jnp.stack(jnp.split(got, 2, axis=1))

    def square_slots(self, feeds, rows):
        return (
            slots_of(
                [[] if slot is None else feeds[slot] for slot in self.slots],
                self.owners,
                D,
                self.group_index(),
            ),
            rows,
        )

    def square_to_owners(self, slots, beside):
        pieces, rows = slots
        rows = lax.all_gather(rows, ("dp", "fsdp"), axis=0, tiled=True)
        return self.to_owners(pieces), rows, beside

    def to_rows(self, whole):
        blocks = whole.reshape(self.row_shards, -1, whole.shape[1])
        return lax.all_to_all(blocks, "fsdp", split_axis=0, concat_axis=0, tiled=True)


class Torus:
    images = ("x", "c", "z", "y")
    rows = ("z", "y")
    chips = ("x", "z", "y")
    wide_parts = 2

    def __init__(self, mesh):
        self.mesh = Mesh(mesh.devices.reshape(2, 2, 4, 2), ("x", "c", "z", "y"))
        self.row_shards = 8
        self.owners = 16
        wide_places = [(1, 0), (2, 1), (1, 1)]
        self.wide_slots = [None] * 16
        self.slots = [None] * 16
        for item, (z, y) in enumerate(wide_places):
            for part in range(2):
                self.wide_slots[(part * 4 + z) * 2 + y] = (item, part)
        free = [i for i in range(16) if self.wide_slots[i] is None]
        for item, slot in enumerate(free):
            self.slots[slot] = item

    def row_index(self):
        return lax.axis_index("z") * 2 + lax.axis_index("y")

    def group_index(self):
        return lax.axis_index("x") * 2 + lax.axis_index("c")

    def owner_index(self):
        return (lax.axis_index("x") * 4 + lax.axis_index("z")) * 2 + lax.axis_index("y")

    def swap(self, value, axis):
        return lax.ppermute(value, axis, [(0, 1), (1, 0)])

    def shift(self, value, by):
        return lax.ppermute(value, "z", [(i, (i + by) % 4) for i in range(4)])

    def exchange(self, value, axis):
        here = lax.axis_index(axis)
        return place([value, self.swap(value, axis)], [here, 1 - here])

    def spread_z(self, value):
        z = lax.axis_index("z")
        ring = [value] + [self.shift(value, by) for by in range(1, 4)]
        return place(ring, [(z - by) % 4 for by in range(4)])

    def gather_weights(self, first, second, modulate, attend):
        x, y, z, c = [lax.axis_index(axis) for axis in "xyzc"]
        slots = [(z - by) % 4 for by in range(4)]

        def ring_of(chunk, *others):
            piece = self.own_rows(chunk)
            if others:
                piece = tie(piece, *others)
            return [piece] + [self.shift(piece, by) for by in range(1, 4)]

        def one_hop(left, right):
            left_other, right_other = self.swap(left, "y"), self.swap(right, "x")
            left = place([left, left_other], [y, 1 - y])
            right = place([right, right_other], [x, 1 - x])
            return left, right

        def other_hop(left, right):
            left, right = meet(left, right)
            left_other, right_other = meet(self.swap(left, "x"), self.swap(right, "y"))
            left = place([left, left_other], [x, 1 - x])
            right = place([right, right_other], [y, 1 - y])
            return left, right

        def by_core(left, right):
            others = self.swap(left, "c"), self.swap(right, "c")
            pair = []
            for half, other, order in ((left, others[0], (2, 1, 0)), (right, others[1], (2, 0, 1))):

                def moves(slot, order=order):
                    found = []
                    for part in range(2):
                        for at in every(2, 2, 4):
                            found.append((part, at, (*[at[i] for i in order], slot[part])))
                    return found

                pair.append(place([half, other], [c, 1 - c], (4, 2, 2, 2), moves).reshape(D, -1))
            return pair

        group = modulate[0]()
        left, right = place_halves(ring_of(first), slots)
        left, right, group = meet(left, right, group)
        ring = ring_of(second, left, right)
        left, right = one_hop(left, right)
        left, right, ring[0], ring[1], ring[3] = meet(left, right, ring[0], ring[1], ring[3])
        left, right = other_hop(left, right)
        modulation = modulate[1](group)
        left, right, ring[2] = meet(left, right, ring[2])
        second_left, second_right = place_halves(ring, slots)
        others = self.swap(second_left, "y"), self.swap(second_right, "x")
        done = by_core(left, right)
        done, others, modulation = meet(done, others, modulation)
        left = place([second_left, others[0]], [y, 1 - y])
        right = place([second_right, others[1]], [x, 1 - x])
        left, right = meet(left, right)
        others = self.swap(left, "x"), self.swap(right, "y")
        done, left, right = meet(done, left, right)
        results = attend(done, modulation)
        left_other, right_other, results = meet(*others, results)
        left = place([left, left_other], [x, 1 - x])
        right = place([right, right_other], [y, 1 - y])
        return done, by_core(left, right), modulation, results

    def to_group(self, value):
        return lax.all_to_all(value, ("z", "y"), split_axis=0, concat_axis=0, tiled=True)

    def halves(self):
        return lax.axis_index("c")

    def begin(self, mine, send):
        return (mine, self.swap(send, "c"))

    def step(self, state, axis, start=0, count=None):
        mine, other = state
        parts = mine.shape[1]
        view = (4, 2) if (parts, axis) == (16, "y") else (parts // 2, 1)
        keep, send = fold(
            mine, other, lax.axis_index(axis), view, start, count or mine.shape[0]
        )
        return (keep, self.swap(send, axis))

    def last(self, *states):
        return self.last_end(self.last_begin(*states))

    def last_begin(self, *states):
        return fold_last(states, lax.axis_index("z"))

    def last_end(self, folded):
        total, *sends = folded
        for by, send in enumerate(sends, 1):
            total = total + self.shift(send, by).astype(F32)
        return total

    def own_rows(self, shard, dim=-2):
        return lax.dynamic_slice_in_dim(
            shard, self.group_index() * (D // 32), D // 32, dim % shard.ndim
        )

    def quarters(self, piece):
        x, c = lax.axis_index("x"), lax.axis_index("c")
        by_x = self.swap(piece, "x")
        by_c = self.swap(piece, "c")
        by_both = self.swap(by_x, "c")
        slots = []
        for at_x, at_c in every(2, 2):
            slots.append(jnp.where(at_x == x, 0, 1) + jnp.where(at_c == c, 0, 2))
        return slots, [piece, by_x, by_c, by_both]

    def complete_begin(self, piece):
        return piece, self.swap(piece, "x")

    def complete_end(self, pair):
        x, c = lax.axis_index("x"), lax.axis_index("c")
        value = place(list(pair), [x, 1 - x])
        moves = lambda slot: [(part, (x,), (x, slot[part])) for part in range(2) for x in range(2)]
        value = place([value, self.swap(value, "c")], [c, 1 - c], (2, 2), moves)
        return value.reshape(D // 8, -1)

    def to_owners(self, pieces):
        return lax.all_to_all(pieces, self.chips, split_axis=0, concat_axis=0, tiled=True)

    def wide_slots_of(self, feeds):
        halved = []
        for slot in self.wide_slots:
            halved.append([] if slot is None else [feeds[slot[0]][slot[1]]])
        return slots_of(halved, self.owners, FF // 2, self.group_index())

    def wide_halves(self, got):
        return got, self.swap(got, "x")

    def wide_whole(self, got):
        half = FF // 2
        x, c = lax.axis_index("x"), lax.axis_index("c")
        both = place(list(got), [x, 1 - x])
        both = both.reshape(2, 2, 4, 2, D // 32, half)

        def moves(slot):
            return [
                (part, (p, x, z, y), (p, z, y, x, slot[part]))
                for part in range(2)
                for p, x, z, y in every(2, 2, 4, 2)
            ]

        whole = place([both, self.swap(both, "c")], [c, 1 - c], (2, 4, 2, 2, 2), moves)
        return whole.reshape(2, D, half)

    def square_slots(self, feeds, rows):
        return slots_of(
            [[] if slot is None else feeds[slot] for slot in self.slots],
            self.owners,
            D,
            self.group_index(),
            rows.reshape(-1, D),
        )

    def square_to_owners(self, slots, beside):
        quarter = D // 32
        got = self.to_owners(slots)
        got, beside = meet(got, beside)
        other = self.swap(got, "c")
        more = got.shape[1] - quarter

        def body(c_ref, mine_ref, other_ref, whole_ref, rows_ref):
            c = c_ref[0]
            for ref, at in ((mine_ref, c), (other_ref, 1 - c)):
                for chip, (x, z, y) in enumerate(every(2, 4, 2)):
                    whole_ref[z, y, x, at] = ref[chip, :quarter]
                    rows_ref[at, chip] = ref[chip, quarter:]

        vmem = pl.BlockSpec(memory_space=pltpu.VMEM)
        square, gathered = pl.pallas_call(
            body,
            out_shape=(
                jax.ShapeDtypeStruct((4, 2, 2, 2, quarter, D), BF16),
                jax.ShapeDtypeStruct((2, 16, more, D), BF16),
            ),
            in_specs=[pl.BlockSpec(memory_space=pltpu.SMEM), vmem, vmem],
            out_specs=(vmem, vmem),
            cost_estimate=pl.CostEstimate(
                flops=0, bytes_accessed=8 * got.size, transcendentals=0
            ),
            compiler_params=pltpu.CompilerParams(vmem_limit_bytes=24 * 1024 * 1024),
            name="place_square",
        )(lax.axis_index("c").reshape(1).astype(jnp.int32), got, other)
        return square.reshape(D, D), gathered.reshape(-1, 8, D), beside

    def to_rows(self, whole):
        cols = whole.shape[1]
        blocks = whole.reshape(4, 2, 2, 2, D // 32, cols)
        blocks = lax.dynamic_index_in_dim(blocks, lax.axis_index("c"), 3, keepdims=False)
        blocks = blocks.transpose(2, 0, 1, 3, 4).reshape(16, D // 32, cols)
        return lax.all_to_all(blocks, self.chips, split_axis=0, concat_axis=0, tiled=True)


def lanes(shape, dim):
    return lax.broadcasted_iota(jnp.int32, shape, dim)


def norm_of(values):
    centred = values - jnp.mean(values, axis=-1, keepdims=True)
    inverse = lax.rsqrt(jnp.mean(centred * centred, axis=-1, keepdims=True) + NORM_EPS)
    return centred * inverse, inverse


def norm_back(incoming, normed, inverse):
    return inverse * (
        incoming
        - jnp.mean(incoming, axis=-1, keepdims=True)
        - normed * jnp.mean(incoming * normed, axis=-1, keepdims=True)
    )


def rotate_pair(value):
    first = lanes(value.shape, 1) % 32 < 16
    return jnp.where(first, -pltpu.roll(value, 112, 1), pltpu.roll(value, 16, 1))


def two_heads(value):
    low = lanes(value.shape, 1) < HDIM
    zero = jnp.zeros_like(value)
    return jnp.where(low, value, zero), jnp.where(low, zero, value)


def pair_at(pair):
    return pl.ds(pl.multiple_of(pair * 2 * HDIM, 2 * HDIM), 2 * HDIM)


def attention_forward_kernel(
    length_ref,
    input_ref,
    cotangent_ref,
    modulation_ref,
    cosine_ref,
    sine_ref,
    query_key_ref,
    value_output_ref,
    first_ref,
    query_ref,
    key_ref,
    value_ref,
    probs_ref,
    attended_ref,
    attention_ref,
    middle_ref,
    second_ref,
    branch_ref,
):
    length = length_ref[pl.program_id(0)]
    row = lambda which: modulation_ref[0, which : which + 1, :]
    stream = input_ref[0].astype(F32)
    positions = stream.shape[0]
    normed, _ = norm_of(stream)
    first = (normed * (1.0 + row(1)) + row(0)).astype(BF16)
    first_ref[0] = first
    inside = lanes((positions, D), 0) < length
    upstream = jnp.where(inside, cotangent_ref[0].astype(F32), 0.0)
    branch_ref[0] = (row(5) * upstream).astype(BF16)
    value_ref[0] = dot(first, value_output_ref[:, :D]).astype(BF16)
    cosine, sine = cosine_ref[0], sine_ref[0]
    keep = lanes((positions, positions), 1) < length

    @pl.loop(0, HEADS // 2)
    def _(pair):
        at = pair_at(pair)
        query = dot(first, query_key_ref[:, at])
        key = dot(first, query_key_ref[:, pair_at(HEADS // 2 + pair)])
        query = (query * cosine + rotate_pair(query) * sine).astype(BF16)
        key = (key * cosine + rotate_pair(key) * sine).astype(BF16)
        query_ref[0, :, at] = query
        key_ref[0, :, at] = key
        low = []
        for head, masked in enumerate(two_heads(query)):
            scores = dot(masked, key, NT) * HDIM ** (-0.5)
            scores = jnp.where(keep, scores, -1000000000.0)
            exponent = jnp.exp(scores - jnp.max(scores, axis=-1, keepdims=True))
            probs = exponent * (1.0 / jnp.sum(exponent, axis=-1, keepdims=True))
            probs_ref[0, 2 * pair + head] = probs
            low.append(probs.astype(BF16))
        values = two_heads(value_ref[0, :, at])
        attended_ref[0, :, at] = dot(
            jnp.concatenate(low, axis=1), jnp.concatenate(values, axis=0)
        ).astype(BF16)

    attention = dot(attended_ref[0], value_output_ref[:, D:])
    attention_ref[0] = attention
    middle = stream + row(2) * attention
    middle_ref[0] = middle
    normed, _ = norm_of(middle)
    second_ref[0] = (normed * (1.0 + row(4)) + row(3)).astype(BF16)


def split_rows(value, scratch, here, keep_ref, send_ref, which, cols):
    scratch[...] = value
    rows = keep_ref.shape[2]
    for i in range(keep_ref.shape[1]):
        for ref, at in ((keep_ref, here), (send_ref, 1 - here)):
            start = pl.multiple_of((2 * i + at) * rows, 8)
            ref[which, i, :, cols] = scratch[pl.ds(start, rows), :].astype(BF16)


def feed_forward_kernel(
    here_ref,
    second_ref,
    branch_ref,
    gate_ref,
    up_ref,
    down_ref,
    out_ref,
    back_ref,
    keep_ref,
    send_ref,
    second_t,
    branch_t,
    rows,
):
    step = pl.program_id(0)

    @pl.when(step == 0)
    def _():
        second_t[...] = second_ref[...].T
        branch_t[...] = branch_ref[...].T
        out_ref[...] = jnp.zeros_like(out_ref)
        back_ref[...] = jnp.zeros_like(back_ref)

    gate, up, down = gate_ref[...], up_ref[...], down_ref[...]
    gate_pre = dot(second_ref[...], gate)
    up_pre = dot(second_ref[...], up)
    sigmoid = 1.0 / (1.0 + jnp.exp(-gate_pre))
    swish = gate_pre * sigmoid
    hidden = (swish * up_pre).astype(BF16)
    out_ref[...] += dot(hidden, down, NT)
    grad_hidden = dot(branch_ref[...], down)
    grad_gate = (grad_hidden * up_pre * sigmoid * (1.0 + gate_pre * (1.0 - sigmoid))).astype(BF16)
    grad_up = (grad_hidden * swish).astype(BF16)
    back_ref[...] += dot(grad_gate, gate, NT) + dot(grad_up, up, NT)
    everything = slice(None)
    products = ((second_t, grad_gate), (second_t, grad_up), (branch_t, hidden))
    for which, (left, right) in enumerate(products):
        split_rows(
            dot(left[...], right), rows, here_ref[0], keep_ref, send_ref, which, everything
        )


def attention_backward_kernel(
    length_ref,
    branch_left_ref,
    branch_right_ref,
    second_left_ref,
    second_right_ref,
    middle_ref,
    cotangent_ref,
    modulation_ref,
    attention_ref,
    value_output_ref,
    query_ref,
    key_ref,
    value_ref,
    probs_ref,
    cosine_ref,
    sine_ref,
    output_ref,
    stream_ref,
    grads_ref,
    sums_ref,
    attended_grad,
):
    length = length_ref[pl.program_id(0)]
    row = lambda which: modulation_ref[0, which : which + 1, :]
    middle = middle_ref[0]
    positions = middle.shape[0]
    inside = lanes((positions, D), 0) < length
    upstream = jnp.where(inside, cotangent_ref[0].astype(F32), 0.0)
    branch = branch_left_ref[0] + branch_right_ref[0]
    output_ref[0] = (middle + row(5) * branch).astype(BF16)
    total = lambda value: jnp.sum(value, axis=0, keepdims=True)
    gate_two = total(upstream * branch)
    second = second_left_ref[0] + second_right_ref[0]
    normed, inverse = norm_of(middle)
    scale_two = total(second * normed)
    shift_two = total(second)
    stream = upstream + norm_back(second * (1.0 + row(4)), normed, inverse)
    stream_ref[0] = stream
    gate_one = total(stream * attention_ref[0])
    blank = jnp.zeros_like(gate_one)
    sums_ref[0] = jnp.concatenate(
        [blank, blank, gate_one, shift_two, scale_two, gate_two, blank, blank], axis=0
    )
    grad_attention = (row(2) * stream).astype(BF16)
    grads_ref[3, 0] = grad_attention
    attended_grad[...] = dot(grad_attention, value_output_ref[:, D:], NT).astype(BF16)
    cosine, sine = cosine_ref[0], sine_ref[0]

    @pl.loop(0, HEADS // 2)
    def _(pair):
        at = pair_at(pair)
        query, key, value = query_ref[0, :, at], key_ref[0, :, at], value_ref[0, :, at]
        attended = two_heads(attended_grad[:, at])
        low, scores = [], []
        for head in range(2):
            probs = probs_ref[0, 2 * pair + head]
            grad_probs = dot(attended[head], value, NT)
            inner = jnp.sum(grad_probs * probs, axis=-1, keepdims=True)
            scores.append((probs * (grad_probs - inner)).astype(BF16))
            low.append(probs.astype(BF16))
        grads_ref[2, 0, :, at] = dot(
            jnp.concatenate(low, axis=0), jnp.concatenate(attended, axis=0), TN
        ).astype(BF16)
        grad_query = dot(
            jnp.concatenate(scores, axis=1), jnp.concatenate(two_heads(key), axis=0)
        ) * HDIM ** (-0.5)
        grad_key = dot(
            jnp.concatenate(scores, axis=0), jnp.concatenate(two_heads(query), axis=0), TN
        ) * HDIM ** (-0.5)
        grads_ref[0, 0, :, at] = (grad_query * cosine - rotate_pair(grad_query * sine)).astype(BF16)
        grads_ref[1, 0, :, at] = (grad_key * cosine - rotate_pair(grad_key * sine)).astype(BF16)


def projection_backward_kernel(
    here_ref,
    grads_in_ref,
    first_ref,
    attended_ref,
    input_ref,
    modulation_ref,
    stream_ref,
    sums_ref,
    active_ref,
    query_key_ref,
    value_output_ref,
    keep_ref,
    send_ref,
    input_grad_ref,
    modulation_grad_ref,
    first_t,
    first_grad,
    rows,
):
    images, positions = input_ref.shape[:2]
    tokens = images * positions
    flat = lambda ref: ref[...].reshape(tokens, D)
    step = pl.program_id(0)

    def product(grads):
        split_rows(dot(first_t[...], grads), rows, here_ref[0], keep_ref, send_ref, 0, slice(None))

    @pl.when(step == 0)
    def _():
        first_t[...] = flat(first_ref).T
        grads = grads_in_ref[0].reshape(tokens, D)
        product(grads)
        first_grad[...] = dot(grads, query_key_ref[:, :D], NT)

    @pl.when(step == 1)
    def _():
        grads = grads_in_ref[0].reshape(tokens, D)
        product(grads)
        first_grad[...] += dot(grads, query_key_ref[:, D:], NT)

    @pl.when(step == 2)
    def _():
        grads = grads_in_ref[0].reshape(tokens, D)
        product(grads)
        first_grad[...] += dot(grads, value_output_ref[:, :D], NT)

    @pl.when(step == 3)
    def _():
        first_t[...] = flat(attended_ref).T
        product(grads_in_ref[0].reshape(tokens, D))
        for image in range(images):
            at = slice(image * positions, (image + 1) * positions)
            normed, inverse = norm_of(input_ref[image].astype(F32))
            first = first_grad[at, :]
            scale_one = jnp.sum(first * normed, axis=0, keepdims=True)
            shift_one = jnp.sum(first, axis=0, keepdims=True)
            scaled = first * (1.0 + modulation_ref[image, 1:2, :])
            input_grad_ref[image] = stream_ref[image] + norm_back(scaled, normed, inverse)
            modulation_grad_ref[image] = jnp.concatenate(
                [
                    shift_one,
                    scale_one,
                    sums_ref[image, 2:6, :],
                    active_ref[image : image + 1, :].astype(F32),
                    jnp.zeros_like(shift_one),
                ],
                axis=0,
            ).astype(BF16)


BIG_VMEM = 36 * 1024 * 1024


def whole(array):
    return pl.BlockSpec(array.shape, lambda *_: (0,) * array.ndim)


def by_image(array):
    return pl.BlockSpec((1, *array.shape[1:]), lambda b: (b,) + (0,) * (array.ndim - 1))


def call(body, grid, ins, in_specs, outs, out_specs, scratch, flops, name):
    size = sum(a.size * a.dtype.itemsize for a in (*ins, *outs))
    return pl.pallas_call(
        body,
        grid=grid,
        out_shape=outs,
        in_specs=in_specs,
        out_specs=out_specs,
        scratch_shapes=scratch,
        compiler_params=pltpu.CompilerParams(vmem_limit_bytes=BIG_VMEM),
        cost_estimate=pl.CostEstimate(flops=flops, bytes_accessed=size, transcendentals=0),
        name=name,
    )(*ins)


def attention_forward(lengths, inputs, cotangent, modulation, cosine, sine, query_key, value_output):
    images, positions, _ = inputs.shape
    ins = (lengths, inputs, cotangent, modulation, cosine, sine, query_key, value_output)
    in_specs = [pl.BlockSpec(memory_space=pltpu.SMEM)]
    in_specs += [by_image(a) for a in ins[1:6]] + [whole(a) for a in ins[6:]]
    token = lambda dtype: jax.ShapeDtypeStruct((images, positions, D), dtype)
    outs = (
        token(BF16),
        token(BF16),
        token(BF16),
        token(BF16),
        jax.ShapeDtypeStruct((images, HEADS, positions, positions), F32),
        token(BF16),
        token(F32),
        token(F32),
        token(BF16),
        token(BF16),
    )
    flops = 2 * images * positions * D * (4 * D + 2 * positions)
    return call(
        attention_forward_kernel,
        (images,),
        ins,
        in_specs,
        outs,
        [by_image(a) for a in outs],
        [],
        flops,
        "attention_forward",
    )


def feed_forward(here, second, branch, weight):
    tokens = second.shape[0]
    units = weight.shape[1] // 3
    tile = 256
    steps = units // tile
    weight = pltpu.with_memory_space_constraint(weight, pltpu.HBM)
    ins = (here.reshape(1).astype(jnp.int32), second, branch, weight, weight, weight)
    in_specs = [pl.BlockSpec(memory_space=pltpu.SMEM), whole(second), whole(branch)] + [
        pl.BlockSpec((D, tile), lambda t, which=which: (0, which * steps + t)) for which in range(3)
    ]
    outs = (
        jax.ShapeDtypeStruct((tokens, D), F32),
        jax.ShapeDtypeStruct((tokens, D), F32),
        jax.ShapeDtypeStruct((3, D // 48, 24, units), BF16),
        jax.ShapeDtypeStruct((3, D // 48, 24, units), BF16),
    )
    out_specs = [whole(outs[0]), whole(outs[1])]
    out_specs += [pl.BlockSpec((3, D // 48, 24, tile), lambda t: (0, 0, 0, t))] * 2
    scratch = [pltpu.VMEM((D, tokens), BF16), pltpu.VMEM((D, tokens), BF16), pltpu.VMEM((D, tile), F32)]
    flops = 2 * 9 * tokens * D * units
    return call(
        feed_forward_kernel, (steps,), ins, in_specs, outs, out_specs, scratch, flops, "feed_forward"
    )


def attention_backward(lengths, *ins):
    images, positions, _ = ins[0].shape
    shared = 8
    in_specs = [pl.BlockSpec(memory_space=pltpu.SMEM)]
    in_specs += [whole(a) if i == shared else by_image(a) for i, a in enumerate(ins)]
    outs = (
        jax.ShapeDtypeStruct((images, positions, D), BF16),
        jax.ShapeDtypeStruct((images, positions, D), F32),
        jax.ShapeDtypeStruct((4, images, positions, D), BF16),
        jax.ShapeDtypeStruct((images, 8, D), F32),
    )
    out_specs = [
        by_image(outs[0]),
        by_image(outs[1]),
        pl.BlockSpec((4, 1, positions, D), lambda b: (0, b, 0, 0)),
        by_image(outs[3]),
    ]
    flops = 2 * images * positions * D * (D + 5 * positions)
    return call(
        attention_backward_kernel,
        (images,),
        (lengths, *ins),
        in_specs,
        outs,
        out_specs,
        [pltpu.VMEM((positions, D), BF16)],
        flops,
        "attention_backward",
    )


def projection_backward(here, *ins):
    _, images, positions, _ = ins[0].shape
    tokens = images * positions
    in_specs = [pl.BlockSpec(memory_space=pltpu.SMEM)]
    in_specs += [pl.BlockSpec((1, images, positions, D), lambda k: (k, 0, 0, 0))]
    in_specs += [whole(a) for a in ins[1:]]
    ins = (here.reshape(1).astype(jnp.int32), *ins)
    outs = (
        jax.ShapeDtypeStruct((4, D // 48, 24, D), BF16),
        jax.ShapeDtypeStruct((4, D // 48, 24, D), BF16),
        jax.ShapeDtypeStruct((images, positions, D), F32),
        jax.ShapeDtypeStruct((images, 8, D), BF16),
    )
    out_specs = [pl.BlockSpec((1, D // 48, 24, D), lambda k: (k, 0, 0, 0))] * 2
    out_specs += [whole(outs[2]), whole(outs[3])]
    scratch = [pltpu.VMEM((D, tokens), BF16), pltpu.VMEM((tokens, D), F32), pltpu.VMEM((D, D), F32)]
    return call(
        projection_backward_kernel,
        (4,),
        ins,
        in_specs,
        outs,
        out_specs,
        scratch,
        2 * 7 * tokens * D * D,
        "projection_backward",
    )


def swish_value(values):
    return values / (1.0 + jnp.exp(-values))


def rope_tables(extents, positions):
    quarter = HDIM // 4
    places = jnp.arange(positions, dtype=jnp.int32)
    widths = extents[:, 1]
    row_place = (places[None, :] // widths[:, None]).astype(F32)
    col_place = (places[None, :] % widths[:, None]).astype(F32)
    lane = jnp.arange(2 * HDIM) % HDIM
    frequency = 10000.0 ** (-(lane % quarter).astype(F32) / quarter)
    by_row = lane < 2 * quarter
    angle = jnp.where(by_row, row_place[:, :, None], col_place[:, :, None]) * frequency
    return jnp.cos(angle), jnp.sin(angle)


def local(
    comm,
    inputs,
    cotangent,
    image_shape,
    time_bins,
    time_table,
    modulation_master,
    projection_master,
    output_master,
    expand_master,
    shrink_master,
    modulation_moment,
    projection_moment,
    output_moment,
    expand_moment,
    shrink_moment,
):
    masters = (modulation_master, projection_master, output_master, expand_master, shrink_master)
    moments = (modulation_moment, projection_moment, output_moment, expand_moment, shrink_moment)
    images, positions, features = inputs.shape
    tokens = images * positions
    rows = modulation_master.shape[1]
    row_index = comm.row_index()

    half = FF // 2
    shrink_low = shrink_master.astype(BF16).T
    packed_attention = jnp.concatenate(
        [projection_master[i].astype(BF16) for i in range(3)] + [output_master.astype(BF16)], axis=1
    )
    packed_units = jnp.concatenate(
        [
            part
            for cols in (slice(None, half), slice(half, None))
            for part in (
                expand_master[0, :, cols].astype(BF16),
                expand_master[1, :, cols].astype(BF16),
                shrink_low[:, cols],
            )
        ],
        axis=1,
    )
    selector = (
        time_bins[:, None] == jnp.arange(time_table.shape[0], dtype=jnp.int32)[None, :]
    ).astype(F32)
    active = swish_value(jnp.dot(selector, time_table, precision=HIGHEST)).astype(BF16)

    def group_rows():
        return comm.to_group(active.reshape(images, comm.row_shards, rows).transpose(1, 0, 2))

    def modulation_of(group):
        partial = jnp.einsum(
            "bd,kde->bke",
            group.reshape(-1, rows),
            modulation_master.astype(BF16),
            preferred_element_type=F32,
        )
        return jnp.sum(
            comm.to_group(partial.reshape(comm.row_shards, images, 6, features)), axis=0
        )

    cosine, sine = rope_tables(image_shape, positions)
    lengths = image_shape[:, 0] * image_shape[:, 1]

    def attend(weights, modulation):
        return attention_forward(
            lengths, inputs, cotangent, modulation, cosine, sine, weights[0], weights[1]
        )

    first, second, modulation, results = comm.gather_weights(
        packed_attention, packed_units, (group_rows, modulation_of), attend
    )
    query_key_weight, value_output_weight = first
    left_weight, right_weight = second
    (first_input, query, key, value, probs, attended, attention, middle, second_input, grad_branch) = (
        results
    )
    second_flat = second_input.reshape(tokens, D)
    branch_flat = grad_branch.reshape(tokens, D)
    shaped = lambda v: v.reshape(images, positions, D)
    here = comm.halves()
    branch_left, back_left, *grads = feed_forward(here, second_flat, branch_flat, left_weight)
    left_sum = comm.begin(*grads)
    second_flat = tie(second_flat, back_left)
    branch_right, back_right, *grads = feed_forward(here, second_flat, branch_flat, right_weight)
    back_right, left_sum, grads = meet(back_right, left_sum, grads)
    left_sum = comm.step(left_sum, "x", 0, 2), comm.step(left_sum, "y", 2, 1)
    right_sum = comm.begin(*grads)
    block_output, grad_stream, grads, sums = attention_backward(
        lengths,
        shaped(branch_left),
        shaped(branch_right),
        shaped(back_left),
        shaped(back_right),
        middle,
        cotangent,
        modulation,
        attention,
        value_output_weight,
        query,
        key,
        value,
        probs,
        cosine,
        sine,
    )
    left_sum, right_sum, grads = meet(left_sum, right_sum, grads)
    left_sum = comm.step(left_sum[0], "y"), comm.step(left_sum[1], "x")
    right_sum = comm.step(right_sum, "x", 0, 2), comm.step(right_sum, "y", 2, 1)
    *grads, input_gradient, grad_modulation = projection_backward(
        here,
        grads,
        first_input,
        attended,
        inputs,
        modulation,
        grad_stream,
        sums,
        active,
        query_key_weight,
        value_output_weight,
    )
    left_sum, right_sum, grads, grad_modulation = meet(left_sum, right_sum, grads, grad_modulation)
    attention_sum = comm.begin(*grads)
    right_sum = comm.step(right_sum[0], "y"), comm.step(right_sum[1], "x")
    left_piece = comm.last(*left_sum)
    attention_sum, right_sum, left_piece = meet(attention_sum, right_sum, left_piece)
    right_begun, attention_sum = meet(comm.last_begin(*right_sum), attention_sum)
    right_piece = comm.last_end(right_begun)
    first_sum = comm.step(attention_sum, "x", 0, 2)
    second_sum = comm.step(attention_sum, "y", 2, 2)
    first_sum, second_sum, right_piece = meet(first_sum, second_sum, right_piece)

    owner = comm.owner_index()
    own_expand, own_shrink = expand_moment, shrink_moment.T
    wide_feed = [
        [
            (
                (piece, ((which,), 0, half)),
                (own_shrink, ((), side * half, half))
                if which == 2
                else (own_expand, ((which,), side * half, half)),
            )
            for side, piece in enumerate((left_piece, right_piece))
        ]
        for which in range(3)
    ]
    wide = comm.to_owners(comm.wide_slots_of(wide_feed))
    first_sum = comm.step(first_sum, "y")
    second_sum = comm.step(second_sum, "x")
    first_sum, second_sum, wide = meet(first_sum, second_sum, wide)
    wide = comm.wide_halves(wide)
    attention_piece, wide = meet(comm.last(first_sum, second_sum), wide)
    own_modulation, own_projection, own_output = modulation_moment, projection_moment, output_moment
    square_feed = [[(None, (own_modulation, ((k,), 0, D)))] for k in range(6)]
    for k in range(3):
        square_feed.append(
            [((attention_piece, ((k,), 0, D)), (own_projection, ((k,), 0, D)))]
        )
    square_feed.append([((attention_piece, ((3,), 0, D)), (own_output, ((), 0, D)))])
    slots = comm.square_slots(square_feed, grad_modulation)
    wide = comm.wide_whole(wide)
    active_wide = pick([0 if slot is None else 1 for slot in comm.wide_slots], owner)
    wide_done = newton_schulz(active_wide, wide)
    slots, left_piece, right_piece, attention_piece = meet(
        slots, left_piece, right_piece, attention_piece
    )
    pieces = [(left_piece, (i,), half) for i in range(3)]
    pieces += [(right_piece, (i,), half) for i in range(3)]
    pieces += [(attention_piece, (i,), D) for i in range(4)]
    totals_low = comm.complete_begin(pack(pieces))
    square, gathered, (wide_done, totals_low) = comm.square_to_owners(slots, (wide_done, totals_low))
    active_all = gathered[:, 6]
    item = pick([-1 if slot is None else slot for slot in comm.slots], owner)
    which = jnp.where((item >= 0) & (item < 6), item, 0)
    right = lax.dynamic_index_in_dim(gathered, which, 1, keepdims=False)
    right = jnp.where(item < 6, right, jnp.zeros_like(right))
    square_done = newton_schulz((item >= 0).astype(jnp.int32), square, active_all, right)
    size = FF // comm.wide_parts
    part = pick([0 if slot is None else slot[1] for slot in comm.wide_slots], owner)
    mine = lax.dynamic_slice_in_dim(wide_done, part * size, size, 1)
    mine = mine + jnp.pad(square_done, ((0, 0), (0, size - D)))
    mine, totals_low = meet(mine, totals_low)
    back = comm.to_rows(mine)

    totals_low = comm.complete_end(totals_low).astype(F32)
    by_unit = [
        jnp.concatenate(
            [totals_low[:, (side * 3 + i) * half : (side * 3 + i + 1) * half] for side in range(2)],
            axis=1,
        )
        for i in range(3)
    ]
    steps = [
        (back, (comm.wide_slots.index((i, p)),), size) for i in range(3) for p in range(comm.wide_parts)
    ]
    steps += [(back, (comm.slots.index(i),), D) for i in range(10)]
    updated = update(*comm.quarters(pack(steps)), masters)
    active_rows = lax.dynamic_slice_in_dim(active_all, row_index * rows, rows, 1)
    modulation_total = jnp.einsum(
        "bd,bke->kde",
        active_rows,
        gathered[:, :6],
        preferred_element_type=F32,
    )
    after = 3 * FF
    totals = (
        modulation_total,
        jnp.stack([totals_low[:, after + i * D : after + (i + 1) * D] for i in range(3)]),
        totals_low[:, after + 3 * D :],
        jnp.stack(by_unit[:2]),
        by_unit[2].T,
    )
    states = tuple((MOMENTUM_DECAY * moment + total for moment, total in zip(moments, totals)))
    return (block_output, input_gradient, *totals, *updated, *states)


def solution(mesh):
    if mesh.shape["dp"] == 4 and mesh.shape["fsdp"] == 8:
        comm = Torus(mesh)
    else:
        comm = Plain(mesh)
    images, rows = comm.images, comm.rows
    by_row = (
        P(None, rows, None),
        P(None, rows, None),
        P(rows, None),
        P(None, rows, None),
        P(None, rows),
    )
    return jax.shard_map(
        functools.partial(local, comm),
        mesh=comm.mesh,
        in_specs=(
            P(images, None, None),
            P(images, None, None),
            P(images, None),
            P(images),
            P(),
            *by_row,
            *by_row,
        ),
        out_specs=(P(images, None, None), P(images, None, None), *by_row, *by_row, *by_row),
        check_vma=False,
    )
```
